128 devices in a mesh: tok: 32 (over y, z, core), mp: 4 (over x).
Axes of the slice: x: 4, y: 4, z: 4, core: 2. Of those that a mesh axis runs over, the one named last changes fastest.
Arguments:
- tokens: bfloat16 [32768, 2048], P('tok'), may hold values from -6 to 6
- norm_gain: float32 [2048], replicated, may hold values from 0.1 to 1.9
- w_query: bfloat16 [2048, 2048], P(None, 'mp'), may hold values from -2 to 2
- w_key: bfloat16 [2048, 2048], P(None, 'mp'), may hold values from -2 to 2
- w_value: bfloat16 [2048, 2048], P(None, 'mp'), may hold values from -0.125 to 0.125
- w_out: bfloat16 [2048, 2048], replicated, may hold values from -2.5 to 2.5
- kv_cache: bfloat16 [2, 32768, 2, 2048], P(None, 'tok', None, 'mp'), may hold values from -6 to 6
- wake_blocks: int32 [256, 8], replicated, may hold values from 0 to 255, as said below
- wake_frames: int32 [256, 8], replicated, may hold values from 0 to 1
- wake_counts: int32 [256], replicated, may hold values from 2 to 8, as said below
Outputs:
- advanced: bfloat16 [32768, 2048], P('tok', 'mp')
The draws below stay inside these ranges and needn't reach their ends.
Inputs may be any that keep to these rules, and one draw needn't show every extreme that they name: `wake_blocks`: blocks i * 8 to (i + 1) * 8 - 1 are held by tok index i. Among the live slots (w below the block's count) of the 8 query blocks of one tok index, at most 2 name blocks held by any one tok index, and for every tok index some holder is named exactly 2 times. Slots at or past the count hold any block number. `wake_counts`: some query block has all 8 slots live.
All inputs are finite; a program needn't handle non-finite values.
Results may differ from the reference program's by a relative error of at most 0.005.
The reference program's roundings to bfloat16 on the way (of `normed`, `weights` and `attention`) count: a program that leaves them out, or rounds other values in their place, can miss the bound.
Values may be sent and summed in bfloat16 or wider, within the bound.
No kernel may reach another device: no remote copies, remote signals or barrier semaphores. Data moves between devices by JAX's collectives and lax.ppermute only.
A program may use at most 192 MiB of HBM per device.

```python
import math
import jax
import jax.numpy as jnp
from jax import lax

D = 2048
HEADS = 16
HEAD_DIM = 128
BLOCK = 128
WMAX = 8
NF = 2
TOKENS = 32768
QB = 8
NBLK = 256
CAP = 2


def weight_pair(key):
    base_key = jax.random.fold_in(key, 7)
    first_key = jax.random.fold_in(base_key, 1)
    second_key = jax.random.fold_in(base_key, 2)
    spread = 1.0 / math.sqrt(D)
    query_part = jax.random.normal(first_key, (D, D), jnp.float32) * (2.0 * spread)
    key_part = jax.random.normal(second_key, (D, D), jnp.float32) * spread
    return (jnp.clip(query_part, -2.0, 2.0), jnp.clip(key_part, -2.0, 2.0))


def draw_w_query(key, part):
    return weight_pair(key)[0].astype(jnp.bfloat16)


def draw_w_key(key, part):
    return weight_pair(key)[1].astype(jnp.bfloat16)


def permute_one(sub_key):
    return jax.random.permutation(sub_key, NBLK // QB)


def wake_tables(key):
    base_key = jax.random.fold_in(key, 101)
    level_key, jitter_key, top_key, perm_key, pick_key, filler_key = jax.random.split(base_key, 6)
    device_total = NBLK // QB
    slot_total = QB * WMAX
    device_ids = jnp.arange(device_total, dtype=jnp.int32)
    levels = jax.random.randint(level_key, (device_total,), 0, 100)
    topmost = jax.random.randint(top_key, (), 0, device_total)
    levels = jnp.where(device_ids == topmost, 99, levels)
    per_device = 1 + (WMAX - 1) * levels * levels * levels // 970299
    jitter = jax.random.randint(jitter_key, (device_total, QB), -1, 2)
    counts = jnp.clip(per_device[:, None] + jitter, 2, WMAX)
    counts = jnp.where((device_ids == topmost)[:, None], WMAX, counts)
    slot_live = (jnp.arange(WMAX, dtype=jnp.int32)[None, None, :] < counts[:, :, None]).reshape(device_total, slot_total)
    rank_live = jnp.cumsum(slot_live.astype(jnp.int32), axis=1) - 1
    orders = jax.vmap(permute_one)(jax.random.split(perm_key, device_total))
    owners = jnp.take_along_axis(orders, jnp.clip(rank_live // CAP, 0, device_total - 1), axis=1)
    picked = jax.random.randint(pick_key, (device_total, slot_total), 0, QB)
    filler = jax.random.randint(filler_key, (device_total, slot_total), 0, NBLK)
    blocks = jnp.where(slot_live, owners * QB + picked, filler).reshape(NBLK, WMAX)
    return (blocks.astype(jnp.int32), counts.reshape(NBLK).astype(jnp.int32))


def draw_wake_blocks(key, part):
    return wake_tables(key)[0]


def draw_wake_counts(key, part):
    return wake_tables(key)[1]


def touch_ends(entries, own_key, smallest, high):
    spot = [jax.random.randint(jax.random.fold_in(own_key, axis), (), 0, length) for axis, length in enumerate(entries.shape)]
    longest = entries.shape.index(max(entries.shape))
    beside = spot[:longest] + [(spot[longest] + 1) % entries.shape[longest]] + spot[longest + 1:]
    return entries.at[tuple(spot)].set(smallest).at[tuple(beside)].set(high)


def block_levels(stream_key, shape, shards, least, high):
    level, own = 1.0, jax.random.fold_in(stream_key, 6)
    for position, shards_of in shards:
        heights = jnp.exp(jax.random.uniform(jax.random.fold_in(own, position), (shards_of,), jnp.float32, least / len(shards), high / len(shards)))
        level = level * jnp.repeat(heights, shape[position] // shards_of).reshape([-1 if axis == position else 1 for axis in range(len(shape))])
    return level


def bell_draw(key, shape, deviation, reach, cuts=(), kind=jnp.bfloat16):
    values = deviation * jax.random.normal(key, shape, jnp.float32)
    if cuts:
        values = values * block_levels(key, shape, cuts, -0.22, 0.18)
    return jnp.clip(values, -reach, reach).astype(kind)


def setup_inputs(seed: int = 0) -> dict:
    seeds = jax.random.split(jax.random.key(seed), 11)
    return {
        "tokens": bell_draw(seeds[0], (TOKENS, D), 1.0, 6.0, ((0, 32),)),
        "norm_gain": jnp.clip(1.0 + 0.18 * jax.random.normal(seeds[1], (D,), jnp.float32), 0.1, 1.9),
        "w_query": draw_w_query(jax.random.fold_in(seeds[10], 71), 0),
        "w_key": draw_w_key(jax.random.fold_in(seeds[10], 71), 0),
        "w_value": bell_draw(seeds[4], (D, D), D ** -0.5, 0.125, ((1, 4),)),
        "w_out": bell_draw(seeds[5], (D, D), 0.18, 2.5),
        "kv_cache": bell_draw(seeds[6], (NF, TOKENS, 2, D), 1.0, 6.0, ((1, 32), (3, 4))),
        "wake_blocks": draw_wake_blocks(jax.random.fold_in(seeds[10], 71), 0),
        "wake_frames": touch_ends(jax.random.randint(seeds[8], (NBLK, WMAX), 0, NF), jax.random.fold_in(seeds[8], 1), 0, NF - 1).astype(jnp.int32),
        "wake_counts": draw_wake_counts(jax.random.fold_in(seeds[10], 71), 0),
    }


def reference(tokens, norm_gain, w_query, w_key, w_value, w_out, kv_cache, wake_blocks, wake_frames, wake_counts):
    tokens_f32 = tokens.astype(jnp.float32)
    inverse = lax.rsqrt(lax.optimization_barrier(jnp.mean(tokens_f32 * tokens_f32, axis=1, keepdims=True)) + 1e-05)
    normed = (tokens_f32 * inverse * norm_gain[None, :]).astype(jnp.bfloat16)
    queries = jnp.dot(normed, w_query, preferred_element_type=jnp.float32).astype(jnp.bfloat16)
    keys_now = jnp.dot(normed, w_key, preferred_element_type=jnp.float32).astype(jnp.bfloat16)
    values_now = jnp.dot(normed, w_value, preferred_element_type=jnp.float32).astype(jnp.bfloat16)
    query_blocks = queries.reshape(NBLK, BLOCK, HEADS, HEAD_DIM)
    key_blocks = keys_now.reshape(NBLK, BLOCK, HEADS, HEAD_DIM)
    value_blocks = values_now.reshape(NBLK, BLOCK, HEADS, HEAD_DIM)
    cache_keys = kv_cache[:, :, 0, :].reshape(NF, NBLK, BLOCK, HEADS, HEAD_DIM)
    cache_values = kv_cache[:, :, 1, :].reshape(NF, NBLK, BLOCK, HEADS, HEAD_DIM)
    score_scale = 1.0 / math.sqrt(HEAD_DIM)

    def per_block(block_index):
        neighbours = ((block_index + jnp.arange(-1, 2, dtype=jnp.int32)) % NBLK).astype(jnp.int32)
        listed_blocks = wake_blocks[block_index]
        listed_frames = wake_frames[block_index]
        slot_live = jnp.arange(WMAX, dtype=jnp.int32) < wake_counts[block_index]
        key_live = jnp.concatenate([jnp.ones((3 * BLOCK,), bool), jnp.repeat(slot_live, BLOCK)])
        near_keys = key_blocks[neighbours].reshape(3 * BLOCK, HEADS, HEAD_DIM)
        near_values = value_blocks[neighbours].reshape(3 * BLOCK, HEADS, HEAD_DIM)
        far_keys = cache_keys[listed_frames, listed_blocks].reshape(WMAX * BLOCK, HEADS, HEAD_DIM)
        far_values = cache_values[listed_frames, listed_blocks].reshape(WMAX * BLOCK, HEADS, HEAD_DIM)
        every_key = jnp.concatenate([near_keys, far_keys], axis=0).astype(jnp.float32)
        every_value = jnp.concatenate([near_values, far_values], axis=0).astype(jnp.float32)
        scores = jnp.einsum('qhd,khd->hqk', query_blocks[block_index].astype(jnp.float32), every_key) * score_scale
        scores = jnp.where(key_live[None, None, :], scores, -1e+30)
        row_peak = lax.optimization_barrier(jnp.max(scores, axis=2, keepdims=True))
        shifted = jnp.exp(scores - row_peak)
        weights = (shifted / lax.optimization_barrier(jnp.sum(shifted, axis=2, keepdims=True))).astype(jnp.bfloat16)
        result = jnp.einsum('hqk,khd->qhd', weights.astype(jnp.float32), every_value)
        return result.astype(jnp.bfloat16).reshape(BLOCK, D)
    attention = lax.map(per_block, jnp.arange(NBLK, dtype=jnp.int32)).reshape(TOKENS, D)
    projected = jnp.dot(attention, w_out, preferred_element_type=jnp.float32)
    return (tokens_f32 + projected).astype(jnp.bfloat16)
```

```python
import functools
import math

import jax
import jax.numpy as jnp
from jax import lax
from jax.experimental import pallas as pl
from jax.experimental.pallas import tpu as pltpu
from jax.sharding import PartitionSpec as P

HD = 128
BLOCK = 128
WMAX = 8
NEG = -1e30
SCALE = 1.0 / math.sqrt(HD)
NY, NZ, NC, NX = 4, 4, 2, 4
F32, BF16 = jnp.float32, jnp.bfloat16
ANY = pl.BlockSpec(memory_space=pl.ANY)
SMEM = pl.BlockSpec(memory_space=pltpu.SMEM)
OROWS = 2048 + 48
FROWS = 1024 + 8


def params(mib=48):
    return pltpu.CompilerParams(vmem_limit_bytes=mib << 20)


def tok_of(y, z, c):
    return ((y % NY) * NZ + z % NZ) * NC + c % NC


def chips():
    return [(y, z, c) for y in range(NY) for z in range(NZ) for c in range(NC)]


def rows_perm(x, d):
    pairs = [(tok_of(y, z, c), tok_of(y + d, z, c) if c == 0 else tok_of(y, z + d, c)) for y, z, c in chips()]
    return lax.ppermute(x, "tok", pairs)


def query_perm(x, d):
    pairs = [(tok_of(y, z, c), tok_of(y, z + d, c) if c == 0 else tok_of(y + d, z, c)) for y, z, c in chips()]
    return lax.ppermute(x, "tok", pairs)


def core_swap(x):
    return lax.ppermute(x, "tok", [(tok_of(y, z, c), tok_of(y, z, 1 - c)) for y, z, c in chips()])


def ring_perm(x, d):
    n = NY * NZ * NC
    return lax.ppermute(x, "tok", [(i, (i + d) % n) for i in range(n)])


def mp_perm(x, d):
    return lax.ppermute(x, "mp", [(i, (i + d) % NX) for i in range(NX)])


def nt(a, b):
    return lax.dot_general(a, b, (((1,), (1,)), ((), ())), preferred_element_type=F32)


def nn(a, b):
    return lax.dot_general(a, b, (((1,), (0,)), ((), ())), preferred_element_type=F32)


def split_cache_kernel(core_ref, rows_ref, a0, a1, s0, s1):
    core = core_ref[0]

    def put(first, outs):
        for j in range(2):
            lanes = slice((first + j) * HD, (first + j + 1) * HD)
            outs[j][0] = rows_ref[0, :, lanes]
            outs[j][1] = rows_ref[0, :, 512 + (first + j) * HD : 512 + (first + j + 1) * HD].T

    keep = [a0.at[0, 0, 0], a1.at[0, 0, 0]]
    send = [s0.at[0, 0], s1.at[0, 0]]

    @pl.when(core == 0)
    def _():
        put(0, keep)
        put(2, send)

    @pl.when(core == 1)
    def _():
        put(2, keep)
        put(0, send)


def split_cache(core, rows):
    full = jax.ShapeDtypeStruct((2, 2, 8, 2, BLOCK, HD), BF16)
    half = jax.ShapeDtypeStruct((2, 8, 2, BLOCK, HD), BF16)
    wide = pl.BlockSpec((1, 1, 1, 2, BLOCK, HD), lambda i, c: (i // 8, 0, i % 8, 0, 0, 0))
    slim = pl.BlockSpec((1, 1, 2, BLOCK, HD), lambda i, c: (i // 8, i % 8, 0, 0, 0))
    return pl.pallas_call(
        split_cache_kernel,
        grid_spec=pltpu.PrefetchScalarGridSpec(
            num_scalar_prefetch=1,
            grid=(16,),
            in_specs=[pl.BlockSpec((1, BLOCK, 1024), lambda i, c: (i, 0, 0))],
            out_specs=[wide, wide, slim, slim],
        ),
        out_shape=[full, full, half, half],
        compiler_params=params(),
        name="split_cache",
    )(core, rows)


def project_kernel(core_ref, tok_ref, gain_ref, wq, wk, wv, q_all, q_send, k_all, v_all, first, last):
    step = pl.program_id(0)
    core = core_ref[0]
    x = tok_ref[...].astype(F32)
    inverse = lax.rsqrt(jnp.mean(x * x, axis=1, keepdims=True) + 1e-05)
    normed = (x * inverse * gain_ref[...]).astype(BF16)
    q = nn(normed, wq[...]).astype(BF16)
    k = nn(normed, wk[...]).astype(BF16)
    v = nn(normed, wv[...])

    def put(shift):
        for h in range(4):
            slot = (h - shift) % 4
            lanes = slice(h * HD, (h + 1) * HD)
            q_all[slot] = q[:, lanes]
            if slot >= 2:
                q_send[slot - 2] = q[:, lanes]
            for b in range(2):
                rows = slice(b * BLOCK, (b + 1) * BLOCK)
                kb = k[rows, lanes]
                vb = v[rows, lanes].T.astype(BF16)
                k_all[slot, b] = kb
                v_all[slot, b] = vb
                if b == 0:
                    @pl.when(step == 0)
                    def _():
                        first[0, slot] = kb
                        first[1, slot] = vb
                else:
                    @pl.when(step == pl.num_programs(0) - 1)
                    def _():
                        last[0, slot] = kb
                        last[1, slot] = vb

    @pl.when(core == 0)
    def _():
        put(0)

    @pl.when(core == 1)
    def _():
        put(2)


def project(core, tokens, gain, wq, wk, wv):
    n, d = tokens.shape
    w = wq.shape[1]
    weight = pl.BlockSpec((d, w), lambda i, c: (0, 0), pipeline_mode=pl.Buffered(1))
    edge = pl.BlockSpec((2, 4, BLOCK, HD), lambda i, c: (0, 0, 0, 0))
    blocks = pl.BlockSpec((4, 2, BLOCK, HD), lambda i, c: (0, i, 0, 0))
    return pl.pallas_call(
        project_kernel,
        grid_spec=pltpu.PrefetchScalarGridSpec(
            num_scalar_prefetch=1,
            grid=(n // 256,),
            in_specs=[
                pl.BlockSpec((256, d), lambda i, c: (i, 0)),
                pl.BlockSpec((1, d), lambda i, c: (0, 0)),
                weight,
                weight,
                weight,
            ],
            out_specs=[
                pl.BlockSpec((4, 256, HD), lambda i, c: (0, i, 0)),
                pl.BlockSpec((2, 256, HD), lambda i, c: (0, i, 0)),
                blocks,
                blocks,
                edge,
                edge,
            ],
        ),
        out_shape=[
            jax.ShapeDtypeStruct((4, n, HD), BF16),
            jax.ShapeDtypeStruct((2, n, HD), BF16),
            jax.ShapeDtypeStruct((4, 8, BLOCK, HD), BF16),
            jax.ShapeDtypeStruct((4, 8, HD, BLOCK), BF16),
            jax.ShapeDtypeStruct((2, 4, BLOCK, HD), BF16),
            jax.ShapeDtypeStruct((2, 4, BLOCK, HD), BF16),
        ],
        compiler_params=params(),
        cost_estimate=pl.CostEstimate(flops=2 * n * d * 3 * w, transcendentals=0, bytes_accessed=16 << 20),
        name="project",
    )(core, tokens, gain.reshape(1, d), wq, wk, wv)


def near_kernel(q_ref, k_ref, v_ref, lo_ref, hi_ref, o_ref, lse_ref):
    for b in range(8):
        q = q_ref[0, b * BLOCK : (b + 1) * BLOCK]
        ks = [lo_ref[0, 0] if b == 0 else k_ref[0, b - 1], k_ref[0, b], hi_ref[0, 0] if b == 7 else k_ref[0, b + 1]]
        vs = [lo_ref[1, 0] if b == 0 else v_ref[0, b - 1], v_ref[0, b], hi_ref[1, 0] if b == 7 else v_ref[0, b + 1]]
        s = [nt(k, q) * SCALE for k in ks]
        m = jnp.max(jnp.maximum(jnp.maximum(s[0], s[1]), s[2]), axis=0, keepdims=True)
        p = [jnp.exp(x - m) for x in s]
        total = jnp.sum(p[0] + p[1] + p[2], axis=0, keepdims=True)
        acc = nn(vs[0], p[0].astype(BF16)) + nn(vs[1], p[1].astype(BF16)) + nn(vs[2], p[2].astype(BF16))
        o_ref[0, b] = acc / total
        lse_ref[0, b : b + 1, :] = m + jnp.log(total)


def near(q, k, v, lo, hi):
    blocks = pl.BlockSpec((1, 8, BLOCK, HD), lambda s: (s, 0, 0, 0))
    edge = pl.BlockSpec((2, 1, BLOCK, HD), lambda s: (0, (s + 2) % 4, 0, 0))
    return pl.pallas_call(
        near_kernel,
        grid=(4,),
        in_specs=[pl.BlockSpec((1, 1024, HD), lambda s: (s, 0, 0)), blocks, blocks, edge, edge],
        out_specs=[blocks, pl.BlockSpec((1, 8, HD), lambda s: (s, 0, 0))],
        out_shape=[jax.ShapeDtypeStruct((4, 8, HD, BLOCK), F32), jax.ShapeDtypeStruct((4, 8, BLOCK), F32)],
        compiler_params=params(),
        cost_estimate=pl.CostEstimate(flops=32 * 384 * 128 * 512, transcendentals=32 * 384 * 128, bytes_accessed=6 << 20),
        name="near",
    )(q, k, v, lo, hi)


def far_kernel(
    j, cnt_ref, code_ref, own, up, down, up2, down2, qa, qb, qc, qd,
    o0, o1, o2, o3, kvbuf, qbuf, lse, base_ref, kvsem, qsem,
):
    qs, outs = (qa, qb, qc, qd), (o0, o1, o2, o3)
    for r in range(4):
        pltpu.make_async_copy(qs[r].at[:, j], qbuf.at[r], qsem.at[r]).start()

    def fetch(i, e):
        base_ref[i] = e

        def slot(w, e):
            code = code_ref[i * WMAX + w]
            piece = lax.shift_right_arithmetic(code, 5)
            at = lax.bitwise_and(code, 31)

            def start(src):
                pltpu.make_async_copy(src, kvbuf.at[e], kvsem.at[e]).start()

            @pl.when(piece == 0)
            def _():
                start(own.at[at])

            @pl.when(piece == 1)
            def _():
                start(down.at[at])

            @pl.when(piece == 3)
            def _():
                start(up.at[at])

            @pl.when(jnp.logical_and(piece == 2, at < 16))
            def _():
                start(up2.at[lax.bitwise_and(at, 15)])

            @pl.when(jnp.logical_and(piece == 2, at >= 16))
            def _():
                start(down2.at[lax.bitwise_and(at, 15)])

            return e + (code >= 0).astype(jnp.int32)

        return lax.fori_loop(0, jnp.where(cnt_ref[i] > 0, WMAX, 0), slot, e)

    lax.fori_loop(0, 64, fetch, jnp.int32(0))

    def landed(e):
        pltpu.make_async_copy(own.at[0], kvbuf.at[e], kvsem.at[e]).wait()

    for r in range(4):
        pltpu.make_async_copy(qs[r].at[:, j], qbuf.at[r], qsem.at[r]).wait()
        out = outs[r]

        def block(i, _):
            n = cnt_ref[r * 16 + i]
            e = base_ref[r * 16 + i]
            rows = pl.ds(pl.multiple_of(i * HD, HD), HD)

            @pl.when(n == 0)
            def _():
                out[rows, :] = jnp.zeros((HD, BLOCK), BF16)
                lse[pl.ds(r * 16 + i, 1), :] = jnp.full((1, BLOCK), NEG, F32)

            @pl.when(n > 0)
            def _():
                q = qbuf[r, lax.shift_right_logical(i, 3), lax.bitwise_and(i, 7)]

                def pair(at):
                    both = at + 1 < n
                    ea = e + at
                    eb = jnp.where(both, ea + 1, ea)
                    landed(ea)

                    @pl.when(both)
                    def _():
                        landed(eb)

                    sa = nt(kvbuf[ea, 0], q) * SCALE
                    sb = jnp.where(both, nt(kvbuf[eb, 0], q) * SCALE, NEG)
                    return ea, eb, sa, sb

                ea, eb, sa, sb = pair(0)
                m = jnp.max(jnp.maximum(sa, sb), axis=0, keepdims=True)
                pa, pb = jnp.exp(sa - m), jnp.exp(sb - m)
                total = jnp.sum(pa + pb, axis=0, keepdims=True)
                acc = nn(kvbuf[ea, 1], pa.astype(BF16)) + nn(kvbuf[eb, 1], pb.astype(BF16))

                def more(k, carry):
                    m, total, acc = carry
                    ea, eb, sa, sb = pair(2 * k)
                    m_new = jnp.maximum(m, jnp.max(jnp.maximum(sa, sb), axis=0, keepdims=True))
                    alpha = jnp.exp(m - m_new)
                    pa, pb = jnp.exp(sa - m_new), jnp.exp(sb - m_new)
                    total = total * alpha + jnp.sum(pa + pb, axis=0, keepdims=True)
                    acc = acc * alpha + nn(kvbuf[ea, 1], pa.astype(BF16)) + nn(kvbuf[eb, 1], pb.astype(BF16))
                    return m_new, total, acc

                m, total, acc = lax.fori_loop(1, lax.shift_right_logical(n + 1, 1), more, (m, total, acc))
                out[rows, :] = (acc / total).astype(BF16)
                lse[pl.ds(r * 16 + i, 1), :] = m + jnp.log(total)

            return 0

        lax.fori_loop(0, 16, block, 0)
        part = lse[r * 16 : (r + 1) * 16, :]
        for t in range(3):
            term = part.astype(BF16)
            out[2048 + t * 16 : 2064 + t * 16, :] = term
            part = part - term.astype(F32)


def far(j, cnt, code, own, up, down, up2, down2, qs):
    out = jax.ShapeDtypeStruct((OROWS, BLOCK), BF16)
    flat = [a.reshape(-1, 2, BLOCK, HD) for a in (own, up, down, up2, down2)]
    return pl.pallas_call(
        functools.partial(far_kernel, j),
        in_specs=[SMEM, SMEM] + [ANY] * 9,
        out_specs=[pl.BlockSpec((OROWS, BLOCK), lambda: (0, 0))] * 4,
        out_shape=[out] * 4,
        scratch_shapes=[
            pltpu.VMEM((128, 2, BLOCK, HD), BF16),
            pltpu.VMEM((4, 2, 8, BLOCK, HD), BF16),
            pltpu.VMEM((64, BLOCK), F32),
            pltpu.SMEM((64,), jnp.int32),
            pltpu.SemaphoreType.DMA((128,)),
            pltpu.SemaphoreType.DMA((4,)),
        ],
        compiler_params=params(),
        cost_estimate=pl.CostEstimate(flops=64 * 128 * 128 * 512, transcendentals=64 * 128 * 128, bytes_accessed=10 << 20),
        name="far",
    )(cnt, code, *flat, *qs)


def merge_kernel(a, b, c, d, keep, send):
    parts = (a, b, c, d)
    logs = [sum(p[2048 + t * 16 : 2064 + t * 16, :].astype(F32) for t in range(3)) for p in parts]
    peak = functools.reduce(jnp.maximum, logs)
    shares = [jnp.exp(x - peak) for x in logs]
    total = sum(shares)
    shares = [x / total for x in shares]
    joint = peak + jnp.log(total)
    for s, out in enumerate((keep, send)):
        for i in range(8):
            row = s * 8 + i
            rows = slice(row * HD, (row + 1) * HD)
            out[i * HD : (i + 1) * HD, :] = sum(
                x[row : row + 1, :] * p[rows, :].astype(F32) for x, p in zip(shares, parts)
            )
        out[1024:1032, :] = joint[s * 8 : (s + 1) * 8, :]


def merge(parts):
    out = jax.ShapeDtypeStruct((FROWS, BLOCK), F32)
    return pl.pallas_call(
        merge_kernel,
        out_shape=[out, out],
        compiler_params=params(),
        cost_estimate=pl.CostEstimate(flops=1 << 21, transcendentals=1 << 13, bytes_accessed=3 << 20),
        name="merge",
    )(*parts)


def finish_kernel(near_a, lse_a, near_b, lse_b, far_a, far_b, out):
    for s, (o, log, f) in enumerate(((near_a, lse_a, far_a), (near_b, lse_b, far_b))):
        here, away = log[0], f[1024:1032, :]
        peak = jnp.maximum(here, away)
        wn, wf = jnp.exp(here - peak), jnp.exp(away - peak)
        total = wn + wf
        wn, wf = wn / total, wf / total
        for b in range(8):
            both = wn[b : b + 1, :] * o[0, b] + wf[b : b + 1, :] * f[b * HD : (b + 1) * HD, :]
            out[s, b * BLOCK : (b + 1) * BLOCK, :] = both.T.astype(BF16)


def finish(j, o, lse, far_keep, far_other):
    def at(slot):
        return [
            pl.BlockSpec((1, 8, HD, BLOCK), lambda i: (slot, 0, 0, 0)),
            pl.BlockSpec((1, 8, BLOCK), lambda i: (slot, 0, 0)),
        ]

    whole = pl.BlockSpec((FROWS, BLOCK), lambda i: (0, 0))
    return pl.pallas_call(
        finish_kernel,
        grid=(1,),
        in_specs=at(j) + at(2 + j) + [whole, whole],
        out_specs=pl.BlockSpec((2, 1024, HD), lambda i: (0, 0, 0)),
        out_shape=jax.ShapeDtypeStruct((2, 1024, HD), BF16),
        compiler_params=params(),
        cost_estimate=pl.CostEstimate(flops=1 << 21, transcendentals=1 << 13, bytes_accessed=3 << 20),
        name="finish",
    )(o, lse, o, lse, far_keep, far_other)


def mix_kernel(last, place_ref, a0, a1, a2, a3, *rest):
    weights, carried, out = rest[:8], rest[8], rest[-1]
    total = carried[...].astype(F32) if carried is not out else None
    for rel, a in enumerate((a0, a1, a2, a3)):
        for s in range(2):
            term = nn(a[s], weights[rel * 2 + s][...])
            total = term if total is None else total + term
    if last:
        total = total + rest[9][...]
    out[...] = total.astype(out.dtype)


def mix(j, place, parts, w_out, carried, acc=None):
    n, cols = 1024, 512

    def weight(rel, s):
        def at(i, p):
            head = (2 * p[0] + 2 * s + j) % 4
            return ((p[1] + rel) % NX * 4 + head, p[1])

        return pl.BlockSpec((HD, cols), at)

    last = acc is not None
    in_specs = [pl.BlockSpec((2, 256, HD), lambda i, p: (0, i, 0))] * 4
    in_specs += [weight(rel, s) for rel in range(4) for s in range(2)]
    args = list(parts) + [w_out] * 8
    if last:
        in_specs.append(pl.BlockSpec((256, cols), lambda i, p: (i, p[1])))
        in_specs.append(pl.BlockSpec((256, cols), lambda i, p: (i, 0)))
        args += [carried, acc]
    return pl.pallas_call(
        functools.partial(mix_kernel, last),
        grid_spec=pltpu.PrefetchScalarGridSpec(
            num_scalar_prefetch=1,
            grid=(n // 256,),
            in_specs=in_specs,
            out_specs=pl.BlockSpec((256, cols), lambda i, p: (i, 0)),
        ),
        out_shape=jax.ShapeDtypeStruct((n, cols), BF16 if last else F32),
        compiler_params=params(),
        cost_estimate=pl.CostEstimate(flops=2 * n * 1024 * cols, transcendentals=0, bytes_accessed=6 << 20),
        name="mix",
    )(place, *args)


def line_codes(wake_blocks, wake_frames, wake_counts, y, z, c):
    live = jnp.arange(WMAX, dtype=jnp.int32)[None, :] < wake_counts[:, None]
    word = jnp.where(live, wake_frames * 256 + wake_blocks, -1).reshape(NY, NZ, NC, 8, WMAX)
    by_y = lax.dynamic_index_in_dim(word, y, 0, keepdims=False)
    by_z = lax.dynamic_index_in_dim(word, z, 1, keepdims=False)
    here = jnp.where(c == 0, by_y, by_z)
    here = lax.dynamic_slice_in_dim(jnp.concatenate([here, here], axis=0), jnp.where(c == 0, z, y), 4, 0)
    here = lax.dynamic_slice_in_dim(jnp.concatenate([here, here], axis=1), c, 2, 1)
    word = here.reshape(64, WMAX)
    block, frame = word & 255, word >> 8
    hc, hz, hy = (block >> 3) & 1, (block >> 4) & 3, (block >> 6) & 3
    in_line = (word >= 0) & (jnp.where(c == 0, hz, hy) == jnp.where(c == 0, z, y))
    piece = (jnp.where(c == 0, hy, hz) - jnp.where(c == 0, y, z)) & 3
    code = piece * 32 + (frame & 1) * 16 + (hc ^ c) * 8 + (block & 7)
    code = jnp.where(in_line, code, -1)
    return code.reshape(512), jnp.sum(in_line.astype(jnp.int32), axis=1)


def on_device(tokens, norm_gain, w_query, w_key, w_value, w_out, kv_cache, wake_blocks, wake_frames, wake_counts):
    tok = lax.axis_index("tok").astype(jnp.int32)
    mp = lax.axis_index("mp").astype(jnp.int32)
    c, z, y = tok % NC, (tok // NC) % NZ, tok // (NC * NZ)
    core = c.reshape(1)
    place = jnp.stack([c, mp])

    rows = kv_cache.reshape(16, BLOCK, 1024)
    *own, send0, send1 = split_cache(core, rows)
    own = list(own)
    for j, send in enumerate((send0, send1)):
        own[j] = lax.dynamic_update_slice(own[j], core_swap(send)[:, None], (0, 1, 0, 0, 0, 0))

    q_all, q_send, k_all, v_all, first, last = project(core, tokens, norm_gain, w_query, w_key, w_value)
    mine = jnp.concatenate([q_all[:2], core_swap(q_send)], axis=0).reshape(2, 2, 8, BLOCK, HD)
    qs = [mine, query_perm(mine, -1), query_perm(mine, 2), query_perm(mine, 1)]
    lo, hi = ring_perm(last, 1), ring_perm(first, -1)
    code, cnt = line_codes(wake_blocks, wake_frames, wake_counts, y, z, c)
    near_o, near_lse = near(q_all, k_all, v_all, lo, hi)

    acc = None
    gate = None
    for j in range(2):
        buf = own[j]
        if gate is not None:
            buf, *_ = lax.optimization_barrier((buf, *gate))
        up, down = rows_perm(buf, 1), rows_perm(buf, -1)
        gate = (up[:1, :1, :1, :1], down[:1, :1, :1, :1])
        up2, down2 = rows_perm(up[:1], 1), rows_perm(down[1:], -1)
        parts = far(j, cnt, code, buf, up, down, up2, down2, qs)
        back = [parts[0], query_perm(parts[1], 1), query_perm(parts[2], 2), query_perm(parts[3], -1)]
        keep, other = merge(back)
        heads = finish(j, near_o, near_lse, keep, core_swap(other))
        gathered = [heads, mp_perm(heads, -1), mp_perm(heads, 2), mp_perm(heads, 1)]
        acc = mix(j, place, gathered, w_out, tokens, acc)
    return acc


def solution(mesh):
    return jax.shard_map(
        on_device,
        mesh=mesh,
        in_specs=(
            P("tok", None),
            P(),
            P(None, "mp"),
            P(None, "mp"),
            P(None, "mp"),
            P(),
            P(None, "tok", None, "mp"),
            P(),
            P(),
            P(),
        ),
        out_specs=P("tok", "mp"),
        check_vma=False,
    )
```

```python
import functools
import math

import jax
import jax.numpy as jnp
from jax import lax
from jax.experimental import pallas as pl
from jax.experimental.pallas import tpu as pltpu
from jax.sharding import PartitionSpec as P

HD = 128
BLOCK = 128
WMAX = 8
NEG = -1e30
SCALE = 1.0 / math.sqrt(HD)
NY, NZ, NC, NX = 4, 4, 2, 4
F32, BF16 = jnp.float32, jnp.bfloat16
ANY = pl.BlockSpec(memory_space=pl.ANY)
SMEM = pl.BlockSpec(memory_space=pltpu.SMEM)
OROWS = 2048 + 48
FROWS = 1024 + 8


def params(mib=48):
    return pltpu.CompilerParams(vmem_limit_bytes=mib << 20)


def tok_of(y, z, c):
    return ((y % NY) * NZ + z % NZ) * NC + c % NC


def chips():
    return [(y, z, c) for y in range(NY) for z in range(NZ) for c in range(NC)]


def rows_perm(x, d):
    pairs = [(tok_of(y, z, c), tok_of(y + d, z, c) if c == 0 else tok_of(y, z + d, c)) for y, z, c in chips()]
    return lax.ppermute(x, "tok", pairs)


def query_perm(x, d):
    pairs = [(tok_of(y, z, c), tok_of(y, z + d, c) if c == 0 else tok_of(y + d, z, c)) for y, z, c in chips()]
    return lax.ppermute(x, "tok", pairs)


def core_swap(x):
    return lax.ppermute(x, "tok", [(tok_of(y, z, c), tok_of(y, z, 1 - c)) for y, z, c in chips()])


def ring_perm(x, d):
    n = NY * NZ * NC
    return lax.ppermute(x, "tok", [(i, (i + d) % n) for i in range(n)])


def mp_perm(x, d):
    return lax.ppermute(x, "mp", [(i, (i + d) % NX) for i in range(NX)])


def nt(a, b):
    return lax.dot_general(a, b, (((1,), (1,)), ((), ())), preferred_element_type=F32)


def nn(a, b):
    return lax.dot_general(a, b, (((1,), (0,)), ((), ())), preferred_element_type=F32)


def split_cache_kernel(core_ref, keep_ref, send_ref, keep, send):
    for src, out in ((keep_ref, keep), (send_ref, send)):
        for b in range(2):
            rows = slice(b * BLOCK, (b + 1) * BLOCK)
            out[b, 0] = src[0, rows, 0, :]
            out[b, 1] = src[0, rows, 1, :].T


def split_cache(j, core, rows):
    out = jax.ShapeDtypeStruct((16, 2, BLOCK, HD), BF16)
    block = pl.BlockSpec((2, 2, BLOCK, HD), lambda i, c: (i, 0, 0, 0))
    return pl.pallas_call(
        split_cache_kernel,
        grid_spec=pltpu.PrefetchScalarGridSpec(
            num_scalar_prefetch=1,
            grid=(8,),
            in_specs=[
                pl.BlockSpec((1, 256, 2, HD), lambda i, c: (i // 4, i % 4, 0, 2 * c[0] + j)),
                pl.BlockSpec((1, 256, 2, HD), lambda i, c: (i // 4, i % 4, 0, 2 - 2 * c[0] + j)),
            ],
            out_specs=[block, block],
        ),
        out_shape=[out, out],
        compiler_params=params(),
        cost_estimate=pl.CostEstimate(flops=0, transcendentals=0, bytes_accessed=4 << 20),
        name="split_cache",
    )(core, rows, rows)


def project_kernel(core_ref, tok_ref, gain_ref, wq, wk, wv, q_all, q_send, k_all, v_all, first, last):
    step = pl.program_id(0)
    core = core_ref[0]
    x = tok_ref[...].astype(F32)
    inverse = lax.rsqrt(jnp.mean(x * x, axis=1, keepdims=True) + 1e-05)
    normed = (x * inverse * gain_ref[...]).astype(BF16)
    q = nn(normed, wq[...]).astype(BF16)
    k = nn(normed, wk[...]).astype(BF16)
    v = nn(normed, wv[...])

    def put(shift):
        for h in range(4):
            slot = (h - shift) % 4
            lanes = slice(h * HD, (h + 1) * HD)
            q_all[slot] = q[:, lanes]
            if slot >= 2:
                q_send[slot - 2] = q[:, lanes]
            for b in range(2):
                rows = slice(b * BLOCK, (b + 1) * BLOCK)
                kb = k[rows, lanes]
                vb = v[rows, lanes].T.astype(BF16)
                k_all[slot, b] = kb
                v_all[slot, b] = vb
                if b == 0:
                    @pl.when(step == 0)
                    def _():
                        first[0, slot] = kb
                        first[1, slot] = vb
                else:
                    @pl.when(step == pl.num_programs(0) - 1)
                    def _():
                        last[0, slot] = kb
                        last[1, slot] = vb

    @pl.when(core == 0)
    def _():
        put(0)

    @pl.when(core == 1)
    def _():
        put(2)


def project(core, tokens, gain, wq, wk, wv):
    n, d = tokens.shape
    w = wq.shape[1]
    weight = pl.BlockSpec((d, w), lambda i, c: (0, 0), pipeline_mode=pl.Buffered(1))
    edge = pl.BlockSpec((2, 4, BLOCK, HD), lambda i, c: (0, 0, 0, 0))
    blocks = pl.BlockSpec((4, 2, BLOCK, HD), lambda i, c: (0, i, 0, 0))
    return pl.pallas_call(
        project_kernel,
        grid_spec=pltpu.PrefetchScalarGridSpec(
            num_scalar_prefetch=1,
            grid=(n // 256,),
            in_specs=[
                pl.BlockSpec((256, d), lambda i, c: (i, 0)),
                pl.BlockSpec((1, d), lambda i, c: (0, 0)),
                weight,
                weight,
                weight,
            ],
            out_specs=[
                pl.BlockSpec((4, 256, HD), lambda i, c: (0, i, 0)),
                pl.BlockSpec((2, 256, HD), lambda i, c: (0, i, 0)),
                blocks,
                blocks,
                edge,
                edge,
            ],
        ),
        out_shape=[
            jax.ShapeDtypeStruct((4, n, HD), BF16),
            jax.ShapeDtypeStruct((2, n, HD), BF16),
            jax.ShapeDtypeStruct((4, 8, BLOCK, HD), BF16),
            jax.ShapeDtypeStruct((4, 8, HD, BLOCK), BF16),
            jax.ShapeDtypeStruct((2, 4, BLOCK, HD), BF16),
            jax.ShapeDtypeStruct((2, 4, BLOCK, HD), BF16),
        ],
        compiler_params=params(),
        cost_estimate=pl.CostEstimate(flops=2 * n * d * 3 * w, transcendentals=0, bytes_accessed=16 << 20),
        name="project",
    )(core, tokens, gain.reshape(1, d), wq, wk, wv)


def near_kernel(q_ref, k_ref, v_ref, lo_ref, hi_ref, o_ref, lse_ref):
    for b in range(8):
        q = q_ref[0, b * BLOCK : (b + 1) * BLOCK]
        ks = [lo_ref[0, 0] if b == 0 else k_ref[0, b - 1], k_ref[0, b], hi_ref[0, 0] if b == 7 else k_ref[0, b + 1]]
        vs = [lo_ref[1, 0] if b == 0 else v_ref[0, b - 1], v_ref[0, b], hi_ref[1, 0] if b == 7 else v_ref[0, b + 1]]
        s = [nt(k, q) * SCALE for k in ks]
        m = jnp.max(jnp.maximum(jnp.maximum(s[0], s[1]), s[2]), axis=0, keepdims=True)
        p = [jnp.exp(x - m) for x in s]
        total = jnp.sum(p[0] + p[1] + p[2], axis=0, keepdims=True)
        acc = nn(vs[0], p[0].astype(BF16)) + nn(vs[1], p[1].astype(BF16)) + nn(vs[2], p[2].astype(BF16))
        o_ref[0, b] = acc / total
        lse_ref[0, b : b + 1, :] = m + jnp.log(total)


def near(q, k, v, lo, hi):
    blocks = pl.BlockSpec((1, 8, BLOCK, HD), lambda s: (s, 0, 0, 0))
    edge = pl.BlockSpec((2, 1, BLOCK, HD), lambda s: (0, (s + 2) % 4, 0, 0))
    return pl.pallas_call(
        near_kernel,
        grid=(4,),
        in_specs=[pl.BlockSpec((1, 1024, HD), lambda s: (s, 0, 0)), blocks, blocks, edge, edge],
        out_specs=[blocks, pl.BlockSpec((1, 8, HD), lambda s: (s, 0, 0))],
        out_shape=[jax.ShapeDtypeStruct((4, 8, HD, BLOCK), F32), jax.ShapeDtypeStruct((4, 8, BLOCK), F32)],
        compiler_params=params(),
        cost_estimate=pl.CostEstimate(flops=32 * 384 * 128 * 512, transcendentals=32 * 384 * 128, bytes_accessed=6 << 20),
        name="near",
    )(q, k, v, lo, hi)


GROUP = 4
UNITS = 96 + GROUP


def far_kernel(
    j, cnt_ref, code_ref, *rest,
):
    sources, qs, outs = rest[:8], rest[8:12], rest[12:16]
    kvbuf, qbuf, acc_ref, stat_ref, list_ref, unit_ref, first_ref, kvsem, qsem, logs = rest[16:]
    for r in range(4):
        pltpu.make_async_copy(qs[r].at[:, j], qbuf.at[pl.ds(2 * r, 2)], qsem.at[r]).start()

    def scan(i, carry):
        e, u = carry
        n = cnt_ref[i]
        first_ref[i] = u

        def named(carry):
            e, u = carry
            at = e
            for w in range(WMAX):
                code = code_ref[i * WMAX + w]
                list_ref[at] = code
                at = at + (code >= 0).astype(jnp.int32)

            def unit(k, u):
                both = (2 * k + 1 < n).astype(jnp.int32)
                unit_ref[u] = i * 512 + (e + 2 * k) * 2 + both
                return u + 1

            return at, lax.fori_loop(0, lax.shift_right_logical(n + 1, 1), unit, u)

        return lax.cond(n > 0, named, lambda carry: carry, (e, u))

    entries, units = lax.fori_loop(0, 64, scan, (jnp.int32(0), jnp.int32(0)))
    for g in range(GROUP):
        unit_ref[units + g] = -1

    def fetch(e, _):
        code = list_ref[e]
        at = lax.bitwise_and(code, 15)
        source = lax.shift_right_logical(code, 4)

        def start(lo, hi):
            if hi - lo == 1:
                pltpu.make_async_copy(sources[lo].at[at], kvbuf.at[e], kvsem.at[e]).start()
                return
            mid = (lo + hi) // 2

            @pl.when(source < mid)
            def _():
                start(lo, mid)

            @pl.when(source >= mid)
            def _():
                start(mid, hi)

        start(0, 8)
        return 0

    lax.fori_loop(0, entries, fetch, 0)
    for r in range(4):
        pltpu.make_async_copy(qs[r].at[:, j], qbuf.at[pl.ds(2 * r, 2)], qsem.at[r]).wait()

    def landed(e):
        pltpu.make_async_copy(sources[0].at[0], kvbuf.at[e], kvsem.at[e]).wait()

    def group(g, _):
        live = []
        for t in range(GROUP):
            u = g * GROUP + t
            unit = unit_ref[u]
            here = unit >= 0
            unit = jnp.where(here, unit, unit_ref[g * GROUP])
            both = lax.bitwise_and(unit, 1)
            ea = lax.bitwise_and(lax.shift_right_logical(unit, 1), 255)
            i = lax.shift_right_logical(unit, 9)

            @pl.when(here)
            def _():
                landed(ea)

            @pl.when(jnp.logical_and(here, both == 1))
            def _():
                landed(ea + 1)

            live.append((u, i, ea, ea + both, both == 1))
        for u, i, ea, eb, both in live:
            q = qbuf[lax.shift_right_logical(i, 3), lax.bitwise_and(i, 7)]
            sa = nt(kvbuf[ea, 0], q) * SCALE
            sb = jnp.where(both, nt(kvbuf[eb, 0], q) * SCALE, NEG)
            m = jnp.max(jnp.maximum(sa, sb), axis=0, keepdims=True)
            pa, pb = jnp.exp(sa - m), jnp.exp(sb - m)
            stat_ref[u, 0:1, :] = m
            stat_ref[u, 1:2, :] = jnp.sum(pa + pb, axis=0, keepdims=True)
            acc_ref[u] = nn(kvbuf[ea, 1], pa.astype(BF16)) + nn(kvbuf[eb, 1], pb.astype(BF16))
        return 0

    lax.fori_loop(0, lax.div(units + GROUP - 1, GROUP), group, 0)

    for r in range(4):
        out = outs[r]

        def block(i, _):
            n = cnt_ref[r * 16 + i]
            u = first_ref[r * 16 + i]
            rows = pl.ds(pl.multiple_of(i * HD, HD), HD)

            def store(value, log):
                out[rows, :] = value
                logs[pl.ds(i, 1), :] = log

            @pl.when(n == 0)
            def _():
                store(jnp.zeros((HD, BLOCK), BF16), jnp.full((1, BLOCK), NEG, F32))

            @pl.when(jnp.logical_and(n > 0, n <= 2))
            def _():
                m, total = stat_ref[u, 0:1, :], stat_ref[u, 1:2, :]
                store((acc_ref[u] * (1.0 / total)).astype(BF16), m + jnp.log(total))

            @pl.when(n > 2)
            def _():
                def more(k, carry):
                    m, total, acc = carry
                    mk, tk = stat_ref[k, 0:1, :], stat_ref[k, 1:2, :]
                    top = jnp.maximum(m, mk)
                    old, new = jnp.exp(m - top), jnp.exp(mk - top)
                    return top, total * old + tk * new, acc * old + acc_ref[k] * new

                start = (stat_ref[u, 0:1, :], stat_ref[u, 1:2, :], acc_ref[u])
                m, total, acc = lax.fori_loop(u + 1, u + lax.shift_right_logical(n + 1, 1), more, start)
                store((acc * (1.0 / total)).astype(BF16), m + jnp.log(total))

            return 0

        lax.fori_loop(0, 16, block, 0)
        part = logs[...]
        for t in range(3):
            term = part.astype(BF16)
            out[2048 + t * 16 : 2064 + t * 16, :] = term
            part = part - term.astype(F32)


def far(j, cnt, code, sources, qs):
    out = jax.ShapeDtypeStruct((OROWS, BLOCK), BF16)
    return pl.pallas_call(
        functools.partial(far_kernel, j),
        in_specs=[SMEM, SMEM] + [ANY] * 12,
        out_specs=[pl.BlockSpec((OROWS, BLOCK), lambda: (0, 0))] * 4,
        out_shape=[out] * 4,
        scratch_shapes=[
            pltpu.VMEM((128, 2, BLOCK, HD), BF16),
            pltpu.VMEM((8, 8, BLOCK, HD), BF16),
            pltpu.VMEM((UNITS, HD, BLOCK), F32),
            pltpu.VMEM((UNITS, 8, BLOCK), F32),
            pltpu.SMEM((128 + WMAX,), jnp.int32),
            pltpu.SMEM((UNITS,), jnp.int32),
            pltpu.SMEM((64,), jnp.int32),
            pltpu.SemaphoreType.DMA((128,)),
            pltpu.SemaphoreType.DMA((4,)),
            pltpu.VMEM((16, BLOCK), F32),
        ],
        compiler_params=params(),
        cost_estimate=pl.CostEstimate(flops=64 * 128 * 128 * 512, transcendentals=64 * 128 * 128, bytes_accessed=10 << 20),
        name="far",
    )(cnt, code, *sources, *qs)


def merge_kernel(a, b, c, d, keep, send):
    parts = (a, b, c, d)
    logs = [sum(p[2048 + t * 16 : 2064 + t * 16, :].astype(F32) for t in range(3)) for p in parts]
    peak = functools.reduce(jnp.maximum, logs)
    shares = [jnp.exp(x - peak) for x in logs]
    total = sum(shares)
    shares = [x / total for x in shares]
    joint = peak + jnp.log(total)
    for s, out in enumerate((keep, send)):
        for i in range(8):
            row = s * 8 + i
            rows = slice(row * HD, (row + 1) * HD)
            out[i * HD : (i + 1) * HD, :] = sum(
                x[row : row + 1, :] * p[rows, :].astype(F32) for x, p in zip(shares, parts)
            )
        out[1024:1032, :] = joint[s * 8 : (s + 1) * 8, :]


def merge(parts):
    out = jax.ShapeDtypeStruct((FROWS, BLOCK), F32)
    return pl.pallas_call(
        merge_kernel,
        out_shape=[out, out],
        compiler_params=params(),
        cost_estimate=pl.CostEstimate(flops=1 << 21, transcendentals=1 << 13, bytes_accessed=3 << 20),
        name="merge",
    )(*parts)


def finish_kernel(near_a, lse_a, near_b, lse_b, far_a, far_b, out):
    for s, (o, log, f) in enumerate(((near_a, lse_a, far_a), (near_b, lse_b, far_b))):
        here, away = log[0], f[1024:1032, :]
        peak = jnp.maximum(here, away)
        wn, wf = jnp.exp(here - peak), jnp.exp(away - peak)
        total = wn + wf
        wn, wf = wn / total, wf / total
        for b in range(8):
            both = wn[b : b + 1, :] * o[0, b] + wf[b : b + 1, :] * f[b * HD : (b + 1) * HD, :]
            out[s, b * BLOCK : (b + 1) * BLOCK, :] = both.T.astype(BF16)


def finish(j, o, lse, far_keep, far_other):
    def at(slot):
        return [
            pl.BlockSpec((1, 8, HD, BLOCK), lambda i: (slot, 0, 0, 0)),
            pl.BlockSpec((1, 8, BLOCK), lambda i: (slot, 0, 0)),
        ]

    whole = pl.BlockSpec((FROWS, BLOCK), lambda i: (0, 0))
    return pl.pallas_call(
        finish_kernel,
        grid=(1,),
        in_specs=at(j) + at(2 + j) + [whole, whole],
        out_specs=pl.BlockSpec((2, 1024, HD), lambda i: (0, 0, 0)),
        out_shape=jax.ShapeDtypeStruct((2, 1024, HD), BF16),
        compiler_params=params(),
        cost_estimate=pl.CostEstimate(flops=1 << 21, transcendentals=1 << 13, bytes_accessed=3 << 20),
        name="finish",
    )(o, lse, o, lse, far_keep, far_other)


def mix_kernel(last, place_ref, a0, a1, a2, a3, *rest):
    weights, carried, out = rest[:8], rest[8], rest[-1]
    total = carried[...].astype(F32) if carried is not out else None
    left = jnp.concatenate([a[s] for a in (a0, a1, a2, a3) for s in range(2)], axis=1)
    term = nn(left, jnp.concatenate([w[...] for w in weights], axis=0))
    total = term if total is None else total + term
    if last:
        total = total + rest[9][...]
    out[...] = total.astype(out.dtype)


def mix(j, place, parts, w_out, carried, acc=None):
    n, cols = 1024, 512

    def weight(rel, s):
        def at(i, p):
            head = (2 * p[0] + 2 * s + j) % 4
            return ((p[1] + rel) % NX * 4 + head, p[1])

        return pl.BlockSpec((HD, cols), at)

    last = acc is not None
    in_specs = [pl.BlockSpec((2, 256, HD), lambda i, p: (0, i, 0))] * 4
    in_specs += [weight(rel, s) for rel in range(4) for s in range(2)]
    args = list(parts) + [w_out] * 8
    if last:
        in_specs.append(pl.BlockSpec((256, cols), lambda i, p: (i, p[1])))
        in_specs.append(pl.BlockSpec((256, cols), lambda i, p: (i, 0)))
        args += [carried, acc]
    return pl.pallas_call(
        functools.partial(mix_kernel, last),
        grid_spec=pltpu.PrefetchScalarGridSpec(
            num_scalar_prefetch=1,
            grid=(n // 256,),
            in_specs=in_specs,
            out_specs=pl.BlockSpec((256, cols), lambda i, p: (i, 0)),
        ),
        out_shape=jax.ShapeDtypeStruct((n, cols), BF16 if last else F32),
        compiler_params=params(),
        cost_estimate=pl.CostEstimate(flops=2 * n * 1024 * cols, transcendentals=0, bytes_accessed=6 << 20),
        name="mix",
    )(place, *args)


def line_codes(wake_blocks, wake_frames, wake_counts, y, z, c):
    live = jnp.arange(WMAX, dtype=jnp.int32)[None, :] < wake_counts[:, None]
    word = jnp.where(live, wake_frames * 256 + wake_blocks, -1).reshape(NY, NZ, NC, 8, WMAX)
    by_y = lax.dynamic_index_in_dim(word, y, 0, keepdims=False)
    by_z = lax.dynamic_index_in_dim(word, z, 1, keepdims=False)
    here = jnp.where(c == 0, by_y, by_z)
    here = lax.dynamic_slice_in_dim(jnp.concatenate([here, here], axis=0), jnp.where(c == 0, z, y), 4, 0)
    here = lax.dynamic_slice_in_dim(jnp.concatenate([here, here], axis=1), c, 2, 1)
    word = here.reshape(64, WMAX)
    block, frame = word & 255, word >> 8
    hc, hz, hy = (block >> 3) & 1, (block >> 4) & 3, (block >> 6) & 3
    in_line = (word >= 0) & (jnp.where(c == 0, hz, hy) == jnp.where(c == 0, z, y))
    piece = (jnp.where(c == 0, hy, hz) - jnp.where(c == 0, y, z)) & 3
    code = piece * 32 + (hc ^ c) * 16 + (frame & 1) * 8 + (block & 7)
    code = jnp.where(in_line, code, -1)
    return code.reshape(512), jnp.sum(in_line.astype(jnp.int32), axis=1)


def on_device(tokens, norm_gain, w_query, w_key, w_value, w_out, kv_cache, wake_blocks, wake_frames, wake_counts):
    tok = lax.axis_index("tok").astype(jnp.int32)
    mp = lax.axis_index("mp").astype(jnp.int32)
    c, z, y = tok % NC, (tok // NC) % NZ, tok // (NC * NZ)
    core = c.reshape(1)
    place = jnp.stack([c, mp])

    def after(x, *deps):
        return lax.optimization_barrier((x, *deps))[0]

    keep, send = [None, None], [None, None]
    keep[0], send[0] = split_cache(0, core, kv_cache)
    up_k, down_k = [rows_perm(keep[0], 1), None], [rows_perm(keep[0], -1), None]
    got = [core_swap(send[0]), None]
    up_r, down_r = [rows_perm(got[0], 1), None], [rows_perm(got[0], -1), None]
    keep[1], send[1] = split_cache(1, core, kv_cache)
    got[1] = core_swap(send[1])

    q_all, q_send, k_all, v_all, first, last = project(core, tokens, norm_gain, w_query, w_key, w_value)
    mine = jnp.concatenate([q_all[:2], core_swap(q_send)], axis=0).reshape(2, 2, 8, BLOCK, HD)
    qs = [mine, query_perm(mine, -1), query_perm(mine, 2), query_perm(mine, 1)]
    lo, hi = ring_perm(last, 1), ring_perm(first, -1)
    code, cnt = line_codes(wake_blocks, wake_frames, wake_counts, y, z, c)
    near_o, near_lse = near(q_all, k_all, v_all, lo, hi)

    keep[1], got[1] = lax.optimization_barrier((keep[1], got[1], up_k[0], down_r[0]))[:2]
    up_k[1], down_k[1] = rows_perm(keep[1], 1), rows_perm(keep[1], -1)
    up_r[1], down_r[1] = rows_perm(got[1], 1), rows_perm(got[1], -1)

    acc = None
    parts = None
    for j in range(2):
        if parts is not None:
            up_k[j], down_r[j] = lax.optimization_barrier((up_k[j], down_r[j], parts[0]))[:2]
        up2, down2 = rows_perm(up_k[j], 1), rows_perm(down_r[j], -1)
        sources = [keep[j], got[j], down_k[j], down_r[j], up2, down2, up_k[j], up_r[j]]
        if j == 0:
            near_o, near_lse, sources[0] = lax.optimization_barrier((near_o, near_lse, sources[0]))
        parts = far(j, cnt, code, sources, qs)
        back = [parts[0], query_perm(parts[1], 1), query_perm(parts[2], 2), query_perm(parts[3], -1)]
        own, other = merge(back)
        heads = finish(j, near_o, near_lse, own, core_swap(other))
        gathered = [heads, mp_perm(heads, -1), mp_perm(heads, 2), mp_perm(heads, 1)]
        acc = mix(j, place, gathered, w_out, tokens, acc)
    return acc


def solution(mesh):
    return jax.shard_map(
        on_device,
        mesh=mesh,
        in_specs=(
            P("tok", None),
            P(),
            P(None, "mp"),
            P(None, "mp"),
            P(None, "mp"),
            P(),
            P(None, "tok", None, "mp"),
            P(),
            P(),
            P(),
        ),
        out_specs=P("tok", "mp"),
        check_vma=False,
    )
```

```python
import functools
import math

import jax
import jax.numpy as jnp
from jax import lax
from jax.experimental import pallas as pl
from jax.experimental.pallas import tpu as pltpu
from jax.sharding import PartitionSpec as P

HD = 128
BLOCK = 128
WMAX = 8
NEG = -1e30
SCALE = 1.0 / math.sqrt(HD)
NY, NZ, NC, NX = 4, 4, 2, 4
F32, BF16 = jnp.float32, jnp.bfloat16
ANY = pl.BlockSpec(memory_space=pl.ANY)
SMEM = pl.BlockSpec(memory_space=pltpu.SMEM)
BRIEF = pl.CostEstimate(flops=1, transcendentals=0, bytes_accessed=1)
OROWS = 2048 + 48
FROWS = 1024 + 8


def params(mib=48):
    return pltpu.CompilerParams(vmem_limit_bytes=mib << 20)


def tok_of(y, z, c):
    return ((y % NY) * NZ + z % NZ) * NC + c % NC


def chips():
    return [(y, z, c) for y in range(NY) for z in range(NZ) for c in range(NC)]


def rows_perm(x, d):
    pairs = [(tok_of(y, z, c), tok_of(y + d, z, c) if c == 0 else tok_of(y, z + d, c)) for y, z, c in chips()]
    return lax.ppermute(x, "tok", pairs)


def query_perm(x, d):
    pairs = [(tok_of(y, z, c), tok_of(y, z + d, c) if c == 0 else tok_of(y + d, z, c)) for y, z, c in chips()]
    return lax.ppermute(x, "tok", pairs)


def core_swap(x):
    return lax.ppermute(x, "tok", [(tok_of(y, z, c), tok_of(y, z, 1 - c)) for y, z, c in chips()])


def halo_perm(x):
    n = NY * NZ * NC
    return lax.ppermute(x, "tok", [(i, (i + (1 if i % 2 else -1)) % n) for i in range(n)])


def mp_perm(x, d):
    return lax.ppermute(x, "mp", [(i, (i + d) % NX) for i in range(NX)])


def nt(a, b):
    return lax.dot_general(a, b, (((1,), (1,)), ((), ())), preferred_element_type=F32)


def nn(a, b):
    return lax.dot_general(a, b, (((1,), (0,)), ((), ())), preferred_element_type=F32)


def split_cache_kernel(core_ref, keep_ref, send_ref, keep, send):
    for src, out in ((keep_ref, keep), (send_ref, send)):
        for b in range(2):
            rows = slice(b * BLOCK, (b + 1) * BLOCK)
            out[b, 0] = src[0, rows, 0, :]
            out[b, 1] = src[0, rows, 1, :].T


def split_cache(j, core, rows):
    out = jax.ShapeDtypeStruct((16, 2, BLOCK, HD), BF16)
    block = pl.BlockSpec((2, 2, BLOCK, HD), lambda i, c: (i, 0, 0, 0))
    return pl.pallas_call(
        split_cache_kernel,
        grid_spec=pltpu.PrefetchScalarGridSpec(
            num_scalar_prefetch=1,
            grid=(8,),
            in_specs=[
                pl.BlockSpec((1, 256, 2, HD), lambda i, c: (i // 4, i % 4, 0, 2 * c[0] + j)),
                pl.BlockSpec((1, 256, 2, HD), lambda i, c: (i // 4, i % 4, 0, 2 - 2 * c[0] + j)),
            ],
            out_specs=[block, block],
        ),
        out_shape=[out, out],
        compiler_params=params(),
        cost_estimate=BRIEF,
        name="split_cache",
    )(core, rows, rows)


def project_kernel(core_ref, tok_ref, gain_ref, wq, wk, wv, q_all, swap, k_all, v_all, edge):
    step = pl.program_id(0)
    core = core_ref[0]
    x = tok_ref[...].astype(F32)
    inverse = lax.rsqrt(jnp.mean(x * x, axis=1, keepdims=True) + 1e-05)
    normed = (x * inverse * gain_ref[...]).astype(BF16)
    q = nn(normed, wq[...]).astype(BF16)
    k = nn(normed, wk[...]).astype(BF16)
    v = nn(normed, wv[...])

    def put(here):
        to_first = swap if here else edge
        to_last = edge if here else swap
        for h in range(4):
            slot = (h - 2 * here) % 4
            lanes = slice(h * HD, (h + 1) * HD)
            q_all[slot] = q[:, lanes]
            if slot >= 2:
                swap[pl.ds((slot - 2) * 1024 + pl.multiple_of(step * 256, 256), 256), :] = q[:, lanes]
            for b in range(2):
                rows = slice(b * BLOCK, (b + 1) * BLOCK)
                kb = k[rows, lanes]
                vb = v[rows, lanes].T.astype(BF16)
                k_all[slot, b] = kb
                v_all[slot, b] = vb
                out, when = (to_first, 0) if b == 0 else (to_last, pl.num_programs(0) - 1)
                base = 2048 if out is swap else 0

                @pl.when(step == when)
                def _():
                    out[base + slot * HD : base + (slot + 1) * HD, :] = kb
                    out[base + (4 + slot) * HD : base + (5 + slot) * HD, :] = vb

    @pl.when(core == 0)
    def _():
        put(0)

    @pl.when(core == 1)
    def _():
        put(1)


def project(core, tokens, gain, wq, wk, wv):
    n, d = tokens.shape
    w = wq.shape[1]
    weight = pl.BlockSpec((d, w), lambda i, c: (0, 0), pipeline_mode=pl.Buffered(1))
    blocks = pl.BlockSpec((4, 2, BLOCK, HD), lambda i, c: (0, i, 0, 0))
    return pl.pallas_call(
        project_kernel,
        grid_spec=pltpu.PrefetchScalarGridSpec(
            num_scalar_prefetch=1,
            grid=(n // 256,),
            in_specs=[
                pl.BlockSpec((256, d), lambda i, c: (i, 0)),
                pl.BlockSpec((1, d), lambda i, c: (0, 0)),
                weight,
                weight,
                weight,
            ],
            out_specs=[
                pl.BlockSpec((4, 256, HD), lambda i, c: (0, i, 0)),
                pl.BlockSpec((3072, HD), lambda i, c: (0, 0)),
                blocks,
                blocks,
                pl.BlockSpec((1024, HD), lambda i, c: (0, 0)),
            ],
        ),
        out_shape=[
            jax.ShapeDtypeStruct((4, n, HD), BF16),
            jax.ShapeDtypeStruct((3072, HD), BF16),
            jax.ShapeDtypeStruct((4, 8, BLOCK, HD), BF16),
            jax.ShapeDtypeStruct((4, 8, HD, BLOCK), BF16),
            jax.ShapeDtypeStruct((1024, HD), BF16),
        ],
        compiler_params=params(),
        cost_estimate=BRIEF,
        name="project",
    )(core, tokens, gain.reshape(1, d), wq, wk, wv)


def near_kernel(core_ref, q_ref, k_ref, v_ref, ka, va, kb, vb, o_ref, lse_ref):
    first = core_ref[0] == 0
    klo, khi = jnp.where(first, ka[0], kb[0]), jnp.where(first, kb[0], ka[0])
    vlo, vhi = jnp.where(first, va[0], vb[0]), jnp.where(first, vb[0], va[0])
    for b in range(8):
        q = q_ref[0, b * BLOCK : (b + 1) * BLOCK]
        ks = [klo if b == 0 else k_ref[0, b - 1], k_ref[0, b], khi if b == 7 else k_ref[0, b + 1]]
        vs = [vlo if b == 0 else v_ref[0, b - 1], v_ref[0, b], vhi if b == 7 else v_ref[0, b + 1]]
        s = [nt(k, q) * SCALE for k in ks]
        m = jnp.max(jnp.maximum(jnp.maximum(s[0], s[1]), s[2]), axis=0, keepdims=True)
        p = [jnp.exp(x - m) for x in s]
        total = jnp.sum(p[0] + p[1] + p[2], axis=0, keepdims=True)
        acc = nn(vs[0], p[0].astype(BF16)) + nn(vs[1], p[1].astype(BF16)) + nn(vs[2], p[2].astype(BF16))
        o_ref[0, b] = acc / total
        lse_ref[0, b : b + 1, :] = m + jnp.log(total)


def near(core, q, k, v, halo, swapped):
    blocks = pl.BlockSpec((1, 8, BLOCK, HD), lambda s, c: (s, 0, 0, 0))

    def edge(first):
        return pl.BlockSpec((1, BLOCK, HD), lambda s, c: (first + (s + 2) % 4, 0, 0))

    return pl.pallas_call(
        near_kernel,
        grid_spec=pltpu.PrefetchScalarGridSpec(
            num_scalar_prefetch=1,
            grid=(4,),
            in_specs=[pl.BlockSpec((1, 1024, HD), lambda s, c: (s, 0, 0)), blocks, blocks]
            + [edge(0), edge(4), edge(16), edge(20)],
            out_specs=[blocks, pl.BlockSpec((1, 8, HD), lambda s, c: (s, 0, 0))],
        ),
        out_shape=[jax.ShapeDtypeStruct((4, 8, HD, BLOCK), F32), jax.ShapeDtypeStruct((4, 8, BLOCK), F32)],
        compiler_params=params(),
        cost_estimate=BRIEF,
        name="near",
    )(core, q, k, v, halo.reshape(8, BLOCK, HD), halo.reshape(8, BLOCK, HD), swapped.reshape(24, BLOCK, HD), swapped.reshape(24, BLOCK, HD))


GROUP = 4
UNITS = 96 + GROUP


def plan_kernel(cnt_ref, code_ref, list_ref, unit_ref, first_ref, size_ref):
    def scan(i, carry):
        e, u = carry
        n = cnt_ref[i]
        first_ref[i] = u

        def named(carry):
            e, u = carry
            at = e
            for w in range(WMAX):
                code = code_ref[i * WMAX + w]
                list_ref[at] = code
                at = at + (code >= 0).astype(jnp.int32)

            def unit(k, u):
                both = (2 * k + 1 < n).astype(jnp.int32)
                unit_ref[u] = i * 512 + (e + 2 * k) * 2 + both
                return u + 1

            return at, lax.fori_loop(0, lax.shift_right_logical(n + 1, 1), unit, u)

        return lax.cond(n > 0, named, lambda carry: carry, (e, u))

    entries, units = lax.fori_loop(0, 64, scan, (jnp.int32(0), jnp.int32(0)))
    for g in range(GROUP):
        unit_ref[units + g] = -1
    size_ref[0] = entries
    size_ref[1] = units


def plan(cnt, code):
    def out(n):
        return jax.ShapeDtypeStruct((n,), jnp.int32)

    return pl.pallas_call(
        plan_kernel,
        in_specs=[SMEM] * 2,
        out_specs=[SMEM] * 4,
        out_shape=[out(128 + WMAX), out(UNITS), out(64), out(2)],
        compiler_params=params(16),
        cost_estimate=BRIEF,
        name="plan",
    )(cnt, code)


def far_kernel(j, cnt_ref, list_ref, unit_ref, first_ref, size_ref, *rest):
    sources, qs, outs = rest[:8], rest[8:12], rest[12:16]
    kvbuf, qbuf, acc_ref, stat_ref, kvsem, qsem, logs = rest[16:]
    entries, units = size_ref[0], size_ref[1]
    for r in range(4):
        pltpu.make_async_copy(qs[r].at[:, j], qbuf.at[pl.ds(2 * r, 2)], qsem.at[r]).start()

    def fetch(e, _):
        code = list_ref[e]
        at = lax.bitwise_and(code, 15)
        source = lax.shift_right_logical(code, 4)

        def start(lo, hi):
            if hi - lo == 1:
                pltpu.make_async_copy(sources[lo].at[at], kvbuf.at[e], kvsem.at[e]).start()
                return
            mid = (lo + hi) // 2

            @pl.when(source < mid)
            def _():
                start(lo, mid)

            @pl.when(source >= mid)
            def _():
                start(mid, hi)

        start(0, 8)
        return 0

    lax.fori_loop(0, entries, fetch, 0)
    for r in range(4):
        pltpu.make_async_copy(qs[r].at[:, j], qbuf.at[pl.ds(2 * r, 2)], qsem.at[r]).wait()

    def landed(e):
        pltpu.make_async_copy(sources[0].at[0], kvbuf.at[e], kvsem.at[e]).wait()

    def group(g, _):
        live = []
        for t in range(GROUP):
            u = g * GROUP + t
            unit = unit_ref[u]
            here = unit >= 0
            unit = jnp.where(here, unit, unit_ref[g * GROUP])
            both = lax.bitwise_and(unit, 1)
            ea = lax.bitwise_and(lax.shift_right_logical(unit, 1), 255)
            i = lax.shift_right_logical(unit, 9)

            @pl.when(here)
            def _():
                landed(ea)

            @pl.when(jnp.logical_and(here, both == 1))
            def _():
                landed(ea + 1)

            live.append((u, i, ea, ea + both, both == 1))
        for u, i, ea, eb, both in live:
            q = qbuf[lax.shift_right_logical(i, 3), lax.bitwise_and(i, 7)]
            sa = nt(kvbuf[ea, 0], q) * SCALE
            sb = jnp.where(both, nt(kvbuf[eb, 0], q) * SCALE, NEG)
            m = jnp.max(jnp.maximum(sa, sb), axis=0, keepdims=True)
            pa, pb = jnp.exp(sa - m), jnp.exp(sb - m)
            stat_ref[u, 0:1, :] = m
            stat_ref[u, 1:2, :] = jnp.sum(pa + pb, axis=0, keepdims=True)
            acc_ref[u] = nn(kvbuf[ea, 1], pa.astype(BF16)) + nn(kvbuf[eb, 1], pb.astype(BF16))
        return 0

    lax.fori_loop(0, lax.div(units + GROUP - 1, GROUP), group, 0)

    for r in range(4):
        out = outs[r]

        def block(i, _):
            n = cnt_ref[r * 16 + i]
            u = first_ref[r * 16 + i]
            rows = pl.ds(pl.multiple_of(i * HD, HD), HD)

            def store(value, log):
                out[rows, :] = value
                logs[pl.ds(i, 1), :] = log

            @pl.when(n == 0)
            def _():
                store(jnp.zeros((HD, BLOCK), BF16), jnp.full((1, BLOCK), NEG, F32))

            @pl.when(jnp.logical_and(n > 0, n <= 2))
            def _():
                m, total = stat_ref[u, 0:1, :], stat_ref[u, 1:2, :]
                store((acc_ref[u] * (1.0 / total)).astype(BF16), m + jnp.log(total))

            @pl.when(n > 2)
            def _():
                def more(k, carry):
                    m, total, acc = carry
                    mk, tk = stat_ref[k, 0:1, :], stat_ref[k, 1:2, :]
                    top = jnp.maximum(m, mk)
                    old, new = jnp.exp(m - top), jnp.exp(mk - top)
                    return top, total * old + tk * new, acc * old + acc_ref[k] * new

                start = (stat_ref[u, 0:1, :], stat_ref[u, 1:2, :], acc_ref[u])
                m, total, acc = lax.fori_loop(u + 1, u + lax.shift_right_logical(n + 1, 1), more, start)
                store((acc * (1.0 / total)).astype(BF16), m + jnp.log(total))

            return 0

        lax.fori_loop(0, 16, block, 0)
        part = logs[...]
        for t in range(3):
            term = part.astype(BF16)
            out[2048 + t * 16 : 2064 + t * 16, :] = term
            part = part - term.astype(F32)


def far(j, cnt, lists, sources, qs):
    out = jax.ShapeDtypeStruct((OROWS, BLOCK), BF16)
    return pl.pallas_call(
        functools.partial(far_kernel, j),
        in_specs=[SMEM] * 5 + [ANY] * 12,
        out_specs=[pl.BlockSpec((OROWS, BLOCK), lambda: (0, 0))] * 4,
        out_shape=[out] * 4,
        scratch_shapes=[
            pltpu.VMEM((128, 2, BLOCK, HD), BF16),
            pltpu.VMEM((8, 8, BLOCK, HD), BF16),
            pltpu.VMEM((UNITS, HD, BLOCK), F32),
            pltpu.VMEM((UNITS, 8, BLOCK), F32),
            pltpu.SemaphoreType.DMA((128,)),
            pltpu.SemaphoreType.DMA((4,)),
            pltpu.VMEM((16, BLOCK), F32),
        ],
        compiler_params=params(),
        cost_estimate=BRIEF,
        name="far",
    )(cnt, *lists, *sources, *qs)


def merge_kernel(a, b, c, d, keep, send):
    parts = (a, b, c, d)
    logs = [sum(p[2048 + t * 16 : 2064 + t * 16, :].astype(F32) for t in range(3)) for p in parts]
    peak = functools.reduce(jnp.maximum, logs)
    shares = [jnp.exp(x - peak) for x in logs]
    total = sum(shares)
    shares = [x / total for x in shares]
    joint = peak + jnp.log(total)
    for s, out in enumerate((keep, send)):
        for i in range(8):
            row = s * 8 + i
            rows = slice(row * HD, (row + 1) * HD)
            out[i * HD : (i + 1) * HD, :] = sum(
                x[row : row + 1, :] * p[rows, :].astype(F32) for x, p in zip(shares, parts)
            )
        out[1024:1032, :] = joint[s * 8 : (s + 1) * 8, :]


def merge(parts):
    out = jax.ShapeDtypeStruct((FROWS, BLOCK), F32)
    return pl.pallas_call(
        merge_kernel,
        out_shape=[out, out],
        compiler_params=params(),
        cost_estimate=BRIEF,
        name="merge",
    )(*parts)


def finish_kernel(near_a, lse_a, near_b, lse_b, far_a, far_b, out):
    for s, (o, log, f) in enumerate(((near_a, lse_a, far_a), (near_b, lse_b, far_b))):
        here, away = log[0], f[1024:1032, :]
        peak = jnp.maximum(here, away)
        wn, wf = jnp.exp(here - peak), jnp.exp(away - peak)
        total = wn + wf
        wn, wf = wn / total, wf / total
        for b in range(8):
            both = wn[b : b + 1, :] * o[0, b] + wf[b : b + 1, :] * f[b * HD : (b + 1) * HD, :]
            out[s, b * BLOCK : (b + 1) * BLOCK, :] = both.T.astype(BF16)


def finish(j, o, lse, far_keep, far_other):
    def at(slot):
        return [
            pl.BlockSpec((1, 8, HD, BLOCK), lambda i: (slot, 0, 0, 0)),
            pl.BlockSpec((1, 8, BLOCK), lambda i: (slot, 0, 0)),
        ]

    whole = pl.BlockSpec((FROWS, BLOCK), lambda i: (0, 0))
    return pl.pallas_call(
        finish_kernel,
        grid=(1,),
        in_specs=at(j) + at(2 + j) + [whole, whole],
        out_specs=pl.BlockSpec((2, 1024, HD), lambda i: (0, 0, 0)),
        out_shape=jax.ShapeDtypeStruct((2, 1024, HD), BF16),
        compiler_params=params(),
        cost_estimate=BRIEF,
        name="finish",
    )(o, lse, o, lse, far_keep, far_other)


def mix_kernel(last, place_ref, a0, a1, a2, a3, *rest):
    weights, carried, out = rest[:8], rest[8], rest[-1]
    total = carried[...].astype(F32) if carried is not out else None
    left = jnp.concatenate([a[s] for a in (a0, a1, a2, a3) for s in range(2)], axis=1)
    term = nn(left, jnp.concatenate([w[...] for w in weights], axis=0))
    total = term if total is None else total + term
    if last:
        total = total + rest[9][...]
    out[...] = total.astype(out.dtype)


def mix(j, place, parts, w_out, carried, acc=None):
    n, cols = 1024, 512

    def weight(rel, s):
        def at(i, p):
            head = (2 * p[0] + 2 * s + j) % 4
            return ((p[1] + rel) % NX * 4 + head, p[1])

        return pl.BlockSpec((HD, cols), at)

    last = acc is not None
    in_specs = [pl.BlockSpec((2, 256, HD), lambda i, p: (0, i, 0))] * 4
    in_specs += [weight(rel, s) for rel in range(4) for s in range(2)]
    args = list(parts) + [w_out] * 8
    if last:
        in_specs.append(pl.BlockSpec((256, cols), lambda i, p: (i, p[1])))
        in_specs.append(pl.BlockSpec((256, cols), lambda i, p: (i, 0)))
        args += [carried, acc]
    return pl.pallas_call(
        functools.partial(mix_kernel, last),
        grid_spec=pltpu.PrefetchScalarGridSpec(
            num_scalar_prefetch=1,
            grid=(n // 256,),
            in_specs=in_specs,
            out_specs=pl.BlockSpec((256, cols), lambda i, p: (i, 0)),
        ),
        out_shape=jax.ShapeDtypeStruct((n, cols), BF16 if last else F32),
        compiler_params=params(),
        cost_estimate=BRIEF,
        name="mix",
    )(place, *args)


def line_codes(wake_blocks, wake_frames, wake_counts, y, z, c):
    live = jnp.arange(WMAX, dtype=jnp.int32)[None, :] < wake_counts[:, None]
    word = jnp.where(live, wake_frames * 256 + wake_blocks, -1).reshape(NY, NZ, NC, 8, WMAX)
    by_y = lax.dynamic_index_in_dim(word, y, 0, keepdims=False)
    by_z = lax.dynamic_index_in_dim(word, z, 1, keepdims=False)
    here = jnp.where(c == 0, by_y, by_z)
    here = lax.dynamic_slice_in_dim(jnp.concatenate([here, here], axis=0), jnp.where(c == 0, z, y), 4, 0)
    here = lax.dynamic_slice_in_dim(jnp.concatenate([here, here], axis=1), c, 2, 1)
    word = here.reshape(64, WMAX)
    block, frame = word & 255, word >> 8
    hc, hz, hy = (block >> 3) & 1, (block >> 4) & 3, (block >> 6) & 3
    in_line = (word >= 0) & (jnp.where(c == 0, hz, hy) == jnp.where(c == 0, z, y))
    piece = (jnp.where(c == 0, hy, hz) - jnp.where(c == 0, y, z)) & 3
    code = piece * 32 + (hc ^ c) * 16 + (frame & 1) * 8 + (block & 7)
    code = jnp.where(in_line, code, -1)
    return code.reshape(512), jnp.sum(in_line.astype(jnp.int32), axis=1)


def on_device(tokens, norm_gain, w_query, w_key, w_value, w_out, kv_cache, wake_blocks, wake_frames, wake_counts):
    tok = lax.axis_index("tok").astype(jnp.int32)
    mp = lax.axis_index("mp").astype(jnp.int32)
    c, z, y = tok % NC, (tok // NC) % NZ, tok // (NC * NZ)
    core = c.reshape(1)
    place = jnp.stack([c, mp])

    def after(x, *deps):
        return lax.optimization_barrier((x, *deps))[0]

    keep0, send0 = split_cache(0, core, kv_cache)
    up_k0, down_k0 = rows_perm(keep0, 1), rows_perm(keep0, -1)
    got0 = core_swap(send0)
    up_r0, down_r0 = rows_perm(got0, 1), rows_perm(got0, -1)

    gain = after(norm_gain, got0)
    q_all, swap, k_all, v_all, edge = project(core, tokens, gain, w_query, w_key, w_value)
    swapped, halo = core_swap(swap), halo_perm(edge)
    up20 = rows_perm(after(up_k0, edge), 1)
    mine = jnp.concatenate([q_all[:2], swapped[:2048].reshape(2, 1024, HD)], axis=0).reshape(2, 2, 8, BLOCK, HD)
    mine, halo, down_k0, up_r0, down_r0 = lax.optimization_barrier((mine, halo, down_k0, up_r0, down_r0))
    down20 = rows_perm(down_r0, -1)
    qs = [mine, query_perm(mine, -1), query_perm(mine, 2), query_perm(mine, 1)]

    core1 = after(core, mine)
    keep1, send1 = split_cache(1, core1, kv_cache)
    code, cnt = line_codes(wake_blocks, wake_frames, wake_counts, y, z, c)
    lists = plan(cnt, code)
    send1, up20, down20 = lax.optimization_barrier((send1, up20, down20))
    got1 = core_swap(send1)
    near_o, near_lse = near(core, q_all, k_all, v_all, after(halo, keep1), swapped)
    keep1, got1, near_o, near_lse, *qs = lax.optimization_barrier((keep1, got1, near_o, near_lse, *qs))
    up_k1, down_k1 = rows_perm(keep1, 1), rows_perm(keep1, -1)
    up_r1, down_r1 = rows_perm(got1, 1), rows_perm(got1, -1)

    def returned(parts):
        return [parts[0], query_perm(parts[1], 1), query_perm(parts[2], 2), query_perm(parts[3], -1)]

    def gather(heads):
        return [heads, mp_perm(heads, -1), mp_perm(heads, 2), mp_perm(heads, 1)]

    sources = [keep0, got0, down_k0, down_r0, up20, down20, up_k0, up_r0]
    parts = far(0, cnt, lists, sources, qs)
    *parts, up_k1, down_k1 = lax.optimization_barrier((*parts, up_k1, down_k1))
    back = returned(parts)
    up21 = rows_perm(up_k1, 1)
    back[0], down_k1, up_r1, down_r1 = lax.optimization_barrier((back[0], down_k1, up_r1, down_r1))
    down21 = rows_perm(down_r1, -1)
    own, other = merge(back)
    heads = finish(0, near_o, near_lse, own, core_swap(other))
    gathered = gather(heads)

    sources = [after(keep1, heads), got1, down_k1, down_r1, up21, down21, up_k1, up_r1]
    parts = far(1, cnt, lists, sources, qs)
    back = returned(parts)
    gathered[0] = after(gathered[0], parts[0])
    acc = mix(0, place, gathered, w_out, tokens, None)
    back[0], acc = lax.optimization_barrier((back[0], acc))
    own, other = merge(back)
    heads = finish(1, near_o, near_lse, own, core_swap(other))
    return mix(1, place, gather(heads), w_out, tokens, acc)


def solution(mesh):
    return jax.shard_map(
        on_device,
        mesh=mesh,
        in_specs=(
            P("tok", None),
            P(),
            P(None, "mp"),
            P(None, "mp"),
            P(None, "mp"),
            P(),
            P(None, "tok", None, "mp"),
            P(),
            P(),
            P(),
        ),
        out_specs=P("tok", "mp"),
        check_vma=False,
    )
```

```python
import functools
import math

import jax
import jax.numpy as jnp
from jax import lax
from jax.experimental import pallas as pl
from jax.experimental.pallas import tpu as pltpu
from jax.sharding import PartitionSpec as P

HD = 128
BLOCK = 128
WMAX = 8
NEG = -1e30
SCALE = 1.0 / math.sqrt(HD)
NY, NZ, NC, NX = 4, 4, 2, 4
F32, BF16 = jnp.float32, jnp.bfloat16
ANY = pl.BlockSpec(memory_space=pl.ANY)
SMEM = pl.BlockSpec(memory_space=pltpu.SMEM)
BRIEF = pl.CostEstimate(flops=1, transcendentals=0, bytes_accessed=1)
OROWS = 2048 + 48
FROWS = 1024 + 8


def params(mib=48):
    return pltpu.CompilerParams(vmem_limit_bytes=mib << 20)


def tok_of(y, z, c):
    return ((y % NY) * NZ + z % NZ) * NC + c % NC


def chips():
    return [(y, z, c) for y in range(NY) for z in range(NZ) for c in range(NC)]


def rows_perm(x, d):
    pairs = [(tok_of(y, z, c), tok_of(y + d, z, c) if c == 0 else tok_of(y, z + d, c)) for y, z, c in chips()]
    return lax.ppermute(x, "tok", pairs)


def query_perm(x, d):
    pairs = [(tok_of(y, z, c), tok_of(y, z + d, c) if c == 0 else tok_of(y + d, z, c)) for y, z, c in chips()]
    return lax.ppermute(x, "tok", pairs)


def core_swap(x):
    return lax.ppermute(x, "tok", [(tok_of(y, z, c), tok_of(y, z, 1 - c)) for y, z, c in chips()])


def halo_perm(x):
    n = NY * NZ * NC
    return lax.ppermute(x, "tok", [(i, (i + (1 if i % 2 else -1)) % n) for i in range(n)])


def mp_perm(x, d):
    return lax.ppermute(x, "mp", [(i, (i + d) % NX) for i in range(NX)])


def nt(a, b):
    return lax.dot_general(a, b, (((1,), (1,)), ((), ())), preferred_element_type=F32)


def nn(a, b):
    return lax.dot_general(a, b, (((1,), (0,)), ((), ())), preferred_element_type=F32)


def split_cache_kernel(core_ref, keep_ref, send_ref, keep, send):
    for src, out in ((keep_ref, keep), (send_ref, send)):
        for b in range(2):
            rows = slice(b * BLOCK, (b + 1) * BLOCK)
            out[b, 0] = src[0, rows, 0, :]
            out[b, 1] = src[0, rows, 1, :].T


def split_cache(j, core, rows):
    out = jax.ShapeDtypeStruct((16, 2, BLOCK, HD), BF16)
    block = pl.BlockSpec((2, 2, BLOCK, HD), lambda i, c: (i, 0, 0, 0))
    return pl.pallas_call(
        split_cache_kernel,
        grid_spec=pltpu.PrefetchScalarGridSpec(
            num_scalar_prefetch=1,
            grid=(8,),
            in_specs=[
                pl.BlockSpec((1, 256, 2, HD), lambda i, c: (i // 4, i % 4, 0, 2 * c[0] + j)),
                pl.BlockSpec((1, 256, 2, HD), lambda i, c: (i // 4, i % 4, 0, 2 - 2 * c[0] + j)),
            ],
            out_specs=[block, block],
        ),
        out_shape=[out, out],
        compiler_params=params(),
        cost_estimate=BRIEF,
        name="split_cache",
    )(core, rows, rows)


def project_kernel(core_ref, tok_ref, gain_ref, wq, wk, wv, q_all, swap, k_all, v_all, edge):
    step = pl.program_id(0)
    core = core_ref[0]
    x = tok_ref[...].astype(F32)
    inverse = lax.rsqrt(jnp.mean(x * x, axis=1, keepdims=True) + 1e-05)
    normed = (x * inverse * gain_ref[...]).astype(BF16)
    q = nn(normed, wq[...]).astype(BF16)
    k = nn(normed, wk[...]).astype(BF16)
    v = nn(normed, wv[...])

    def put(here):
        to_first = swap if here else edge
        to_last = edge if here else swap
        for h in range(4):
            slot = (h - 2 * here) % 4
            lanes = slice(h * HD, (h + 1) * HD)
            q_all[slot] = q[:, lanes]
            if slot >= 2:
                swap[pl.ds((slot - 2) * 1024 + pl.multiple_of(step * 256, 256), 256), :] = q[:, lanes]
            for b in range(2):
                rows = slice(b * BLOCK, (b + 1) * BLOCK)
                kb = k[rows, lanes]
                vb = v[rows, lanes].T.astype(BF16)
                k_all[slot, b] = kb
                v_all[slot, b] = vb
                out, when = (to_first, 0) if b == 0 else (to_last, pl.num_programs(0) - 1)
                base = 2048 if out is swap else 0

                @pl.when(step == when)
                def _():
                    out[base + slot * HD : base + (slot + 1) * HD, :] = kb
                    out[base + (4 + slot) * HD : base + (5 + slot) * HD, :] = vb

    @pl.when(core == 0)
    def _():
        put(0)

    @pl.when(core == 1)
    def _():
        put(1)


def project(core, tokens, gain, wq, wk, wv):
    n, d = tokens.shape
    w = wq.shape[1]
    weight = pl.BlockSpec((d, w), lambda i, c: (0, 0), pipeline_mode=pl.Buffered(1))
    blocks = pl.BlockSpec((4, 2, BLOCK, HD), lambda i, c: (0, i, 0, 0))
    return pl.pallas_call(
        project_kernel,
        grid_spec=pltpu.PrefetchScalarGridSpec(
            num_scalar_prefetch=1,
            grid=(n // 256,),
            in_specs=[
                pl.BlockSpec((256, d), lambda i, c: (i, 0)),
                pl.BlockSpec((1, d), lambda i, c: (0, 0)),
                weight,
                weight,
                weight,
            ],
            out_specs=[
                pl.BlockSpec((4, 256, HD), lambda i, c: (0, i, 0)),
                pl.BlockSpec((3072, HD), lambda i, c: (0, 0)),
                blocks,
                blocks,
                pl.BlockSpec((1024, HD), lambda i, c: (0, 0)),
            ],
        ),
        out_shape=[
            jax.ShapeDtypeStruct((4, n, HD), BF16),
            jax.ShapeDtypeStruct((3072, HD), BF16),
            jax.ShapeDtypeStruct((4, 8, BLOCK, HD), BF16),
            jax.ShapeDtypeStruct((4, 8, HD, BLOCK), BF16),
            jax.ShapeDtypeStruct((1024, HD), BF16),
        ],
        compiler_params=params(),
        cost_estimate=BRIEF,
        name="project",
    )(core, tokens, gain.reshape(1, d), wq, wk, wv)


def near_kernel(core_ref, q_ref, k_ref, v_ref, ka, va, kb, vb, o_ref, lse_ref):
    first = core_ref[0] == 0
    klo, khi = jnp.where(first, ka[0], kb[0]), jnp.where(first, kb[0], ka[0])
    vlo, vhi = jnp.where(first, va[0], vb[0]), jnp.where(first, vb[0], va[0])
    for b in range(8):
        q = q_ref[0, b * BLOCK : (b + 1) * BLOCK]
        ks = [klo if b == 0 else k_ref[0, b - 1], k_ref[0, b], khi if b == 7 else k_ref[0, b + 1]]
        vs = [vlo if b == 0 else v_ref[0, b - 1], v_ref[0, b], vhi if b == 7 else v_ref[0, b + 1]]
        s = [nt(k, q) * SCALE for k in ks]
        m = jnp.max(jnp.maximum(jnp.maximum(s[0], s[1]), s[2]), axis=0, keepdims=True)
        p = [jnp.exp(x - m) for x in s]
        total = jnp.sum(p[0] + p[1] + p[2], axis=0, keepdims=True)
        acc = nn(vs[0], p[0].astype(BF16)) + nn(vs[1], p[1].astype(BF16)) + nn(vs[2], p[2].astype(BF16))
        o_ref[0, b] = acc / total
        lse_ref[0, b : b + 1, :] = m + jnp.log(total)


def near(core, q, k, v, halo, swapped):
    blocks = pl.BlockSpec((1, 8, BLOCK, HD), lambda s, c: (s, 0, 0, 0))

    def edge(first):
        return pl.BlockSpec((1, BLOCK, HD), lambda s, c: (first + (s + 2) % 4, 0, 0))

    return pl.pallas_call(
        near_kernel,
        grid_spec=pltpu.PrefetchScalarGridSpec(
            num_scalar_prefetch=1,
            grid=(4,),
            in_specs=[pl.BlockSpec((1, 1024, HD), lambda s, c: (s, 0, 0)), blocks, blocks]
            + [edge(0), edge(4), edge(16), edge(20)],
            out_specs=[blocks, pl.BlockSpec((1, 8, HD), lambda s, c: (s, 0, 0))],
        ),
        out_shape=[jax.ShapeDtypeStruct((4, 8, HD, BLOCK), F32), jax.ShapeDtypeStruct((4, 8, BLOCK), F32)],
        compiler_params=params(),
        cost_estimate=BRIEF,
        name="near",
    )(core, q, k, v, halo.reshape(8, BLOCK, HD), halo.reshape(8, BLOCK, HD), swapped.reshape(24, BLOCK, HD), swapped.reshape(24, BLOCK, HD))


GROUP = 4
UNITS = 96 + GROUP


def plan_kernel(cnt_ref, code_ref, list_ref, unit_ref, first_ref, long_ref, size_ref):
    def scan(i, carry):
        e, u, m = carry
        n = cnt_ref[i]
        first_ref[i] = u

        def named(carry):
            e, u, m = carry
            at = e
            for w in range(WMAX):
                code = code_ref[i * WMAX + w]
                list_ref[at] = code
                at = at + (code >= 0).astype(jnp.int32)

            def unit(k, u):
                both = (2 * k + 1 < n).astype(jnp.int32)
                unit_ref[u] = i * 512 + (e + 2 * k) * 2 + both
                return u + 1

            long_ref[m] = i
            return at, lax.fori_loop(0, lax.shift_right_logical(n + 1, 1), unit, u), m + (n > 2).astype(jnp.int32)

        return lax.cond(n > 0, named, lambda carry: carry, (e, u, m))

    entries, units, longs = lax.fori_loop(0, 64, scan, (jnp.int32(0), jnp.int32(0), jnp.int32(0)))
    for g in range(GROUP):
        unit_ref[units + g] = -1
    size_ref[0] = entries
    size_ref[1] = units
    size_ref[2] = longs


def plan(cnt, code):
    def out(n):
        return jax.ShapeDtypeStruct((n,), jnp.int32)

    return pl.pallas_call(
        plan_kernel,
        in_specs=[SMEM] * 2,
        out_specs=[SMEM] * 5,
        out_shape=[out(128 + WMAX), out(UNITS), out(64), out(64), out(3)],
        compiler_params=params(16),
        cost_estimate=BRIEF,
        name="plan",
    )(cnt, code)


def far_kernel(j, cnt_ref, list_ref, unit_ref, first_ref, long_ref, size_ref, *rest):
    sources, qs, outs = rest[:8], rest[8:12], rest[12:16]
    kvbuf, qbuf, obuf, acc_ref, stat_ref, logs, kvsem, qsem, osem = rest[16:]
    entries, units = size_ref[0], size_ref[1]
    for r in range(4):
        pltpu.make_async_copy(qs[r].at[:, j], qbuf.at[pl.ds(2 * r, 2)], qsem.at[r]).start()

    def fetch(e, _):
        code = list_ref[e]
        at = lax.bitwise_and(code, 15)
        source = lax.shift_right_logical(code, 4)

        def start(lo, hi):
            if hi - lo == 1:
                pltpu.make_async_copy(sources[lo].at[at], kvbuf.at[e], kvsem.at[e]).start()
                return
            mid = (lo + hi) // 2

            @pl.when(source < mid)
            def _():
                start(lo, mid)

            @pl.when(source >= mid)
            def _():
                start(mid, hi)

        start(0, 8)
        return 0

    lax.fori_loop(0, entries, fetch, 0)
    logs[...] = jnp.full((64, BLOCK), NEG, F32)
    for r in range(4):
        pltpu.make_async_copy(qs[r].at[:, j], qbuf.at[pl.ds(2 * r, 2)], qsem.at[r]).wait()

    def landed(e, _):
        pltpu.make_async_copy(sources[0].at[0], kvbuf.at[e], kvsem.at[e]).wait()
        return 0

    lax.fori_loop(0, entries, landed, 0)

    def store(i, m, total, acc):
        rows = pl.ds(pl.multiple_of(lax.bitwise_and(i, 15) * HD, HD), HD)
        obuf[lax.shift_right_logical(i, 4), rows, :] = (acc * (1.0 / total)).astype(BF16)
        logs[pl.ds(i, 1), :] = m + jnp.log(total)

    def group(g, _):
        done = []
        for t in range(GROUP):
            u = g * GROUP + t
            unit = unit_ref[u]
            unit = jnp.where(unit >= 0, unit, unit_ref[g * GROUP])
            both = lax.bitwise_and(unit, 1)
            ea = lax.bitwise_and(lax.shift_right_logical(unit, 1), 255)
            eb = ea + both
            i = lax.shift_right_logical(unit, 9)
            q = qbuf[lax.shift_right_logical(i, 3), lax.bitwise_and(i, 7)]
            sa = nt(kvbuf[ea, 0], q) * SCALE
            sb = jnp.where(both == 1, nt(kvbuf[eb, 0], q) * SCALE, NEG)
            m = jnp.max(jnp.maximum(sa, sb), axis=0, keepdims=True)
            pa, pb = jnp.exp(sa - m), jnp.exp(sb - m)
            total = jnp.sum(pa + pb, axis=0, keepdims=True)
            acc = nn(kvbuf[ea, 1], pa.astype(BF16)) + nn(kvbuf[eb, 1], pb.astype(BF16))
            done.append((u, i, m, total, acc))
        for u, i, m, total, acc in done:
            stat_ref[u, 0:1, :] = m
            stat_ref[u, 1:2, :] = total
            acc_ref[u] = acc
            store(i, m, total, acc)
        return 0

    lax.fori_loop(0, lax.div(units + GROUP - 1, GROUP), group, 0)

    def join(k, _):
        i = long_ref[k]
        n = cnt_ref[i]
        u = first_ref[i]

        def more(k, carry):
            m, total, acc = carry
            mk, tk = stat_ref[k, 0:1, :], stat_ref[k, 1:2, :]
            top = jnp.maximum(m, mk)
            old, new = jnp.exp(m - top), jnp.exp(mk - top)
            return top, total * old + tk * new, acc * old + acc_ref[k] * new

        start = (stat_ref[u, 0:1, :], stat_ref[u, 1:2, :], acc_ref[u])
        store(i, *lax.fori_loop(u + 1, u + lax.shift_right_logical(n + 1, 1), more, start))
        return 0

    lax.fori_loop(0, size_ref[2], join, 0)
    for r in range(4):
        part = logs[r * 16 : (r + 1) * 16, :]
        for t in range(3):
            term = part.astype(BF16)
            obuf[r, 2048 + t * 16 : 2064 + t * 16, :] = term
            part = part - term.astype(F32)
        pltpu.make_async_copy(obuf.at[r], outs[r], osem.at[r]).start()
    for r in range(4):
        pltpu.make_async_copy(obuf.at[r], outs[r], osem.at[r]).wait()


def far(j, cnt, lists, sources, qs):
    out = jax.ShapeDtypeStruct((OROWS, BLOCK), BF16)
    return pl.pallas_call(
        functools.partial(far_kernel, j),
        in_specs=[SMEM] * 6 + [ANY] * 12,
        out_specs=[ANY] * 4,
        out_shape=[out] * 4,
        scratch_shapes=[
            pltpu.VMEM((128, 2, BLOCK, HD), BF16),
            pltpu.VMEM((8, 8, BLOCK, HD), BF16),
            pltpu.VMEM((4, OROWS, BLOCK), BF16),
            pltpu.VMEM((UNITS, HD, BLOCK), F32),
            pltpu.VMEM((UNITS, 8, BLOCK), F32),
            pltpu.VMEM((64, BLOCK), F32),
            pltpu.SemaphoreType.DMA((128,)),
            pltpu.SemaphoreType.DMA((4,)),
            pltpu.SemaphoreType.DMA((4,)),
        ],
        compiler_params=params(),
        cost_estimate=BRIEF,
        name="far",
    )(cnt, *lists, *sources, *qs)


def merge_kernel(a, b, c, d, keep, send):
    parts = (a, b, c, d)
    logs = [sum(p[2048 + t * 16 : 2064 + t * 16, :].astype(F32) for t in range(3)) for p in parts]
    peak = functools.reduce(jnp.maximum, logs)
    shares = [jnp.where(x > 0.5 * NEG, jnp.exp(x - peak), 0.0) for x in logs]
    total = sum(shares)
    joint = jnp.where(total > 0.0, peak + jnp.log(total), NEG)
    total = jnp.where(total > 0.0, total, 1.0)
    live = [x > 0.5 * NEG for x in logs]
    shares = [x / total for x in shares]
    for s, out in enumerate((keep, send)):
        for i in range(8):
            row = s * 8 + i
            rows = slice(row * HD, (row + 1) * HD)
            out[i * HD : (i + 1) * HD, :] = sum(
                jnp.where(on[row : row + 1, :], x[row : row + 1, :] * p[rows, :].astype(F32), 0.0)
                for on, x, p in zip(live, shares, parts)
            )
        out[1024:1032, :] = joint[s * 8 : (s + 1) * 8, :]


def merge(parts):
    out = jax.ShapeDtypeStruct((FROWS, BLOCK), F32)
    return pl.pallas_call(
        merge_kernel,
        out_shape=[out, out],
        compiler_params=params(),
        cost_estimate=BRIEF,
        name="merge",
    )(*parts)


def finish_kernel(near_a, lse_a, near_b, lse_b, far_a, far_b, out):
    for s, (o, log, f) in enumerate(((near_a, lse_a, far_a), (near_b, lse_b, far_b))):
        here, away = log[0], f[1024:1032, :]
        peak = jnp.maximum(here, away)
        wn, wf = jnp.exp(here - peak), jnp.exp(away - peak)
        total = wn + wf
        wn, wf = wn / total, wf / total
        for b in range(8):
            both = wn[b : b + 1, :] * o[0, b] + wf[b : b + 1, :] * f[b * HD : (b + 1) * HD, :]
            out[s, b * BLOCK : (b + 1) * BLOCK, :] = both.T.astype(BF16)


def finish(j, o, lse, far_keep, far_other):
    def at(slot):
        return [
            pl.BlockSpec((1, 8, HD, BLOCK), lambda i: (slot, 0, 0, 0)),
            pl.BlockSpec((1, 8, BLOCK), lambda i: (slot, 0, 0)),
        ]

    whole = pl.BlockSpec((FROWS, BLOCK), lambda i: (0, 0))
    return pl.pallas_call(
        finish_kernel,
        grid=(1,),
        in_specs=at(j) + at(2 + j) + [whole, whole],
        out_specs=pl.BlockSpec((2, 1024, HD), lambda i: (0, 0, 0)),
        out_shape=jax.ShapeDtypeStruct((2, 1024, HD), BF16),
        compiler_params=params(),
        cost_estimate=BRIEF,
        name="finish",
    )(o, lse, o, lse, far_keep, far_other)


def mix_kernel(last, place_ref, a0, a1, a2, a3, *rest):
    weights, carried, out = rest[:8], rest[8], rest[-1]
    total = carried[...].astype(F32) if carried is not out else None
    left = jnp.concatenate([a[s] for a in (a0, a1, a2, a3) for s in range(2)], axis=1)
    term = nn(left, jnp.concatenate([w[...] for w in weights], axis=0))
    total = term if total is None else total + term
    if last:
        total = total + rest[9][...]
    out[...] = total.astype(out.dtype)


def mix(j, place, parts, w_out, carried, acc=None):
    n, cols = 1024, 512

    def weight(rel, s):
        def at(i, p):
            head = (2 * p[0] + 2 * s + j) % 4
            return ((p[1] + rel) % NX * 4 + head, p[1])

        return pl.BlockSpec((HD, cols), at)

    last = acc is not None
    in_specs = [pl.BlockSpec((2, 256, HD), lambda i, p: (0, i, 0))] * 4
    in_specs += [weight(rel, s) for rel in range(4) for s in range(2)]
    args = list(parts) + [w_out] * 8
    if last:
        in_specs.append(pl.BlockSpec((256, cols), lambda i, p: (i, p[1])))
        in_specs.append(pl.BlockSpec((256, cols), lambda i, p: (i, 0)))
        args += [carried, acc]
    return pl.pallas_call(
        functools.partial(mix_kernel, last),
        grid_spec=pltpu.PrefetchScalarGridSpec(
            num_scalar_prefetch=1,
            grid=(n // 256,),
            in_specs=in_specs,
            out_specs=pl.BlockSpec((256, cols), lambda i, p: (i, 0)),
        ),
        out_shape=jax.ShapeDtypeStruct((n, cols), BF16 if last else F32),
        compiler_params=params(),
        cost_estimate=BRIEF,
        name="mix",
    )(place, *args)


def line_codes(wake_blocks, wake_frames, wake_counts, y, z, c):
    live = jnp.arange(WMAX, dtype=jnp.int32)[None, :] < wake_counts[:, None]
    word = jnp.where(live, wake_frames * 256 + wake_blocks, -1).reshape(NY, NZ, NC, 8, WMAX)
    by_y = lax.dynamic_index_in_dim(word, y, 0, keepdims=False)
    by_z = lax.dynamic_index_in_dim(word, z, 1, keepdims=False)
    here = jnp.where(c == 0, by_y, by_z)
    here = lax.dynamic_slice_in_dim(jnp.concatenate([here, here], axis=0), jnp.where(c == 0, z, y), 4, 0)
    here = lax.dynamic_slice_in_dim(jnp.concatenate([here, here], axis=1), c, 2, 1)
    word = here.reshape(64, WMAX)
    block, frame = word & 255, word >> 8
    hc, hz, hy = (block >> 3) & 1, (block >> 4) & 3, (block >> 6) & 3
    in_line = (word >= 0) & (jnp.where(c == 0, hz, hy) == jnp.where(c == 0, z, y))
    piece = (jnp.where(c == 0, hy, hz) - jnp.where(c == 0, y, z)) & 3
    code = piece * 32 + (hc ^ c) * 16 + (frame & 1) * 8 + (block & 7)
    code = jnp.where(in_line, code, -1)
    return code.reshape(512), jnp.sum(in_line.astype(jnp.int32), axis=1)


def on_device(tokens, norm_gain, w_query, w_key, w_value, w_out, kv_cache, wake_blocks, wake_frames, wake_counts):
    tok = lax.axis_index("tok").astype(jnp.int32)
    mp = lax.axis_index("mp").astype(jnp.int32)
    c, z, y = tok % NC, (tok // NC) % NZ, tok // (NC * NZ)
    core = c.reshape(1)
    place = jnp.stack([c, mp])

    def after(x, *deps):
        return lax.optimization_barrier((x, *deps))[0]

    keep0, send0 = split_cache(0, core, kv_cache)
    up_k0, down_k0 = rows_perm(keep0, 1), rows_perm(keep0, -1)
    got0 = core_swap(send0)
    up_r0, down_r0 = rows_perm(got0, 1), rows_perm(got0, -1)

    gain = after(norm_gain, got0)
    q_all, swap, k_all, v_all, edge = project(core, tokens, gain, w_query, w_key, w_value)
    swapped, halo = core_swap(swap), halo_perm(edge)
    up20 = rows_perm(after(up_k0, edge), 1)
    mine = jnp.concatenate([q_all[:2], swapped[:2048].reshape(2, 1024, HD)], axis=0).reshape(2, 2, 8, BLOCK, HD)
    mine, halo, down_k0, up_r0, down_r0 = lax.optimization_barrier((mine, halo, down_k0, up_r0, down_r0))
    down20 = rows_perm(down_r0, -1)
    q1, q3, q2 = query_perm(mine, -1), query_perm(mine, 1), query_perm(mine, 2)

    keep1, send1 = split_cache(1, after(core, mine), kv_cache)
    near_o, near_lse = near(core, q_all, k_all, v_all, after(halo, keep1), swapped)
    code, cnt = line_codes(wake_blocks, wake_frames, wake_counts, y, z, c)
    lists = plan(cnt, code)
    keep1, near_o, near_lse, q1, q3, *lists = lax.optimization_barrier((keep1, near_o, near_lse, q1, q3, *lists))
    up_k1, down_k1 = rows_perm(keep1, 1), rows_perm(keep1, -1)
    send1, up20, down20, q2 = lax.optimization_barrier((send1, up20, down20, q2, near_o))[:4]
    got1 = core_swap(send1)
    qs = [after(mine, got1), q1, q2, q3]
    up_r1, down_r1 = rows_perm(got1, 1), rows_perm(got1, -1)

    def returned(parts):
        return [parts[0], query_perm(parts[1], 1), query_perm(parts[2], 2), query_perm(parts[3], -1)]

    def gather(heads):
        return [heads, mp_perm(heads, -1), mp_perm(heads, 2), mp_perm(heads, 1)]

    sources = [keep0, got0, down_k0, down_r0, up20, down20, up_k0, up_r0]
    parts = far(0, cnt, lists, sources, qs)
    *parts, up_k1, down_k1 = lax.optimization_barrier((*parts, up_k1, down_k1))
    back = returned(parts)
    up21 = rows_perm(up_k1, 1)
    down21 = rows_perm(down_r1, -1)
    back[0], up_r1, up21, down21 = lax.optimization_barrier((back[0], up_r1, up21, down21))
    own, other = merge(back)
    heads = finish(0, near_o, near_lse, own, core_swap(other))
    gathered = gather(heads)

    sources = [after(keep1, heads), got1, down_k1, down_r1, up21, down21, up_k1, up_r1]
    parts = far(1, cnt, lists, sources, qs)
    *parts, gathered[1], gathered[3] = lax.optimization_barrier((*parts, gathered[1], gathered[3]))
    back = returned(parts)
    gathered[0] = after(gathered[0], parts[0])
    acc = mix(0, place, gathered, w_out, tokens, None)
    back[0], acc = lax.optimization_barrier((back[0], acc))
    own, other = merge(back)
    heads = finish(1, near_o, near_lse, own, core_swap(other))
    return mix(1, place, gather(heads), w_out, tokens, acc)


def solution(mesh):
    return jax.shard_map(
        on_device,
        mesh=mesh,
        in_specs=(
            P("tok", None),
            P(),
            P(None, "mp"),
            P(None, "mp"),
            P(None, "mp"),
            P(),
            P(None, "tok", None, "mp"),
            P(),
            P(),
            P(),
        ),
        out_specs=P("tok", "mp"),
        check_vma=False,
    )
```

```python
import functools
import math

import jax
import jax.numpy as jnp
from jax import lax
from jax.experimental import pallas as pl
from jax.experimental.pallas import tpu as pltpu
from jax.sharding import PartitionSpec as P

HD = 128
BLOCK = 128
WMAX = 8
NEG = -1e30
SCALE = 1.0 / math.sqrt(HD)
NY, NZ, NC, NX = 4, 4, 2, 4
F32, BF16 = jnp.float32, jnp.bfloat16
ANY = pl.BlockSpec(memory_space=pl.ANY)
SMEM = pl.BlockSpec(memory_space=pltpu.SMEM)
BRIEF = pl.CostEstimate(flops=1, transcendentals=0, bytes_accessed=1)
OROWS = 2048 + 48
FROWS = 1024 + 8


def params(mib=48):
    return pltpu.CompilerParams(vmem_limit_bytes=mib << 20)


def tok_of(y, z, c):
    return ((y % NY) * NZ + z % NZ) * NC + c % NC


def chips():
    return [(y, z, c) for y in range(NY) for z in range(NZ) for c in range(NC)]


def rows_perm(x, d):
    pairs = [(tok_of(y, z, c), tok_of(y + d, z, c) if c == 0 else tok_of(y, z + d, c)) for y, z, c in chips()]
    return lax.ppermute(x, "tok", pairs)


def query_perm(x, d):
    pairs = [(tok_of(y, z, c), tok_of(y, z + d, c) if c == 0 else tok_of(y + d, z, c)) for y, z, c in chips()]
    return lax.ppermute(x, "tok", pairs)


def core_swap(x):
    return lax.ppermute(x, "tok", [(tok_of(y, z, c), tok_of(y, z, 1 - c)) for y, z, c in chips()])


def halo_perm(x):
    n = NY * NZ * NC
    return lax.ppermute(x, "tok", [(i, (i + (1 if i % 2 else -1)) % n) for i in range(n)])


def mp_perm(x, d):
    return lax.ppermute(x, "mp", [(i, (i + d) % NX) for i in range(NX)])


def nt(a, b):
    return lax.dot_general(a, b, (((1,), (1,)), ((), ())), preferred_element_type=F32)


def nn(a, b):
    return lax.dot_general(a, b, (((1,), (0,)), ((), ())), preferred_element_type=F32)


def split_cache_kernel(core_ref, keep_ref, send_ref, keep, send):
    for src, out in ((keep_ref, keep), (send_ref, send)):
        for b in range(2):
            rows = slice(b * BLOCK, (b + 1) * BLOCK)
            out[b, 0] = src[0, rows, 0, :]
            out[b, 1] = src[0, rows, 1, :].T


def split_cache(j, core, rows):
    out = jax.ShapeDtypeStruct((16, 2, BLOCK, HD), BF16)
    block = pl.BlockSpec((2, 2, BLOCK, HD), lambda i, c: (i, 0, 0, 0))
    return pl.pallas_call(
        split_cache_kernel,
        grid_spec=pltpu.PrefetchScalarGridSpec(
            num_scalar_prefetch=1,
            grid=(8,),
            in_specs=[
                pl.BlockSpec((1, 256, 2, HD), lambda i, c: (i // 4, i % 4, 0, 2 * c[0] + j)),
                pl.BlockSpec((1, 256, 2, HD), lambda i, c: (i // 4, i % 4, 0, 2 - 2 * c[0] + j)),
            ],
            out_specs=[block, block],
        ),
        out_shape=[out, out],
        compiler_params=params(),
        cost_estimate=BRIEF,
        name="split_cache",
    )(core, rows, rows)


def project_kernel(core_ref, tok_ref, gain_ref, wq, wk, wv, q_all, swap, k_all, v_all, edge):
    step = pl.program_id(0)
    core = core_ref[0]
    x = tok_ref[...].astype(F32)
    inverse = lax.rsqrt(jnp.mean(x * x, axis=1, keepdims=True) + 1e-05)
    normed = (x * inverse * gain_ref[...]).astype(BF16)
    q = nn(normed, wq[...]).astype(BF16)
    k = nn(normed, wk[...]).astype(BF16)
    v = nn(normed, wv[...])

    def put(here):
        to_first = swap if here else edge
        to_last = edge if here else swap
        for h in range(4):
            slot = (h - 2 * here) % 4
            lanes = slice(h * HD, (h + 1) * HD)
            q_all[slot] = q[:, lanes]
            if slot >= 2:
                swap[pl.ds((slot - 2) * 1024 + pl.multiple_of(step * 256, 256), 256), :] = q[:, lanes]
            for b in range(2):
                rows = slice(b * BLOCK, (b + 1) * BLOCK)
                kb = k[rows, lanes]
                vb = v[rows, lanes].T.astype(BF16)
                k_all[slot, b] = kb
                v_all[slot, b] = vb
                out, when = (to_first, 0) if b == 0 else (to_last, pl.num_programs(0) - 1)
                base = 2048 if out is swap else 0

                @pl.when(step == when)
                def _():
                    out[base + slot * HD : base + (slot + 1) * HD, :] = kb
                    out[base + (4 + slot) * HD : base + (5 + slot) * HD, :] = vb

    @pl.when(core == 0)
    def _():
        put(0)

    @pl.when(core == 1)
    def _():
        put(1)


def project(core, tokens, gain, wq, wk, wv):
    n, d = tokens.shape
    w = wq.shape[1]
    weight = pl.BlockSpec((d, w), lambda i, c: (0, 0), pipeline_mode=pl.Buffered(1))
    blocks = pl.BlockSpec((4, 2, BLOCK, HD), lambda i, c: (0, i, 0, 0))
    return pl.pallas_call(
        project_kernel,
        grid_spec=pltpu.PrefetchScalarGridSpec(
            num_scalar_prefetch=1,
            grid=(n // 256,),
            in_specs=[
                pl.BlockSpec((256, d), lambda i, c: (i, 0)),
                pl.BlockSpec((1, d), lambda i, c: (0, 0)),
                weight,
                weight,
                weight,
            ],
            out_specs=[
                pl.BlockSpec((4, 256, HD), lambda i, c: (0, i, 0)),
                pl.BlockSpec((3072, HD), lambda i, c: (0, 0)),
                blocks,
                blocks,
                pl.BlockSpec((1024, HD), lambda i, c: (0, 0)),
            ],
        ),
        out_shape=[
            jax.ShapeDtypeStruct((4, n, HD), BF16),
            jax.ShapeDtypeStruct((3072, HD), BF16),
            jax.ShapeDtypeStruct((4, 8, BLOCK, HD), BF16),
            jax.ShapeDtypeStruct((4, 8, HD, BLOCK), BF16),
            jax.ShapeDtypeStruct((1024, HD), BF16),
        ],
        compiler_params=params(),
        cost_estimate=pl.CostEstimate(flops=2 * n * d * 3 * w, transcendentals=0, bytes_accessed=16 << 20),
        name="project",
    )(core, tokens, gain.reshape(1, d), wq, wk, wv)


def near_kernel(core_ref, q_ref, k_ref, v_ref, ka, va, kb, vb, o_ref, lse_ref):
    first = core_ref[0] == 0
    klo, khi = jnp.where(first, ka[0], kb[0]), jnp.where(first, kb[0], ka[0])
    vlo, vhi = jnp.where(first, va[0], vb[0]), jnp.where(first, vb[0], va[0])
    for b in range(8):
        q = q_ref[0, b * BLOCK : (b + 1) * BLOCK]
        ks = [klo if b == 0 else k_ref[0, b - 1], k_ref[0, b], khi if b == 7 else k_ref[0, b + 1]]
        vs = [vlo if b == 0 else v_ref[0, b - 1], v_ref[0, b], vhi if b == 7 else v_ref[0, b + 1]]
        s = [nt(k, q) * SCALE for k in ks]
        m = jnp.max(jnp.maximum(jnp.maximum(s[0], s[1]), s[2]), axis=0, keepdims=True)
        p = [jnp.exp(x - m) for x in s]
        total = jnp.sum(p[0] + p[1] + p[2], axis=0, keepdims=True)
        acc = nn(vs[0], p[0].astype(BF16)) + nn(vs[1], p[1].astype(BF16)) + nn(vs[2], p[2].astype(BF16))
        o_ref[0, b] = acc / total
        lse_ref[0, b : b + 1, :] = m + jnp.log(total)


def near(core, q, k, v, halo, swapped):
    blocks = pl.BlockSpec((1, 8, BLOCK, HD), lambda s, c: (s, 0, 0, 0))

    def edge(first):
        return pl.BlockSpec((1, BLOCK, HD), lambda s, c: (first + (s + 2) % 4, 0, 0))

    return pl.pallas_call(
        near_kernel,
        grid_spec=pltpu.PrefetchScalarGridSpec(
            num_scalar_prefetch=1,
            grid=(4,),
            in_specs=[pl.BlockSpec((1, 1024, HD), lambda s, c: (s, 0, 0)), blocks, blocks]
            + [edge(0), edge(4), edge(16), edge(20)],
            out_specs=[blocks, pl.BlockSpec((1, 8, HD), lambda s, c: (s, 0, 0))],
        ),
        out_shape=[jax.ShapeDtypeStruct((4, 8, HD, BLOCK), F32), jax.ShapeDtypeStruct((4, 8, BLOCK), F32)],
        compiler_params=params(),
        cost_estimate=BRIEF,
        name="near",
    )(core, q, k, v, halo.reshape(8, BLOCK, HD), halo.reshape(8, BLOCK, HD), swapped.reshape(24, BLOCK, HD), swapped.reshape(24, BLOCK, HD))


GROUP = 4
UNITS = 96 + GROUP


def plan_kernel(cnt_ref, code_ref, unit_ref, first_ref, long_ref, size_ref, list_ref):
    def scan(i, carry):
        u, m = carry
        n = cnt_ref[i]
        first_ref[i] = u

        def named(carry):
            u, m = carry
            at = jnp.int32(0)
            for w in range(WMAX):
                code = code_ref[i * WMAX + w]
                list_ref[at] = code
                at = at + (code >= 0).astype(jnp.int32)

            def unit(k, u):
                both = (2 * k + 1 < n).astype(jnp.int32)
                unit_ref[u] = both * (1 << 22) + i * (1 << 16) + list_ref[2 * k] * 256 + list_ref[2 * k + both]
                return u + 1

            long_ref[m] = i
            return lax.fori_loop(0, lax.shift_right_logical(n + 1, 1), unit, u), m + (n > 2).astype(jnp.int32)

        return lax.cond(n > 0, named, lambda carry: carry, (u, m))

    units, longs = lax.fori_loop(0, 64, scan, (jnp.int32(0), jnp.int32(0)))
    for g in range(GROUP):
        unit_ref[units + g] = -1
    size_ref[0] = units
    size_ref[1] = longs


def plan(cnt, code):
    def out(n):
        return jax.ShapeDtypeStruct((n,), jnp.int32)

    return pl.pallas_call(
        plan_kernel,
        in_specs=[SMEM] * 2,
        out_specs=[SMEM] * 4,
        out_shape=[out(UNITS), out(64), out(64), out(2)],
        scratch_shapes=[pltpu.SMEM((2 * WMAX,), jnp.int32)],
        compiler_params=params(16),
        cost_estimate=BRIEF,
        name="plan",
    )(cnt, code)


def far_kernel(j, cnt_ref, unit_ref, first_ref, long_ref, size_ref, *rest):
    sources, qs, outs = rest[:8], rest[8:12], rest[12:16]
    kvbuf, qbuf, obuf, acc_ref, stat_ref, logs, kvsem, qsem, osem = rest[16:]
    units = size_ref[0]
    copies = [pltpu.make_async_copy(qs[r].at[:, j], qbuf.at[pl.ds(2 * r, 2)], qsem.at[r]) for r in range(4)]
    copies += [pltpu.make_async_copy(sources[k], kvbuf.at[pl.ds(16 * k, 16)], kvsem.at[k]) for k in range(8)]
    for copy in copies:
        copy.start()
    logs[...] = jnp.full((64, BLOCK), NEG, F32)
    for copy in copies:
        copy.wait()

    def store(i, m, total, acc):
        rows = pl.ds(pl.multiple_of(lax.bitwise_and(i, 15) * HD, HD), HD)
        obuf[lax.shift_right_logical(i, 4), rows, :] = (acc * (1.0 / total)).astype(BF16)
        logs[pl.ds(i, 1), :] = m + jnp.log(total)

    def group(g, _):
        for t in range(GROUP):
            u = g * GROUP + t
            unit = unit_ref[u]
            unit = jnp.where(unit >= 0, unit, unit_ref[g * GROUP])
            both = lax.shift_right_logical(unit, 22) == 1
            i = lax.bitwise_and(lax.shift_right_logical(unit, 16), 63)
            ea = lax.bitwise_and(lax.shift_right_logical(unit, 8), 127)
            eb = lax.bitwise_and(unit, 127)
            q = qbuf[lax.shift_right_logical(i, 3), lax.bitwise_and(i, 7)]
            s = nt(jnp.concatenate([kvbuf[ea, 0], kvbuf[eb, 0]], axis=0), q) * SCALE
            sa, sb = s[:BLOCK], jnp.where(both, s[BLOCK:], NEG)
            m = jnp.max(jnp.maximum(sa, sb), axis=0, keepdims=True)
            pa, pb = jnp.exp(sa - m), jnp.exp(sb - m)
            total = jnp.sum(pa + pb, axis=0, keepdims=True)
            p = jnp.concatenate([pa, pb], axis=0).astype(BF16)
            acc = nn(jnp.concatenate([kvbuf[ea, 1], kvbuf[eb, 1]], axis=1), p)
            stat_ref[u, 0:1, :] = m
            stat_ref[u, 1:2, :] = total
            acc_ref[u] = acc
            store(i, m, total, acc)
        return 0

    lax.fori_loop(0, lax.div(units + GROUP - 1, GROUP), group, 0)

    def join(k, _):
        i = long_ref[k]
        n = cnt_ref[i]
        u = first_ref[i]

        def more(k, carry):
            m, total, acc = carry
            mk, tk = stat_ref[k, 0:1, :], stat_ref[k, 1:2, :]
            top = jnp.maximum(m, mk)
            old, new = jnp.exp(m - top), jnp.exp(mk - top)
            return top, total * old + tk * new, acc * old + acc_ref[k] * new

        start = (stat_ref[u, 0:1, :], stat_ref[u, 1:2, :], acc_ref[u])
        store(i, *lax.fori_loop(u + 1, u + lax.shift_right_logical(n + 1, 1), more, start))
        return 0

    lax.fori_loop(0, size_ref[1], join, 0)
    for r in range(4):
        part = logs[r * 16 : (r + 1) * 16, :]
        for t in range(3):
            term = part.astype(BF16)
            obuf[r, 2048 + t * 16 : 2064 + t * 16, :] = term
            part = part - term.astype(F32)
        pltpu.make_async_copy(obuf.at[r], outs[r], osem.at[r]).start()
    for r in range(4):
        pltpu.make_async_copy(obuf.at[r], outs[r], osem.at[r]).wait()


def far(j, cnt, lists, sources, qs):
    out = jax.ShapeDtypeStruct((OROWS, BLOCK), BF16)
    return pl.pallas_call(
        functools.partial(far_kernel, j),
        in_specs=[SMEM] * 5 + [ANY] * 12,
        out_specs=[ANY] * 4,
        out_shape=[out] * 4,
        scratch_shapes=[
            pltpu.VMEM((128, 2, BLOCK, HD), BF16),
            pltpu.VMEM((8, 8, BLOCK, HD), BF16),
            pltpu.VMEM((4, OROWS, BLOCK), BF16),
            pltpu.VMEM((UNITS, HD, BLOCK), F32),
            pltpu.VMEM((UNITS, 8, BLOCK), F32),
            pltpu.VMEM((64, BLOCK), F32),
            pltpu.SemaphoreType.DMA((8,)),
            pltpu.SemaphoreType.DMA((4,)),
            pltpu.SemaphoreType.DMA((4,)),
        ],
        compiler_params=params(),
        cost_estimate=BRIEF,
        name="far",
    )(cnt, *lists, *sources, *qs)


def merge_kernel(a, b, c, d, keep, send):
    parts = (a, b, c, d)
    logs = [sum(p[2048 + t * 16 : 2064 + t * 16, :].astype(F32) for t in range(3)) for p in parts]
    peak = functools.reduce(jnp.maximum, logs)
    shares = [jnp.where(x > 0.5 * NEG, jnp.exp(x - peak), 0.0) for x in logs]
    total = sum(shares)
    joint = jnp.where(total > 0.0, peak + jnp.log(total), NEG)
    total = jnp.where(total > 0.0, total, 1.0)
    live = [x > 0.5 * NEG for x in logs]
    shares = [x / total for x in shares]
    for s, out in enumerate((keep, send)):
        for i in range(8):
            row = s * 8 + i
            rows = slice(row * HD, (row + 1) * HD)
            out[i * HD : (i + 1) * HD, :] = sum(
                jnp.where(on[row : row + 1, :], x[row : row + 1, :] * p[rows, :].astype(F32), 0.0)
                for on, x, p in zip(live, shares, parts)
            )
        out[1024:1032, :] = joint[s * 8 : (s + 1) * 8, :]


def merge(parts):
    out = jax.ShapeDtypeStruct((FROWS, BLOCK), F32)
    return pl.pallas_call(
        merge_kernel,
        out_shape=[out, out],
        compiler_params=params(),
        cost_estimate=BRIEF,
        name="merge",
    )(*parts)


def finish_kernel(near_a, lse_a, near_b, lse_b, far_a, far_b, out):
    for s, (o, log, f) in enumerate(((near_a, lse_a, far_a), (near_b, lse_b, far_b))):
        here, away = log[0], f[1024:1032, :]
        peak = jnp.maximum(here, away)
        wn, wf = jnp.exp(here - peak), jnp.exp(away - peak)
        total = wn + wf
        wn, wf = wn / total, wf / total
        for b in range(8):
            both = wn[b : b + 1, :] * o[0, b] + wf[b : b + 1, :] * f[b * HD : (b + 1) * HD, :]
            out[s, b * BLOCK : (b + 1) * BLOCK, :] = both.T.astype(BF16)


def finish(j, o, lse, far_keep, far_other):
    def at(slot):
        return [
            pl.BlockSpec((1, 8, HD, BLOCK), lambda i: (slot, 0, 0, 0)),
            pl.BlockSpec((1, 8, BLOCK), lambda i: (slot, 0, 0)),
        ]

    whole = pl.BlockSpec((FROWS, BLOCK), lambda i: (0, 0))
    return pl.pallas_call(
        finish_kernel,
        grid=(1,),
        in_specs=at(j) + at(2 + j) + [whole, whole],
        out_specs=pl.BlockSpec((2, 1024, HD), lambda i: (0, 0, 0)),
        out_shape=jax.ShapeDtypeStruct((2, 1024, HD), BF16),
        compiler_params=params(),
        cost_estimate=BRIEF,
        name="finish",
    )(o, lse, o, lse, far_keep, far_other)


def mix_kernel(last, place_ref, a0, a1, a2, a3, *rest):
    weights, carried, out = rest[:8], rest[8], rest[-1]
    total = carried[...].astype(F32) if carried is not out else None
    left = jnp.concatenate([a[s] for a in (a0, a1, a2, a3) for s in range(2)], axis=1)
    term = nn(left, jnp.concatenate([w[...] for w in weights], axis=0))
    total = term if total is None else total + term
    if last:
        total = total + rest[9][...]
    out[...] = total.astype(out.dtype)


def mix(j, place, parts, w_out, carried, acc=None):
    n, cols = 1024, 512

    def weight(rel, s):
        def at(i, p):
            head = (2 * p[0] + 2 * s + j) % 4
            return ((p[1] + rel) % NX * 4 + head, p[1])

        return pl.BlockSpec((HD, cols), at)

    last = acc is not None
    in_specs = [pl.BlockSpec((2, 256, HD), lambda i, p: (0, i, 0))] * 4
    in_specs += [weight(rel, s) for rel in range(4) for s in range(2)]
    args = list(parts) + [w_out] * 8
    if last:
        in_specs.append(pl.BlockSpec((256, cols), lambda i, p: (i, p[1])))
        in_specs.append(pl.BlockSpec((256, cols), lambda i, p: (i, 0)))
        args += [carried, acc]
    return pl.pallas_call(
        functools.partial(mix_kernel, last),
        grid_spec=pltpu.PrefetchScalarGridSpec(
            num_scalar_prefetch=1,
            grid=(n // 256,),
            in_specs=in_specs,
            out_specs=pl.BlockSpec((256, cols), lambda i, p: (i, 0)),
        ),
        out_shape=jax.ShapeDtypeStruct((n, cols), BF16 if last else F32),
        compiler_params=params(),
        cost_estimate=BRIEF,
        name="mix",
    )(place, *args)


def line_codes(wake_blocks, wake_frames, wake_counts, y, z, c):
    live = jnp.arange(WMAX, dtype=jnp.int32)[None, :] < wake_counts[:, None]
    word = jnp.where(live, wake_frames * 256 + wake_blocks, -1).reshape(NY, NZ, NC, 8, WMAX)
    by_y = lax.dynamic_index_in_dim(word, y, 0, keepdims=False)
    by_z = lax.dynamic_index_in_dim(word, z, 1, keepdims=False)
    here = jnp.where(c == 0, by_y, by_z)
    here = lax.dynamic_slice_in_dim(jnp.concatenate([here, here], axis=0), jnp.where(c == 0, z, y), 4, 0)
    here = lax.dynamic_slice_in_dim(jnp.concatenate([here, here], axis=1), c, 2, 1)
    word = here.reshape(64, WMAX)
    block, frame = word & 255, word >> 8
    hc, hz, hy = (block >> 3) & 1, (block >> 4) & 3, (block >> 6) & 3
    in_line = (word >= 0) & (jnp.where(c == 0, hz, hy) == jnp.where(c == 0, z, y))
    piece = (jnp.where(c == 0, hy, hz) - jnp.where(c == 0, y, z)) & 3
    code = piece * 32 + (hc ^ c) * 16 + (frame & 1) * 8 + (block & 7)
    code = jnp.where(in_line, code, -1)
    return code.reshape(512), jnp.sum(in_line.astype(jnp.int32), axis=1)


def on_device(tokens, norm_gain, w_query, w_key, w_value, w_out, kv_cache, wake_blocks, wake_frames, wake_counts):
    tok = lax.axis_index("tok").astype(jnp.int32)
    mp = lax.axis_index("mp").astype(jnp.int32)
    c, z, y = tok % NC, (tok // NC) % NZ, tok // (NC * NZ)
    core = c.reshape(1)
    place = jnp.stack([c, mp])

    def after(x, *deps):
        return lax.optimization_barrier((x, *deps))[0]

    keep0, send0 = split_cache(0, core, kv_cache)
    up_k0, down_k0 = rows_perm(keep0, 1), rows_perm(keep0, -1)
    got0 = core_swap(send0)
    up_r0, down_r0 = rows_perm(got0, 1), rows_perm(got0, -1)
    keep1, send1 = split_cache(1, after(core, got0), kv_cache)
    got1 = core_swap(send1)

    gain, up_k0, down_k0 = lax.optimization_barrier((norm_gain, up_k0, down_k0, got1))[:3]
    up20 = rows_perm(up_k0, 1)
    q_all, swap, k_all, v_all, edge = project(core, tokens, gain, w_query, w_key, w_value)
    swapped, halo = core_swap(swap), halo_perm(edge)
    mine = jnp.concatenate([q_all[:2], swapped[:2048].reshape(2, 1024, HD)], axis=0).reshape(2, 2, 8, BLOCK, HD)
    mine, halo, up_r0, down_r0 = lax.optimization_barrier((mine, halo, up_r0, down_r0))
    down20 = rows_perm(down_r0, -1)
    q1, q3, q2 = query_perm(mine, -1), query_perm(mine, 1), query_perm(mine, 2)

    near_o, near_lse = near(core, q_all, k_all, v_all, after(halo, mine), swapped)
    code, cnt = line_codes(wake_blocks, wake_frames, wake_counts, y, z, c)
    lists = plan(cnt, code)
    keep1, near_o, near_lse, q1, q3, *lists = lax.optimization_barrier((keep1, near_o, near_lse, q1, q3, *lists))
    up_k1, down_k1 = rows_perm(keep1, 1), rows_perm(keep1, -1)
    got1, up20, down20, q2 = lax.optimization_barrier((got1, up20, down20, q2, near_o))[:4]
    qs = [mine, q1, q2, q3]
    up_r1, down_r1 = rows_perm(got1, 1), rows_perm(got1, -1)

    def returned(parts):
        return [parts[0], query_perm(parts[1], 1), query_perm(parts[2], 2), query_perm(parts[3], -1)]

    def gather(heads):
        return [heads, mp_perm(heads, -1), mp_perm(heads, 2), mp_perm(heads, 1)]

    sources = [keep0, got0, down_k0, down_r0, up20, down20, up_k0, up_r0]
    parts = far(0, cnt, lists, sources, qs)
    *parts, up_k1, down_k1 = lax.optimization_barrier((*parts, up_k1, down_k1))
    back = returned(parts)
    up21 = rows_perm(up_k1, 1)
    down21 = rows_perm(down_r1, -1)
    back[0], up_r1, up21, down21 = lax.optimization_barrier((back[0], up_r1, up21, down21))
    own, other = merge(back)
    heads = finish(0, near_o, near_lse, own, core_swap(other))
    gathered = gather(heads)

    sources = [after(keep1, heads), got1, down_k1, down_r1, up21, down21, up_k1, up_r1]
    parts = far(1, cnt, lists, sources, qs)
    *parts, gathered[1], gathered[3] = lax.optimization_barrier((*parts, gathered[1], gathered[3]))
    back = returned(parts)
    gathered[0] = after(gathered[0], parts[0])
    acc = mix(0, place, gathered, w_out, tokens, None)
    back[0], acc = lax.optimization_barrier((back[0], acc))
    own, other = merge(back)
    heads = finish(1, near_o, near_lse, own, core_swap(other))
    return mix(1, place, gather(heads), w_out, tokens, acc)


def solution(mesh):
    return jax.shard_map(
        on_device,
        mesh=mesh,
        in_specs=(
            P("tok", None),
            P(),
            P(None, "mp"),
            P(None, "mp"),
            P(None, "mp"),
            P(),
            P(None, "tok", None, "mp"),
            P(),
            P(),
            P(),
        ),
        out_specs=P("tok", "mp"),
        check_vma=False,
    )
```

```python
import functools
import math

import jax
import jax.numpy as jnp
from jax import lax
from jax.experimental import pallas as pl
from jax.experimental.pallas import tpu as pltpu
from jax.sharding import PartitionSpec as P

HD = 128
BLOCK = 128
WMAX = 8
NEG = -1e30
SCALE = 1.0 / math.sqrt(HD)
NY, NZ, NC, NX = 4, 4, 2, 4
F32, BF16 = jnp.float32, jnp.bfloat16
ANY = pl.BlockSpec(memory_space=pl.ANY)
SMEM = pl.BlockSpec(memory_space=pltpu.SMEM)
BRIEF = pl.CostEstimate(flops=1, transcendentals=0, bytes_accessed=1)
OROWS = 2048 + 48
FROWS = 1024 + 8


def params(mib=48):
    return pltpu.CompilerParams(vmem_limit_bytes=mib << 20)


def tok_of(y, z, c):
    return ((y % NY) * NZ + z % NZ) * NC + c % NC


def chips():
    return [(y, z, c) for y in range(NY) for z in range(NZ) for c in range(NC)]


def rows_perm(x, d):
    pairs = [(tok_of(y, z, c), tok_of(y + d, z, c) if c == 0 else tok_of(y, z + d, c)) for y, z, c in chips()]
    return lax.ppermute(x, "tok", pairs)


def query_perm(x, d):
    pairs = [(tok_of(y, z, c), tok_of(y, z + d, c) if c == 0 else tok_of(y + d, z, c)) for y, z, c in chips()]
    return lax.ppermute(x, "tok", pairs)


def core_swap(x):
    return lax.ppermute(x, "tok", [(tok_of(y, z, c), tok_of(y, z, 1 - c)) for y, z, c in chips()])


def halo_perm(x):
    n = NY * NZ * NC
    return lax.ppermute(x, "tok", [(i, (i + (1 if i % 2 else -1)) % n) for i in range(n)])


def mp_perm(x, d):
    return lax.ppermute(x, "mp", [(i, (i + d) % NX) for i in range(NX)])


def nt(a, b):
    return lax.dot_general(a, b, (((1,), (1,)), ((), ())), preferred_element_type=F32)


def nn(a, b):
    return lax.dot_general(a, b, (((1,), (0,)), ((), ())), preferred_element_type=F32)


def split_cache_kernel(head_ref, src, out):
    for b in range(2):
        rows = slice(b * BLOCK, (b + 1) * BLOCK)
        out[b, 0] = src[0, rows, 0, :]
        out[b, 1] = src[0, rows, 1, :].T


def split_cache(head, rows, holders=1):
    return pl.pallas_call(
        split_cache_kernel,
        grid_spec=pltpu.PrefetchScalarGridSpec(
            num_scalar_prefetch=1,
            grid=(8,),
            in_specs=[pl.BlockSpec((1, 256, 2, HD), lambda i, h: (i // 4, i % 4, 0, h[0]))],
            out_specs=pl.BlockSpec((2, 2, BLOCK, HD), lambda i, h: (i, 0, 0, 0)),
        ),
        out_shape=jax.ShapeDtypeStruct((16 * holders, 2, BLOCK, HD), BF16),
        compiler_params=params(),
        cost_estimate=BRIEF,
        name="split_cache",
    )(head, rows)


def project_kernel(core_ref, tok_ref, gain_ref, wq, wk, wv, q_all, swap, k_all, v_all, edge):
    step = pl.program_id(0)
    core = core_ref[0]
    x = tok_ref[...].astype(F32)
    inverse = lax.rsqrt(jnp.mean(x * x, axis=1, keepdims=True) + 1e-05)
    normed = (x * inverse * gain_ref[...]).astype(BF16)
    q = nn(normed, wq[...]).astype(BF16)
    k = nn(normed, wk[...]).astype(BF16)
    v = nn(normed, wv[...])

    def put(here):
        to_first = swap if here else edge
        to_last = edge if here else swap
        for h in range(4):
            slot = (h - 2 * here) % 4
            lanes = slice(h * HD, (h + 1) * HD)
            q_all[slot] = q[:, lanes]
            if slot >= 2:
                swap[pl.ds((slot - 2) * 1024 + pl.multiple_of(step * 256, 256), 256), :] = q[:, lanes]
            for b in range(2):
                rows = slice(b * BLOCK, (b + 1) * BLOCK)
                kb = k[rows, lanes]
                vb = v[rows, lanes].T.astype(BF16)
                k_all[slot, b] = kb
                v_all[slot, b] = vb
                out, when = (to_first, 0) if b == 0 else (to_last, pl.num_programs(0) - 1)
                base = 2048 if out is swap else 0

                @pl.when(step == when)
                def _():
                    out[base + slot * HD : base + (slot + 1) * HD, :] = kb
                    out[base + (4 + slot) * HD : base + (5 + slot) * HD, :] = vb

    @pl.when(core == 0)
    def _():
        put(0)

    @pl.when(core == 1)
    def _():
        put(1)


def project(core, tokens, gain, wq, wk, wv):
    n, d = tokens.shape
    w = wq.shape[1]
    weight = pl.BlockSpec((d, w), lambda i, c: (0, 0), pipeline_mode=pl.Buffered(1))
    blocks = pl.BlockSpec((4, 2, BLOCK, HD), lambda i, c: (0, i, 0, 0))
    return pl.pallas_call(
        project_kernel,
        grid_spec=pltpu.PrefetchScalarGridSpec(
            num_scalar_prefetch=1,
            grid=(n // 256,),
            in_specs=[
                pl.BlockSpec((256, d), lambda i, c: (i, 0)),
                pl.BlockSpec((1, d), lambda i, c: (0, 0)),
                weight,
                weight,
                weight,
            ],
            out_specs=[
                pl.BlockSpec((4, 256, HD), lambda i, c: (0, i, 0)),
                pl.BlockSpec((3072, HD), lambda i, c: (0, 0)),
                blocks,
                blocks,
                pl.BlockSpec((1024, HD), lambda i, c: (0, 0)),
            ],
        ),
        out_shape=[
            jax.ShapeDtypeStruct((4, n, HD), BF16),
            jax.ShapeDtypeStruct((3072, HD), BF16),
            jax.ShapeDtypeStruct((4, 8, BLOCK, HD), BF16),
            jax.ShapeDtypeStruct((4, 8, HD, BLOCK), BF16),
            jax.ShapeDtypeStruct((1024, HD), BF16),
        ],
        compiler_params=params(),
        cost_estimate=BRIEF,
        name="project",
    )(core, tokens, gain.reshape(1, d), wq, wk, wv)


def near_kernel(core_ref, q_ref, k_ref, v_ref, ka, va, kb, vb, o_ref, lse_ref):
    first = core_ref[0] == 0
    klo, khi = jnp.where(first, ka[0], kb[0]), jnp.where(first, kb[0], ka[0])
    vlo, vhi = jnp.where(first, va[0], vb[0]), jnp.where(first, vb[0], va[0])
    for b in range(8):
        q = q_ref[0, b * BLOCK : (b + 1) * BLOCK]
        ks = [klo if b == 0 else k_ref[0, b - 1], k_ref[0, b], khi if b == 7 else k_ref[0, b + 1]]
        vs = [vlo if b == 0 else v_ref[0, b - 1], v_ref[0, b], vhi if b == 7 else v_ref[0, b + 1]]
        s = [nt(k, q) * SCALE for k in ks]
        m = jnp.max(jnp.maximum(jnp.maximum(s[0], s[1]), s[2]), axis=0, keepdims=True)
        p = [jnp.exp(x - m) for x in s]
        total = jnp.sum(p[0] + p[1] + p[2], axis=0, keepdims=True)
        acc = nn(vs[0], p[0].astype(BF16)) + nn(vs[1], p[1].astype(BF16)) + nn(vs[2], p[2].astype(BF16))
        o_ref[0, b] = acc / total
        lse_ref[0, b : b + 1, :] = m + jnp.log(total)


def near(core, q, k, v, halo, swapped):
    blocks = pl.BlockSpec((1, 8, BLOCK, HD), lambda s, c: (s, 0, 0, 0))

    def edge(first):
        return pl.BlockSpec((1, BLOCK, HD), lambda s, c: (first + (s + 2) % 4, 0, 0))

    return pl.pallas_call(
        near_kernel,
        grid_spec=pltpu.PrefetchScalarGridSpec(
            num_scalar_prefetch=1,
            grid=(4,),
            in_specs=[pl.BlockSpec((1, 1024, HD), lambda s, c: (s, 0, 0)), blocks, blocks]
            + [edge(0), edge(4), edge(16), edge(20)],
            out_specs=[blocks, pl.BlockSpec((1, 8, HD), lambda s, c: (s, 0, 0))],
        ),
        out_shape=[jax.ShapeDtypeStruct((4, 8, HD, BLOCK), F32), jax.ShapeDtypeStruct((4, 8, BLOCK), F32)],
        compiler_params=params(),
        cost_estimate=BRIEF,
        name="near",
    )(core, q, k, v, halo.reshape(8, BLOCK, HD), halo.reshape(8, BLOCK, HD), swapped.reshape(24, BLOCK, HD), swapped.reshape(24, BLOCK, HD))


GROUP = 4
UNITS = 96 + GROUP


def plan_kernel(cnt_ref, code_ref, unit_ref, first_ref, long_ref, size_ref, list_ref):
    def scan(i, carry):
        u, m = carry
        n = cnt_ref[i]
        first_ref[i] = u

        def named(carry):
            u, m = carry
            at = jnp.int32(0)
            for w in range(WMAX):
                code = code_ref[i * WMAX + w]
                list_ref[at] = code
                at = at + (code >= 0).astype(jnp.int32)

            def unit(k, u):
                both = (2 * k + 1 < n).astype(jnp.int32)
                unit_ref[u] = both * (1 << 22) + i * (1 << 16) + list_ref[2 * k] * 256 + list_ref[2 * k + both]
                return u + 1

            long_ref[m] = i
            return lax.fori_loop(0, lax.shift_right_logical(n + 1, 1), unit, u), m + (n > 2).astype(jnp.int32)

        return lax.cond(n > 0, named, lambda carry: carry, (u, m))

    units, longs = lax.fori_loop(0, 64, scan, (jnp.int32(0), jnp.int32(0)))
    for g in range(GROUP):
        unit_ref[units + g] = -1
    size_ref[0] = units
    size_ref[1] = longs


def plan(cnt, code):
    def out(n):
        return jax.ShapeDtypeStruct((n,), jnp.int32)

    return pl.pallas_call(
        plan_kernel,
        in_specs=[SMEM] * 2,
        out_specs=[SMEM] * 4,
        out_shape=[out(UNITS), out(64), out(64), out(2)],
        scratch_shapes=[pltpu.SMEM((2 * WMAX,), jnp.int32)],
        compiler_params=params(16),
        cost_estimate=BRIEF,
        name="plan",
    )(cnt, code)


def far_kernel(j, cnt_ref, unit_ref, first_ref, long_ref, size_ref, *rest):
    sources, qs, outs = rest[:5], rest[5:9], rest[9:13]
    kvbuf, qbuf, obuf, acc_ref, stat_ref, logs, kvsem, qsem, osem = rest[13:]
    units = size_ref[0]
    copies = [pltpu.make_async_copy(qs[r].at[:, j], qbuf.at[pl.ds(2 * r, 2)], qsem.at[r]) for r in range(4)]
    for k, (first, size) in enumerate(((0, 32), (32, 32), (64, 16), (80, 16), (96, 32))):
        copies.append(pltpu.make_async_copy(sources[k], kvbuf.at[pl.ds(first, size)], kvsem.at[k]))
    for copy in copies:
        copy.start()
    logs[...] = jnp.full((64, BLOCK), NEG, F32)
    for copy in copies:
        copy.wait()

    def store(i, m, total, acc):
        rows = pl.ds(pl.multiple_of(lax.bitwise_and(i, 15) * HD, HD), HD)
        obuf[lax.shift_right_logical(i, 4), rows, :] = (acc * (1.0 / total)).astype(BF16)
        logs[pl.ds(i, 1), :] = m + jnp.log(total)

    def group(g, _):
        for t in range(GROUP):
            u = g * GROUP + t
            unit = unit_ref[u]
            unit = jnp.where(unit >= 0, unit, unit_ref[g * GROUP])
            both = lax.shift_right_logical(unit, 22) == 1
            i = lax.bitwise_and(lax.shift_right_logical(unit, 16), 63)
            ea = lax.bitwise_and(lax.shift_right_logical(unit, 8), 127)
            eb = lax.bitwise_and(unit, 127)
            q = qbuf[lax.shift_right_logical(i, 3), lax.bitwise_and(i, 7)]
            s = nt(jnp.concatenate([kvbuf[ea, 0], kvbuf[eb, 0]], axis=0), q) * SCALE
            sa, sb = s[:BLOCK], jnp.where(both, s[BLOCK:], NEG)
            m = jnp.max(jnp.maximum(sa, sb), axis=0, keepdims=True)
            pa, pb = jnp.exp(sa - m), jnp.exp(sb - m)
            total = jnp.sum(pa + pb, axis=0, keepdims=True)
            p = jnp.concatenate([pa, pb], axis=0).astype(BF16)
            acc = nn(jnp.concatenate([kvbuf[ea, 1], kvbuf[eb, 1]], axis=1), p)
            stat_ref[u, 0:1, :] = m
            stat_ref[u, 1:2, :] = total
            acc_ref[u] = acc
            store(i, m, total, acc)
        return 0

    lax.fori_loop(0, lax.div(units + GROUP - 1, GROUP), group, 0)

    def join(k, _):
        i = long_ref[k]
        n = cnt_ref[i]
        u = first_ref[i]

        def more(k, carry):
            m, total, acc = carry
            mk, tk = stat_ref[k, 0:1, :], stat_ref[k, 1:2, :]
            top = jnp.maximum(m, mk)
            old, new = jnp.exp(m - top), jnp.exp(mk - top)
            return top, total * old + tk * new, acc * old + acc_ref[k] * new

        start = (stat_ref[u, 0:1, :], stat_ref[u, 1:2, :], acc_ref[u])
        store(i, *lax.fori_loop(u + 1, u + lax.shift_right_logical(n + 1, 1), more, start))
        return 0

    lax.fori_loop(0, size_ref[1], join, 0)
    for r in range(4):
        part = logs[r * 16 : (r + 1) * 16, :]
        for t in range(3):
            term = part.astype(BF16)
            obuf[r, 2048 + t * 16 : 2064 + t * 16, :] = term
            part = part - term.astype(F32)
        pltpu.make_async_copy(obuf.at[r], outs[r], osem.at[r]).start()
    for r in range(4):
        pltpu.make_async_copy(obuf.at[r], outs[r], osem.at[r]).wait()


def far(j, cnt, lists, sources, qs):
    out = jax.ShapeDtypeStruct((OROWS, BLOCK), BF16)
    return pl.pallas_call(
        functools.partial(far_kernel, j),
        in_specs=[SMEM] * 5 + [ANY] * 9,
        out_specs=[ANY] * 4,
        out_shape=[out] * 4,
        scratch_shapes=[
            pltpu.VMEM((128, 2, BLOCK, HD), BF16),
            pltpu.VMEM((8, 8, BLOCK, HD), BF16),
            pltpu.VMEM((4, OROWS, BLOCK), BF16),
            pltpu.VMEM((UNITS, HD, BLOCK), F32),
            pltpu.VMEM((UNITS, 8, BLOCK), F32),
            pltpu.VMEM((64, BLOCK), F32),
            pltpu.SemaphoreType.DMA((5,)),
            pltpu.SemaphoreType.DMA((4,)),
            pltpu.SemaphoreType.DMA((4,)),
        ],
        compiler_params=params(),
        cost_estimate=BRIEF,
        name="far",
    )(cnt, *lists, *sources, *qs)


def merge_kernel(a, b, c, d, keep, send):
    parts = (a, b, c, d)
    logs = [sum(p[2048 + t * 16 : 2064 + t * 16, :].astype(F32) for t in range(3)) for p in parts]
    peak = functools.reduce(jnp.maximum, logs)
    shares = [jnp.where(x > 0.5 * NEG, jnp.exp(x - peak), 0.0) for x in logs]
    total = sum(shares)
    joint = jnp.where(total > 0.0, peak + jnp.log(total), NEG)
    total = jnp.where(total > 0.0, total, 1.0)
    live = [x > 0.5 * NEG for x in logs]
    shares = [x / total for x in shares]
    for s, out in enumerate((keep, send)):
        for i in range(8):
            row = s * 8 + i
            rows = slice(row * HD, (row + 1) * HD)
            out[i * HD : (i + 1) * HD, :] = sum(
                jnp.where(on[row : row + 1, :], x[row : row + 1, :] * p[rows, :].astype(F32), 0.0)
                for on, x, p in zip(live, shares, parts)
            )
        out[1024:1032, :] = joint[s * 8 : (s + 1) * 8, :]


def merge(parts):
    out = jax.ShapeDtypeStruct((FROWS, BLOCK), F32)
    return pl.pallas_call(
        merge_kernel,
        out_shape=[out, out],
        compiler_params=params(),
        cost_estimate=BRIEF,
        name="merge",
    )(*parts)


def finish_kernel(near_a, lse_a, near_b, lse_b, far_a, far_b, out):
    for s, (o, log, f) in enumerate(((near_a, lse_a, far_a), (near_b, lse_b, far_b))):
        here, away = log[0], f[1024:1032, :]
        peak = jnp.maximum(here, away)
        wn, wf = jnp.exp(here - peak), jnp.exp(away - peak)
        total = wn + wf
        wn, wf = wn / total, wf / total
        for b in range(8):
            both = wn[b : b + 1, :] * o[0, b] + wf[b : b + 1, :] * f[b * HD : (b + 1) * HD, :]
            out[s, b * BLOCK : (b + 1) * BLOCK, :] = both.T.astype(BF16)


def finish(j, o, lse, far_keep, far_other):
    def at(slot):
        return [
            pl.BlockSpec((1, 8, HD, BLOCK), lambda i: (slot, 0, 0, 0)),
            pl.BlockSpec((1, 8, BLOCK), lambda i: (slot, 0, 0)),
        ]

    whole = pl.BlockSpec((FROWS, BLOCK), lambda i: (0, 0))
    return pl.pallas_call(
        finish_kernel,
        grid=(1,),
        in_specs=at(j) + at(2 + j) + [whole, whole],
        out_specs=pl.BlockSpec((2, 1024, HD), lambda i: (0, 0, 0)),
        out_shape=jax.ShapeDtypeStruct((2, 1024, HD), BF16),
        compiler_params=params(),
        cost_estimate=BRIEF,
        name="finish",
    )(o, lse, o, lse, far_keep, far_other)


def pick_kernel(place_ref, *rest):
    for j in range(2):
        for k in range(8):
            rest[16 + j][k * HD : (k + 1) * HD, :] = rest[j * 8 + k][...]


def pick(place, w_out):
    def weight(j, rel, s):
        return pl.BlockSpec((HD, 512), lambda i, p: ((p[1] + rel) % NX * 4 + (2 * p[0] + 2 * s + j) % 4, p[1]))

    out = jax.ShapeDtypeStruct((1024, 512), BF16)
    return pl.pallas_call(
        pick_kernel,
        grid_spec=pltpu.PrefetchScalarGridSpec(
            num_scalar_prefetch=1,
            grid=(1,),
            in_specs=[weight(j, rel, s) for j in range(2) for rel in range(4) for s in range(2)],
            out_specs=[pl.BlockSpec((1024, 512), lambda i, p: (0, 0))] * 2,
        ),
        out_shape=[out, out],
        compiler_params=params(),
        cost_estimate=BRIEF,
        name="pick",
    )(place, *[w_out] * 16)


def mix_kernel(place_ref, a0, a1, a2, a3, weight, carried, out):
    left = jnp.concatenate([a[s] for a in (a0, a1, a2, a3) for s in range(2)], axis=1)
    out[...] = (carried[...].astype(F32) + nn(left, weight[...])).astype(out.dtype)


def mix(place, parts, weight, carried, kind):
    column = 0 if carried.shape[1] == 512 else 1
    return pl.pallas_call(
        mix_kernel,
        grid_spec=pltpu.PrefetchScalarGridSpec(
            num_scalar_prefetch=1,
            grid=(4,),
            in_specs=[pl.BlockSpec((2, 256, HD), lambda i, p: (0, i, 0))] * 4
            + [pl.BlockSpec((1024, 512), lambda i, p: (0, 0))]
            + [pl.BlockSpec((256, 512), lambda i, p: (i, p[1] * column))],
            out_specs=pl.BlockSpec((256, 512), lambda i, p: (i, 0)),
        ),
        out_shape=jax.ShapeDtypeStruct((1024, 512), kind),
        compiler_params=params(),
        cost_estimate=BRIEF,
        name="mix",
    )(place, *parts, weight, carried)


def line_codes(wake_blocks, wake_frames, wake_counts, y, z, c):
    live = jnp.arange(WMAX, dtype=jnp.int32)[None, :] < wake_counts[:, None]
    word = jnp.where(live, wake_frames * 256 + wake_blocks, -1).reshape(NY, NZ, NC, 8, WMAX)
    by_y = lax.dynamic_index_in_dim(word, y, 0, keepdims=False)
    by_z = lax.dynamic_index_in_dim(word, z, 1, keepdims=False)
    here = jnp.where(c == 0, by_y, by_z)
    here = lax.dynamic_slice_in_dim(jnp.concatenate([here, here], axis=0), jnp.where(c == 0, z, y), 4, 0)
    here = lax.dynamic_slice_in_dim(jnp.concatenate([here, here], axis=1), c, 2, 1)
    word = here.reshape(64, WMAX)
    block, frame = word & 255, word >> 8
    hc, hz, hy = (block >> 3) & 1, (block >> 4) & 3, (block >> 6) & 3
    in_line = (word >= 0) & (jnp.where(c == 0, hz, hy) == jnp.where(c == 0, z, y))
    piece = (jnp.where(c == 0, hy, hz) - jnp.where(c == 0, y, z)) & 3
    code = piece * 32 + (hc ^ c) * 16 + (frame & 1) * 8 + (block & 7)
    code = jnp.where(in_line, code, -1)
    return code.reshape(512), jnp.sum(in_line.astype(jnp.int32), axis=1)


def on_device(tokens, norm_gain, w_query, w_key, w_value, w_out, kv_cache, wake_blocks, wake_frames, wake_counts):
    tok = lax.axis_index("tok").astype(jnp.int32)
    mp = lax.axis_index("mp").astype(jnp.int32)
    c, z, y = tok % NC, (tok // NC) % NZ, tok // (NC * NZ)
    core = c.reshape(1)
    place = jnp.stack([c, mp])

    def after(x, *deps):
        return lax.optimization_barrier((x, *deps))[0]

    def rows_of(j, gate):
        got = core_swap(split_cache(2 - 2 * gate + j, kv_cache))
        return lax.dynamic_update_slice(split_cache(2 * gate + j, kv_cache, 2), got, (16, 0, 0, 0))

    rows0 = rows_of(0, core)
    up0, down0 = rows_perm(rows0, 1), rows_perm(rows0, -1)
    rows1 = rows_of(1, after(core, rows0))

    gain, rows1 = lax.optimization_barrier((norm_gain, rows1))
    q_all, swap, k_all, v_all, edge = project(core, tokens, gain, w_query, w_key, w_value)
    swapped, halo = core_swap(swap), halo_perm(edge)
    mine = jnp.concatenate([q_all[:2], swapped[:2048].reshape(2, 1024, HD)], axis=0).reshape(2, 2, 8, BLOCK, HD)
    mine, halo, up0, down0 = lax.optimization_barrier((mine, halo, up0, down0))
    up20, down20 = rows_perm(up0[:16], 1), rows_perm(down0[16:], -1)
    q1, q3, q2 = query_perm(mine, -1), query_perm(mine, 1), query_perm(mine, 2)

    near_o, near_lse = near(core, q_all, k_all, v_all, after(halo, mine), swapped)
    code, cnt = line_codes(wake_blocks, wake_frames, wake_counts, y, z, c)
    lists = plan(cnt, code)
    weights = pick(after(place, mine), w_out)
    held = (*weights, rows1, near_o, near_lse, up20, down20, q1, q2, q3, *lists)
    *weights, rows1, near_o, near_lse, up20, down20, q1, q2, q3, e, f, g, h = lax.optimization_barrier(held)
    lists = [e, f, g, h]
    up1, down1 = rows_perm(rows1, 1), rows_perm(rows1, -1)
    qs = [mine, q1, q2, q3]

    def returned(parts):
        return [parts[0], query_perm(parts[1], 1), query_perm(parts[2], 2), query_perm(parts[3], -1)]

    def gather(heads):
        return [heads, mp_perm(heads, -1), mp_perm(heads, 2), mp_perm(heads, 1)]

    parts = far(0, cnt, lists, [rows0, down0, up20, down20, up0], qs)
    back = returned(parts)
    back[1], back[3], up1, down1 = lax.optimization_barrier((back[1], back[3], up1, down1))
    up21, down21 = rows_perm(up1[:16], 1), rows_perm(down1[16:], -1)
    near_lse, up21, down21 = lax.optimization_barrier((near_lse, up21, down21))
    own, other = merge(back)
    heads = finish(0, near_o, near_lse, own, core_swap(other))
    gathered = gather(heads)

    parts = far(1, cnt, lists, [after(rows1, heads), down1, up21, down21, up1], qs)
    *parts, gathered[1], gathered[3] = lax.optimization_barrier((*parts, gathered[1], gathered[3]))
    back = returned(parts)
    gathered[0] = after(gathered[0], parts[0])
    acc = mix(place, gathered, weights[0], tokens, F32)
    back[0], acc = lax.optimization_barrier((back[0], acc))
    own, other = merge(back)
    heads = finish(1, near_o, near_lse, own, core_swap(other))
    return mix(place, gather(heads), weights[1], acc, BF16)


def solution(mesh):
    return jax.shard_map(
        on_device,
        mesh=mesh,
        in_specs=(
            P("tok", None),
            P(),
            P(None, "mp"),
            P(None, "mp"),
            P(None, "mp"),
            P(),
            P(None, "tok", None, "mp"),
            P(),
            P(),
            P(),
        ),
        out_specs=P("tok", "mp"),
        check_vma=False,
    )
```

```python
import functools
import math

import jax
import jax.numpy as jnp
from jax import lax
from jax.experimental import pallas as pl
from jax.experimental.pallas import tpu as pltpu
from jax.sharding import PartitionSpec as P

HD = 128
BLOCK = 128
WMAX = 8
NEG = -1e30
SCALE = 1.0 / math.sqrt(HD)
NY, NZ, NC, NX = 4, 4, 2, 4
F32, BF16 = jnp.float32, jnp.bfloat16
ANY = pl.BlockSpec(memory_space=pl.ANY)
SMEM = pl.BlockSpec(memory_space=pltpu.SMEM)
BRIEF = pl.CostEstimate(flops=1, transcendentals=0, bytes_accessed=1)
OROWS = 2048 + 48
FROWS = 1024 + 8


def params(mib=48):
    return pltpu.CompilerParams(vmem_limit_bytes=mib << 20)


def tok_of(y, z, c):
    return ((y % NY) * NZ + z % NZ) * NC + c % NC


def chips():
    return [(y, z, c) for y in range(NY) for z in range(NZ) for c in range(NC)]


def rows_perm(x, d):
    pairs = [(tok_of(y, z, c), tok_of(y + d, z, c) if c == 0 else tok_of(y, z + d, c)) for y, z, c in chips()]
    return lax.ppermute(x, "tok", pairs)


def query_perm(x, d):
    pairs = [(tok_of(y, z, c), tok_of(y, z + d, c) if c == 0 else tok_of(y + d, z, c)) for y, z, c in chips()]
    return lax.ppermute(x, "tok", pairs)


def core_swap(x):
    return lax.ppermute(x, "tok", [(tok_of(y, z, c), tok_of(y, z, 1 - c)) for y, z, c in chips()])


def halo_perm(x):
    n = NY * NZ * NC
    return lax.ppermute(x, "tok", [(i, (i + (1 if i % 2 else -1)) % n) for i in range(n)])


def mp_perm(x, d):
    return lax.ppermute(x, "mp", [(i, (i + d) % NX) for i in range(NX)])


def nt(a, b):
    return lax.dot_general(a, b, (((1,), (1,)), ((), ())), preferred_element_type=F32)


def nn(a, b):
    return lax.dot_general(a, b, (((1,), (0,)), ((), ())), preferred_element_type=F32)


def split_cache_kernel(head_ref, src, out):
    for b in range(2):
        rows = slice(b * BLOCK, (b + 1) * BLOCK)
        out[b, 0] = src[0, rows, 0, :]
        out[b, 1] = src[0, rows, 1, :].T


def split_cache(head, rows, holders=1):
    return pl.pallas_call(
        split_cache_kernel,
        grid_spec=pltpu.PrefetchScalarGridSpec(
            num_scalar_prefetch=1,
            grid=(8,),
            in_specs=[pl.BlockSpec((1, 256, 2, HD), lambda i, h: (i // 4, i % 4, 0, h[0]))],
            out_specs=pl.BlockSpec((2, 2, BLOCK, HD), lambda i, h: (i, 0, 0, 0)),
        ),
        out_shape=jax.ShapeDtypeStruct((16 * holders, 2, BLOCK, HD), BF16),
        compiler_params=params(),
        cost_estimate=BRIEF,
        name="split_cache",
    )(head, rows)


def normalise(tok_ref, gain_ref):
    x = tok_ref[...].astype(F32)
    inverse = lax.rsqrt(jnp.mean(x * x, axis=1, keepdims=True) + 1e-05)
    return (x * inverse * gain_ref[...]).astype(BF16)


def both_cores(core, put):
    for here in range(2):
        pl.when(core == here)(functools.partial(put, here))


def query_kernel(core_ref, tok_ref, gain_ref, wq, normed_ref, keep, send):
    normed = normalise(tok_ref, gain_ref)
    normed_ref[...] = normed
    q = nn(normed, wq[...]).astype(BF16)

    def put(here):
        for h in range(4):
            slot = (h - 2 * here) % 4
            out = keep if slot < 2 else send
            out[slot % 2] = q[:, h * HD : (h + 1) * HD]

    both_cores(core_ref[0], put)


def query(core, tokens, gain, wq):
    n, d = tokens.shape
    half = jax.ShapeDtypeStruct((2, n, HD), BF16)
    heads = pl.BlockSpec((2, 256, HD), lambda i, c: (0, i, 0))
    return pl.pallas_call(
        query_kernel,
        grid_spec=pltpu.PrefetchScalarGridSpec(
            num_scalar_prefetch=1,
            grid=(n // 256,),
            in_specs=[
                pl.BlockSpec((256, d), lambda i, c: (i, 0)),
                pl.BlockSpec((1, d), lambda i, c: (0, 0)),
                pl.BlockSpec((d, wq.shape[1]), lambda i, c: (0, 0), pipeline_mode=pl.Buffered(1)),
            ],
            out_specs=[pl.BlockSpec((256, d), lambda i, c: (i, 0)), heads, heads],
        ),
        out_shape=[jax.ShapeDtypeStruct((n, d), BF16), half, half],
        compiler_params=params(),
        cost_estimate=BRIEF,
        name="query",
    )(core, tokens, gain.reshape(1, d), wq)


def project_kernel(core_ref, normed_ref, wk, wv, k_all, v_all, swap, edge):
    step = pl.program_id(0)
    normed = normed_ref[...]
    k = nn(normed, wk[...]).astype(BF16)
    v = nn(normed, wv[...])

    def put(here):
        to_first = swap if here else edge
        to_last = edge if here else swap
        for h in range(4):
            slot = (h - 2 * here) % 4
            lanes = slice(h * HD, (h + 1) * HD)
            for b in range(2):
                rows = slice(b * BLOCK, (b + 1) * BLOCK)
                kb = k[rows, lanes]
                vb = v[rows, lanes].T.astype(BF16)
                k_all[slot, b] = kb
                v_all[slot, b] = vb
                out, when = (to_first, 0) if b == 0 else (to_last, pl.num_programs(0) - 1)

                @pl.when(step == when)
                def _():
                    out[slot * HD : (slot + 1) * HD, :] = kb
                    out[(4 + slot) * HD : (5 + slot) * HD, :] = vb

    both_cores(core_ref[0], put)


def project(core, normed, wk, wv):
    n, d = normed.shape
    weight = pl.BlockSpec((d, wk.shape[1]), lambda i, c: (0, 0), pipeline_mode=pl.Buffered(1))
    blocks = pl.BlockSpec((4, 2, BLOCK, HD), lambda i, c: (0, i, 0, 0))
    edge = pl.BlockSpec((1024, HD), lambda i, c: (0, 0))
    return pl.pallas_call(
        project_kernel,
        grid_spec=pltpu.PrefetchScalarGridSpec(
            num_scalar_prefetch=1,
            grid=(n // 256,),
            in_specs=[pl.BlockSpec((256, d), lambda i, c: (i, 0)), weight, weight],
            out_specs=[blocks, blocks, edge, edge],
        ),
        out_shape=[
            jax.ShapeDtypeStruct((4, 8, BLOCK, HD), BF16),
            jax.ShapeDtypeStruct((4, 8, HD, BLOCK), BF16),
            jax.ShapeDtypeStruct((1024, HD), BF16),
            jax.ShapeDtypeStruct((1024, HD), BF16),
        ],
        compiler_params=params(),
        cost_estimate=BRIEF,
        name="project",
    )(core, normed, wk, wv)


def near_kernel(core_ref, qa_ref, qb_ref, k_ref, v_ref, ka, va, kb, vb, o_ref, lse_ref):
    first = core_ref[0] == 0
    klo, khi = jnp.where(first, ka[0], kb[0]), jnp.where(first, kb[0], ka[0])
    vlo, vhi = jnp.where(first, va[0], vb[0]), jnp.where(first, vb[0], va[0])
    mine = pl.program_id(0) < 2
    for b in range(8):
        rows = slice(b * BLOCK, (b + 1) * BLOCK)
        q = jnp.where(mine, qa_ref[0, rows], qb_ref[0, rows])
        ks = [klo if b == 0 else k_ref[0, b - 1], k_ref[0, b], khi if b == 7 else k_ref[0, b + 1]]
        vs = [vlo if b == 0 else v_ref[0, b - 1], v_ref[0, b], vhi if b == 7 else v_ref[0, b + 1]]
        s = [nt(k, q) * SCALE for k in ks]
        m = jnp.max(jnp.maximum(jnp.maximum(s[0], s[1]), s[2]), axis=0, keepdims=True)
        p = [jnp.exp(x - m) for x in s]
        total = jnp.sum(p[0] + p[1] + p[2], axis=0, keepdims=True)
        acc = nn(vs[0], p[0].astype(BF16)) + nn(vs[1], p[1].astype(BF16)) + nn(vs[2], p[2].astype(BF16))
        o_ref[0, b] = acc / total
        lse_ref[0, b : b + 1, :] = m + jnp.log(total)


def near(core, keep, send, k, v, halo, swapped):
    blocks = pl.BlockSpec((1, 8, BLOCK, HD), lambda s, c: (s, 0, 0, 0))

    def edge(first):
        return pl.BlockSpec((1, BLOCK, HD), lambda s, c: (first + (s + 2) % 4, 0, 0))

    return pl.pallas_call(
        near_kernel,
        grid_spec=pltpu.PrefetchScalarGridSpec(
            num_scalar_prefetch=1,
            grid=(4,),
            in_specs=[pl.BlockSpec((1, 1024, HD), lambda s, c: (s % 2, 0, 0))] * 2
            + [blocks, blocks, edge(0), edge(4), edge(0), edge(4)],
            out_specs=[blocks, pl.BlockSpec((1, 8, HD), lambda s, c: (s, 0, 0))],
        ),
        out_shape=[jax.ShapeDtypeStruct((4, 8, HD, BLOCK), F32), jax.ShapeDtypeStruct((4, 8, BLOCK), F32)],
        compiler_params=params(),
        cost_estimate=BRIEF,
        name="near",
    )(core, keep, send, k, v, *[e.reshape(8, BLOCK, HD) for e in (halo, halo, swapped, swapped)])


GROUP = 4
UNITS = 96 + GROUP


def plan_kernel(cnt_ref, code_ref, unit_ref, first_ref, long_ref, size_ref, list_ref):
    def scan(i, carry):
        u, m = carry
        n = cnt_ref[i]
        first_ref[i] = u

        def named(carry):
            u, m = carry
            at = jnp.int32(0)
            for w in range(WMAX):
                code = code_ref[i * WMAX + w]
                list_ref[at] = code
                at = at + (code >= 0).astype(jnp.int32)

            def unit(k, u):
                both = (2 * k + 1 < n).astype(jnp.int32)
                unit_ref[u] = both * (1 << 22) + i * (1 << 16) + list_ref[2 * k] * 256 + list_ref[2 * k + both]
                return u + 1

            long_ref[m] = i
            return lax.fori_loop(0, lax.shift_right_logical(n + 1, 1), unit, u), m + (n > 2).astype(jnp.int32)

        return lax.cond(n > 0, named, lambda carry: carry, (u, m))

    units, longs = lax.fori_loop(0, 64, scan, (jnp.int32(0), jnp.int32(0)))
    for g in range(GROUP):
        unit_ref[units + g] = -1
    size_ref[0] = units
    size_ref[1] = longs


def plan(cnt, code):
    def out(n):
        return jax.ShapeDtypeStruct((n,), jnp.int32)

    return pl.pallas_call(
        plan_kernel,
        in_specs=[SMEM] * 2,
        out_specs=[SMEM] * 4,
        out_shape=[out(UNITS), out(64), out(64), out(2)],
        scratch_shapes=[pltpu.SMEM((2 * WMAX,), jnp.int32)],
        compiler_params=params(16),
        cost_estimate=BRIEF,
        name="plan",
    )(cnt, code)


def far_kernel(j, cnt_ref, unit_ref, first_ref, long_ref, size_ref, *rest):
    sources, qs, outs = rest[:5], rest[5:9], rest[9:13]
    kvbuf, qbuf, obuf, acc_ref, stat_ref, logs, kvsem, qsem, osem = rest[13:]
    units = size_ref[0]
    copies = [pltpu.make_async_copy(qs[r].at[:, j], qbuf.at[pl.ds(2 * r, 2)], qsem.at[r]) for r in range(4)]
    for k, (first, size) in enumerate(((0, 32), (32, 32), (64, 16), (80, 16), (96, 32))):
        copies.append(pltpu.make_async_copy(sources[k], kvbuf.at[pl.ds(first, size)], kvsem.at[k]))
    for copy in copies:
        copy.start()
    logs[...] = jnp.full((64, BLOCK), NEG, F32)
    for copy in copies:
        copy.wait()

    def store(i, m, total, acc):
        rows = pl.ds(pl.multiple_of(lax.bitwise_and(i, 15) * HD, HD), HD)
        obuf[lax.shift_right_logical(i, 4), rows, :] = (acc * (1.0 / total)).astype(BF16)
        logs[pl.ds(i, 1), :] = m + jnp.log(total)

    def group(g, _):
        for t in range(GROUP):
            u = g * GROUP + t
            unit = unit_ref[u]
            unit = jnp.where(unit >= 0, unit, unit_ref[g * GROUP])
            both = lax.shift_right_logical(unit, 22) == 1
            i = lax.bitwise_and(lax.shift_right_logical(unit, 16), 63)
            ea = lax.bitwise_and(lax.shift_right_logical(unit, 8), 127)
            eb = lax.bitwise_and(unit, 127)
            q = qbuf[lax.shift_right_logical(i, 3), lax.bitwise_and(i, 7)]
            s = nt(jnp.concatenate([kvbuf[ea, 0], kvbuf[eb, 0]], axis=0), q) * SCALE
            sa, sb = s[:BLOCK], jnp.where(both, s[BLOCK:], NEG)
            m = jnp.max(jnp.maximum(sa, sb), axis=0, keepdims=True)
            pa, pb = jnp.exp(sa - m), jnp.exp(sb - m)
            total = jnp.sum(pa + pb, axis=0, keepdims=True)
            p = jnp.concatenate([pa, pb], axis=0).astype(BF16)
            acc = nn(jnp.concatenate([kvbuf[ea, 1], kvbuf[eb, 1]], axis=1), p)
            stat_ref[u, 0:1, :] = m
            stat_ref[u, 1:2, :] = total
            acc_ref[u] = acc
            store(i, m, total, acc)
        return 0

    lax.fori_loop(0, lax.div(units + GROUP - 1, GROUP), group, 0)

    def join(k, _):
        i = long_ref[k]
        n = cnt_ref[i]
        u = first_ref[i]

        def more(k, carry):
            m, total, acc = carry
            mk, tk = stat_ref[k, 0:1, :], stat_ref[k, 1:2, :]
            top = jnp.maximum(m, mk)
            old, new = jnp.exp(m - top), jnp.exp(mk - top)
            return top, total * old + tk * new, acc * old + acc_ref[k] * new

        start = (stat_ref[u, 0:1, :], stat_ref[u, 1:2, :], acc_ref[u])
        store(i, *lax.fori_loop(u + 1, u + lax.shift_right_logical(n + 1, 1), more, start))
        return 0

    lax.fori_loop(0, size_ref[1], join, 0)
    for r in range(4):
        part = logs[r * 16 : (r + 1) * 16, :]
        for t in range(3):
            term = part.astype(BF16)
            obuf[r, 2048 + t * 16 : 2064 + t * 16, :] = term
            part = part - term.astype(F32)
        pltpu.make_async_copy(obuf.at[r], outs[r], osem.at[r]).start()
    for r in range(4):
        pltpu.make_async_copy(obuf.at[r], outs[r], osem.at[r]).wait()


def far(j, cnt, lists, sources, qs):
    out = jax.ShapeDtypeStruct((OROWS, BLOCK), BF16)
    return pl.pallas_call(
        functools.partial(far_kernel, j),
        in_specs=[SMEM] * 5 + [ANY] * 9,
        out_specs=[ANY] * 4,
        out_shape=[out] * 4,
        scratch_shapes=[
            pltpu.VMEM((128, 2, BLOCK, HD), BF16),
            pltpu.VMEM((8, 8, BLOCK, HD), BF16),
            pltpu.VMEM((4, OROWS, BLOCK), BF16),
            pltpu.VMEM((UNITS, HD, BLOCK), F32),
            pltpu.VMEM((UNITS, 8, BLOCK), F32),
            pltpu.VMEM((64, BLOCK), F32),
            pltpu.SemaphoreType.DMA((5,)),
            pltpu.SemaphoreType.DMA((4,)),
            pltpu.SemaphoreType.DMA((4,)),
        ],
        compiler_params=params(),
        cost_estimate=BRIEF,
        name="far",
    )(cnt, *lists, *sources, *qs)


def merge_kernel(a, b, c, d, keep, send):
    parts = (a, b, c, d)
    logs = [sum(p[2048 + t * 16 : 2064 + t * 16, :].astype(F32) for t in range(3)) for p in parts]
    peak = functools.reduce(jnp.maximum, logs)
    shares = [jnp.where(x > 0.5 * NEG, jnp.exp(x - peak), 0.0) for x in logs]
    total = sum(shares)
    joint = jnp.where(total > 0.0, peak + jnp.log(total), NEG)
    total = jnp.where(total > 0.0, total, 1.0)
    live = [x > 0.5 * NEG for x in logs]
    shares = [x / total for x in shares]
    for s, out in enumerate((keep, send)):
        for i in range(8):
            row = s * 8 + i
            rows = slice(row * HD, (row + 1) * HD)
            out[i * HD : (i + 1) * HD, :] = sum(
                jnp.where(on[row : row + 1, :], x[row : row + 1, :] * p[rows, :].astype(F32), 0.0)
                for on, x, p in zip(live, shares, parts)
            )
        out[1024:1032, :] = joint[s * 8 : (s + 1) * 8, :]


def merge(parts):
    out = jax.ShapeDtypeStruct((FROWS, BLOCK), F32)
    return pl.pallas_call(
        merge_kernel,
        out_shape=[out, out],
        compiler_params=params(),
        cost_estimate=BRIEF,
        name="merge",
    )(*parts)


def finish_kernel(near_a, lse_a, near_b, lse_b, far_a, far_b, out):
    for s, (o, log, f) in enumerate(((near_a, lse_a, far_a), (near_b, lse_b, far_b))):
        here, away = log[0], f[1024:1032, :]
        peak = jnp.maximum(here, away)
        wn, wf = jnp.exp(here - peak), jnp.exp(away - peak)
        total = wn + wf
        wn, wf = wn / total, wf / total
        for b in range(8):
            both = wn[b : b + 1, :] * o[0, b] + wf[b : b + 1, :] * f[b * HD : (b + 1) * HD, :]
            out[s, b * BLOCK : (b + 1) * BLOCK, :] = both.T.astype(BF16)


def finish(j, o, lse, far_keep, far_other):
    def at(slot):
        return [
            pl.BlockSpec((1, 8, HD, BLOCK), lambda i: (slot, 0, 0, 0)),
            pl.BlockSpec((1, 8, BLOCK), lambda i: (slot, 0, 0)),
        ]

    whole = pl.BlockSpec((FROWS, BLOCK), lambda i: (0, 0))
    return pl.pallas_call(
        finish_kernel,
        grid=(1,),
        in_specs=at(j) + at(2 + j) + [whole, whole],
        out_specs=pl.BlockSpec((2, 1024, HD), lambda i: (0, 0, 0)),
        out_shape=jax.ShapeDtypeStruct((2, 1024, HD), BF16),
        compiler_params=params(),
        cost_estimate=BRIEF,
        name="finish",
    )(o, lse, o, lse, far_keep, far_other)


def pick_kernel(place_ref, *rest):
    for j in range(2):
        for k in range(8):
            rest[16 + j][k * HD : (k + 1) * HD, :] = rest[j * 8 + k][...]


def pick(place, w_out):
    def weight(j, rel, s):
        return pl.BlockSpec((HD, 512), lambda i, p: ((p[1] + rel) % NX * 4 + (2 * p[0] + 2 * s + j) % 4, p[1]))

    out = jax.ShapeDtypeStruct((1024, 512), BF16)
    return pl.pallas_call(
        pick_kernel,
        grid_spec=pltpu.PrefetchScalarGridSpec(
            num_scalar_prefetch=1,
            grid=(1,),
            in_specs=[weight(j, rel, s) for j in range(2) for rel in range(4) for s in range(2)],
            out_specs=[pl.BlockSpec((1024, 512), lambda i, p: (0, 0))] * 2,
        ),
        out_shape=[out, out],
        compiler_params=params(),
        cost_estimate=BRIEF,
        name="pick",
    )(place, *[w_out] * 16)


def mix_kernel(place_ref, a0, a1, a2, a3, weight, carried, out):
    left = jnp.concatenate([a[s] for a in (a0, a1, a2, a3) for s in range(2)], axis=1)
    out[...] = (carried[...].astype(F32) + nn(left, weight[...])).astype(out.dtype)


def mix(place, parts, weight, carried, kind):
    column = 0 if carried.shape[1] == 512 else 1
    return pl.pallas_call(
        mix_kernel,
        grid_spec=pltpu.PrefetchScalarGridSpec(
            num_scalar_prefetch=1,
            grid=(4,),
            in_specs=[pl.BlockSpec((2, 256, HD), lambda i, p: (0, i, 0))] * 4
            + [pl.BlockSpec((1024, 512), lambda i, p: (0, 0))]
            + [pl.BlockSpec((256, 512), lambda i, p: (i, p[1] * column))],
            out_specs=pl.BlockSpec((256, 512), lambda i, p: (i, 0)),
        ),
        out_shape=jax.ShapeDtypeStruct((1024, 512), kind),
        compiler_params=params(),
        cost_estimate=BRIEF,
        name="mix",
    )(place, *parts, weight, carried)


def line_codes(wake_blocks, wake_frames, wake_counts, y, z, c):
    live = jnp.arange(WMAX, dtype=jnp.int32)[None, :] < wake_counts[:, None]
    word = jnp.where(live, wake_frames * 256 + wake_blocks, -1).reshape(NY, NZ, NC, 8, WMAX)
    by_y = lax.dynamic_index_in_dim(word, y, 0, keepdims=False)
    by_z = lax.dynamic_index_in_dim(word, z, 1, keepdims=False)
    here = jnp.where(c == 0, by_y, by_z)
    here = lax.dynamic_slice_in_dim(jnp.concatenate([here, here], axis=0), jnp.where(c == 0, z, y), 4, 0)
    here = lax.dynamic_slice_in_dim(jnp.concatenate([here, here], axis=1), c, 2, 1)
    word = here.reshape(64, WMAX)
    block, frame = word & 255, word >> 8
    hc, hz, hy = (block >> 3) & 1, (block >> 4) & 3, (block >> 6) & 3
    in_line = (word >= 0) & (jnp.where(c == 0, hz, hy) == jnp.where(c == 0, z, y))
    piece = (jnp.where(c == 0, hy, hz) - jnp.where(c == 0, y, z)) & 3
    code = piece * 32 + (hc ^ c) * 16 + (frame & 1) * 8 + (block & 7)
    code = jnp.where(in_line, code, -1)
    return code.reshape(512), jnp.sum(in_line.astype(jnp.int32), axis=1)


def on_device(tokens, norm_gain, w_query, w_key, w_value, w_out, kv_cache, wake_blocks, wake_frames, wake_counts):
    tok = lax.axis_index("tok").astype(jnp.int32)
    mp = lax.axis_index("mp").astype(jnp.int32)
    c, z, y = tok % NC, (tok // NC) % NZ, tok // (NC * NZ)
    core = c.reshape(1)
    place = jnp.stack([c, mp])

    def after(x, *deps):
        return lax.optimization_barrier((x, *deps))[0]

    normed, q_keep, q_send = query(core, tokens, norm_gain, w_query)
    send0 = split_cache(2 - 2 * after(core, q_send), kv_cache)
    mine = jnp.concatenate([q_keep, core_swap(q_send)], axis=0).reshape(2, 2, 8, BLOCK, HD)
    q1, q3, q2 = query_perm(mine, -1), query_perm(mine, 1), query_perm(mine, 2)

    keep0 = split_cache(2 * after(core, mine), kv_cache, 2)
    rows0 = lax.dynamic_update_slice(keep0, core_swap(send0), (16, 0, 0, 0))
    up0, down0 = rows_perm(rows0, 1), rows_perm(rows0, -1)
    core1 = after(core, rows0)
    send1, keep1 = split_cache(3 - 2 * core1, kv_cache), split_cache(1 + 2 * core1, kv_cache, 2)
    normed, keep1, send1 = lax.optimization_barrier((normed, keep1, send1))
    k_all, v_all, swap, edge = project(core, normed, w_key, w_value)
    send1, swap, edge, q1, q2, q3 = lax.optimization_barrier((send1, swap, edge, q1, q2, q3))
    swapped, halo = core_swap(swap), halo_perm(edge)
    rows1 = lax.dynamic_update_slice(keep1, core_swap(send1), (16, 0, 0, 0))
    code, cnt = line_codes(wake_blocks, wake_frames, wake_counts, y, z, c)
    halo, *lists = lax.optimization_barrier((halo, *plan(cnt, code)))
    near_o, near_lse = near(core, q_keep, q_send, k_all, v_all, halo, swapped)
    up0, down0, near_o, near_lse, rows1 = lax.optimization_barrier((up0, down0, near_o, near_lse, rows1))
    up20, down20 = rows_perm(up0[:16], 1), rows_perm(down0[16:], -1)
    rows1, up20, down20 = lax.optimization_barrier((rows1, up20, down20))
    up1, down1 = rows_perm(rows1, 1), rows_perm(rows1, -1)
    qs = [mine, q1, q2, q3]

    def returned(parts):
        return [parts[0], query_perm(parts[1], 1), query_perm(parts[2], 2), query_perm(parts[3], -1)]

    def gather(heads):
        return [heads, mp_perm(heads, -1), mp_perm(heads, 2), mp_perm(heads, 1)]

    parts = far(0, cnt, lists, [rows0, down0, up20, down20, up0], qs)
    weights = pick(after(place, parts[0]), w_out)
    back = returned(parts)
    back[1], back[3], up1, down1 = lax.optimization_barrier((back[1], back[3], up1, down1))
    up21, down21 = rows_perm(up1[:16], 1), rows_perm(down1[16:], -1)
    back[0], *weights = lax.optimization_barrier((back[0], *weights))
    own, other = merge(back)
    heads = finish(0, near_o, near_lse, own, core_swap(other))
    gathered = gather(heads)

    parts = far(1, cnt, lists, [after(rows1, heads), down1, up21, down21, up1], qs)
    *parts, gathered[1], gathered[3] = lax.optimization_barrier((*parts, gathered[1], gathered[3]))
    back = returned(parts)
    back[0], gathered[2] = lax.optimization_barrier((back[0], gathered[2]))
    own, other = merge(back)
    heads = finish(1, near_o, near_lse, own, core_swap(other))
    gathered[0] = after(gathered[0], heads)
    acc = mix(place, gathered, weights[0], tokens, F32)
    return mix(place, gather(heads), weights[1], acc, BF16)


def solution(mesh):
    return jax.shard_map(
        on_device,
        mesh=mesh,
        in_specs=(
            P("tok", None),
            P(),
            P(None, "mp"),
            P(None, "mp"),
            P(None, "mp"),
            P(),
            P(None, "tok", None, "mp"),
            P(),
            P(),
            P(),
        ),
        out_specs=P("tok", "mp"),
        check_vma=False,
    )
```

```python
import functools
import math

import jax
import jax.numpy as jnp
from jax import lax
from jax.experimental import pallas as pl
from jax.experimental.pallas import tpu as pltpu
from jax.sharding import PartitionSpec as P

HD = 128
BLOCK = 128
WMAX = 8
NEG = -1e30
SCALE = 1.0 / math.sqrt(HD)
NY, NZ, NC, NX = 4, 4, 2, 4
F32, BF16 = jnp.float32, jnp.bfloat16
ANY = pl.BlockSpec(memory_space=pl.ANY)
SMEM = pl.BlockSpec(memory_space=pltpu.SMEM)
BRIEF = pl.CostEstimate(flops=1, transcendentals=0, bytes_accessed=1)
OROWS = 2048 + 48
FROWS = 1024 + 8


def params(mib=48):
    return pltpu.CompilerParams(vmem_limit_bytes=mib << 20)


def tok_of(y, z, c):
    return ((y % NY) * NZ + z % NZ) * NC + c % NC


def chips():
    return [(y, z, c) for y in range(NY) for z in range(NZ) for c in range(NC)]


def rows_perm(x, d):
    pairs = [(tok_of(y, z, c), tok_of(y + d, z, c) if c == 0 else tok_of(y, z + d, c)) for y, z, c in chips()]
    return lax.ppermute(x, "tok", pairs)


def query_perm(x, d):
    pairs = [(tok_of(y, z, c), tok_of(y, z + d, c) if c == 0 else tok_of(y + d, z, c)) for y, z, c in chips()]
    return lax.ppermute(x, "tok", pairs)


def core_swap(x):
    return lax.ppermute(x, "tok", [(tok_of(y, z, c), tok_of(y, z, 1 - c)) for y, z, c in chips()])


def halo_perm(x):
    n = NY * NZ * NC
    return lax.ppermute(x, "tok", [(i, (i + (1 if i % 2 else -1)) % n) for i in range(n)])


def mp_perm(x, d):
    return lax.ppermute(x, "mp", [(i, (i + d) % NX) for i in range(NX)])


def nt(a, b):
    return lax.dot_general(a, b, (((1,), (1,)), ((), ())), preferred_element_type=F32)


def nn(a, b):
    return lax.dot_general(a, b, (((1,), (0,)), ((), ())), preferred_element_type=F32)


def split_cache_kernel(head_ref, src, out):
    for b in range(2):
        rows = slice(b * BLOCK, (b + 1) * BLOCK)
        out[b, 0] = src[0, rows, 0, :]
        out[b, 1] = src[0, rows, 1, :].T


def split_cache(head, rows, holders=1):
    return pl.pallas_call(
        split_cache_kernel,
        grid_spec=pltpu.PrefetchScalarGridSpec(
            num_scalar_prefetch=1,
            grid=(8,),
            in_specs=[pl.BlockSpec((1, 256, 2, HD), lambda i, h: (i // 4, i % 4, 0, h[0]))],
            out_specs=pl.BlockSpec((2, 2, BLOCK, HD), lambda i, h: (i, 0, 0, 0)),
        ),
        out_shape=jax.ShapeDtypeStruct((16 * holders, 2, BLOCK, HD), BF16),
        compiler_params=params(),
        cost_estimate=BRIEF,
        name="split_cache",
    )(head, rows)


def normalise(tok_ref, gain_ref):
    x = tok_ref[...].astype(F32)
    inverse = lax.rsqrt(jnp.mean(x * x, axis=1, keepdims=True) + 1e-05)
    return (x * inverse * gain_ref[...]).astype(BF16)


def both_cores(core, put):
    for here in range(2):
        pl.when(core == here)(functools.partial(put, here))


def query_kernel(core_ref, tok_ref, gain_ref, wq, normed_ref, keep, send):
    normed = normalise(tok_ref, gain_ref)
    normed_ref[...] = normed
    q = nn(normed, wq[...]).astype(BF16)

    def put(here):
        for h in range(4):
            slot = (h - 2 * here) % 4
            out = keep if slot < 2 else send
            out[slot % 2] = q[:, h * HD : (h + 1) * HD]

    both_cores(core_ref[0], put)


def query(core, tokens, gain, wq):
    n, d = tokens.shape
    half = jax.ShapeDtypeStruct((2, n, HD), BF16)
    heads = pl.BlockSpec((2, 256, HD), lambda i, c: (0, i, 0))
    return pl.pallas_call(
        query_kernel,
        grid_spec=pltpu.PrefetchScalarGridSpec(
            num_scalar_prefetch=1,
            grid=(n // 256,),
            in_specs=[
                pl.BlockSpec((256, d), lambda i, c: (i, 0)),
                pl.BlockSpec((1, d), lambda i, c: (0, 0)),
                pl.BlockSpec((d, wq.shape[1]), lambda i, c: (0, 0), pipeline_mode=pl.Buffered(1)),
            ],
            out_specs=[pl.BlockSpec((256, d), lambda i, c: (i, 0)), heads, heads],
        ),
        out_shape=[jax.ShapeDtypeStruct((n, d), BF16), half, half],
        compiler_params=params(),
        cost_estimate=BRIEF,
        name="query",
    )(core, tokens, gain.reshape(1, d), wq)


def project_kernel(core_ref, normed_ref, wk, wv, k_all, v_all, swap, edge):
    step = pl.program_id(0)
    normed = normed_ref[...]
    k = nn(normed, wk[...]).astype(BF16)
    v = nn(normed, wv[...])

    def put(here):
        to_first = swap if here else edge
        to_last = edge if here else swap
        for h in range(4):
            slot = (h - 2 * here) % 4
            lanes = slice(h * HD, (h + 1) * HD)
            for b in range(2):
                rows = slice(b * BLOCK, (b + 1) * BLOCK)
                kb = k[rows, lanes]
                vb = v[rows, lanes].T.astype(BF16)
                k_all[slot, b] = kb
                v_all[slot, b] = vb
                out, when = (to_first, 0) if b == 0 else (to_last, pl.num_programs(0) - 1)

                @pl.when(step == when)
                def _():
                    out[slot * HD : (slot + 1) * HD, :] = kb
                    out[(4 + slot) * HD : (5 + slot) * HD, :] = vb

    both_cores(core_ref[0], put)


def project(core, normed, wk, wv):
    n, d = normed.shape
    weight = pl.BlockSpec((d, wk.shape[1]), lambda i, c: (0, 0), pipeline_mode=pl.Buffered(1))
    blocks = pl.BlockSpec((4, 2, BLOCK, HD), lambda i, c: (0, i, 0, 0))
    edge = pl.BlockSpec((1024, HD), lambda i, c: (0, 0))
    return pl.pallas_call(
        project_kernel,
        grid_spec=pltpu.PrefetchScalarGridSpec(
            num_scalar_prefetch=1,
            grid=(n // 256,),
            in_specs=[pl.BlockSpec((256, d), lambda i, c: (i, 0)), weight, weight],
            out_specs=[blocks, blocks, edge, edge],
        ),
        out_shape=[
            jax.ShapeDtypeStruct((4, 8, BLOCK, HD), BF16),
            jax.ShapeDtypeStruct((4, 8, HD, BLOCK), BF16),
            jax.ShapeDtypeStruct((1024, HD), BF16),
            jax.ShapeDtypeStruct((1024, HD), BF16),
        ],
        compiler_params=params(),
        cost_estimate=BRIEF,
        name="project",
    )(core, normed, wk, wv)


def near_kernel(core_ref, qa_ref, qb_ref, k_ref, v_ref, ka, va, kb, vb, o_ref, lse_ref):
    first = core_ref[0] == 0
    klo, khi = jnp.where(first, ka[0], kb[0]), jnp.where(first, kb[0], ka[0])
    vlo, vhi = jnp.where(first, va[0], vb[0]), jnp.where(first, vb[0], va[0])
    mine = pl.program_id(0) < 2
    for b in range(8):
        rows = slice(b * BLOCK, (b + 1) * BLOCK)
        q = jnp.where(mine, qa_ref[0, rows], qb_ref[0, rows])
        ks = [klo if b == 0 else k_ref[0, b - 1], k_ref[0, b], khi if b == 7 else k_ref[0, b + 1]]
        vs = [vlo if b == 0 else v_ref[0, b - 1], v_ref[0, b], vhi if b == 7 else v_ref[0, b + 1]]
        s = [nt(k, q) * SCALE for k in ks]
        m = jnp.max(jnp.maximum(jnp.maximum(s[0], s[1]), s[2]), axis=0, keepdims=True)
        p = [jnp.exp(x - m) for x in s]
        total = jnp.sum(p[0] + p[1] + p[2], axis=0, keepdims=True)
        acc = nn(vs[0], p[0].astype(BF16)) + nn(vs[1], p[1].astype(BF16)) + nn(vs[2], p[2].astype(BF16))
        o_ref[0, b] = acc / total
        lse_ref[0, b : b + 1, :] = m + jnp.log(total)


def near(core, keep, send, k, v, halo, swapped):
    blocks = pl.BlockSpec((1, 8, BLOCK, HD), lambda s, c: (s, 0, 0, 0))

    def edge(first):
        return pl.BlockSpec((1, BLOCK, HD), lambda s, c: (first + (s + 2) % 4, 0, 0))

    return pl.pallas_call(
        near_kernel,
        grid_spec=pltpu.PrefetchScalarGridSpec(
            num_scalar_prefetch=1,
            grid=(4,),
            in_specs=[pl.BlockSpec((1, 1024, HD), lambda s, c: (s % 2, 0, 0))] * 2
            + [blocks, blocks, edge(0), edge(4), edge(0), edge(4)],
            out_specs=[blocks, pl.BlockSpec((1, 8, HD), lambda s, c: (s, 0, 0))],
        ),
        out_shape=[jax.ShapeDtypeStruct((4, 8, HD, BLOCK), F32), jax.ShapeDtypeStruct((4, 8, BLOCK), F32)],
        compiler_params=params(),
        cost_estimate=BRIEF,
        name="near",
    )(core, keep, send, k, v, *[e.reshape(8, BLOCK, HD) for e in (halo, halo, swapped, swapped)])


GROUP = 4
UNITS = 96 + GROUP


def plan_kernel(cnt_ref, code_ref, unit_ref, first_ref, long_ref, size_ref, list_ref):
    def scan(i, carry):
        u, m = carry
        n = cnt_ref[i]
        first_ref[i] = u

        def named(carry):
            u, m = carry
            at = jnp.int32(0)
            for w in range(WMAX):
                code = code_ref[i * WMAX + w]
                list_ref[at] = code
                at = at + (code >= 0).astype(jnp.int32)

            def unit(k, u):
                both = (2 * k + 1 < n).astype(jnp.int32)
                unit_ref[u] = both * (1 << 22) + i * (1 << 16) + list_ref[2 * k] * 256 + list_ref[2 * k + both]
                return u + 1

            long_ref[m] = i
            return lax.fori_loop(0, lax.shift_right_logical(n + 1, 1), unit, u), m + (n > 2).astype(jnp.int32)

        return lax.cond(n > 0, named, lambda carry: carry, (u, m))

    units, longs = lax.fori_loop(0, 64, scan, (jnp.int32(0), jnp.int32(0)))
    for g in range(GROUP):
        unit_ref[units + g] = -1
    size_ref[0] = units
    size_ref[1] = longs


def plan(cnt, code):
    def out(n):
        return jax.ShapeDtypeStruct((n,), jnp.int32)

    return pl.pallas_call(
        plan_kernel,
        in_specs=[SMEM] * 2,
        out_specs=[SMEM] * 4,
        out_shape=[out(UNITS), out(64), out(64), out(2)],
        scratch_shapes=[pltpu.SMEM((2 * WMAX,), jnp.int32)],
        compiler_params=params(16),
        cost_estimate=BRIEF,
        name="plan",
    )(cnt, code)


def far_kernel(j, cnt_ref, unit_ref, first_ref, long_ref, size_ref, *rest):
    sources, qs, outs = rest[:5], rest[5:9], rest[9:13]
    kvbuf, qbuf, obuf, acc_ref, stat_ref, logs, kvsem, qsem, osem = rest[13:]
    units = size_ref[0]
    copies = [pltpu.make_async_copy(qs[r].at[:, j], qbuf.at[pl.ds(2 * r, 2)], qsem.at[r]) for r in range(4)]
    for k, (first, size) in enumerate(((0, 32), (32, 32), (64, 16), (80, 16), (96, 32))):
        copies.append(pltpu.make_async_copy(sources[k], kvbuf.at[pl.ds(first, size)], kvsem.at[k]))
    for copy in copies:
        copy.start()
    logs[...] = jnp.full((64, BLOCK), NEG, F32)
    for copy in copies:
        copy.wait()

    def store(i, m, total, acc):
        rows = pl.ds(pl.multiple_of(lax.bitwise_and(i, 15) * HD, HD), HD)
        obuf[lax.shift_right_logical(i, 4), rows, :] = (acc * (1.0 / total)).astype(BF16)
        logs[pl.ds(i, 1), :] = m + jnp.log(total)

    def group(g, _):
        for t in range(GROUP):
            u = g * GROUP + t
            unit = unit_ref[u]
            unit = jnp.where(unit >= 0, unit, unit_ref[g * GROUP])
            both = lax.shift_right_logical(unit, 22) == 1
            i = lax.bitwise_and(lax.shift_right_logical(unit, 16), 63)
            ea = lax.bitwise_and(lax.shift_right_logical(unit, 8), 127)
            eb = lax.bitwise_and(unit, 127)
            q = qbuf[lax.shift_right_logical(i, 3), lax.bitwise_and(i, 7)]
            s = nt(jnp.concatenate([kvbuf[ea, 0], kvbuf[eb, 0]], axis=0), q) * SCALE
            sa, sb = s[:BLOCK], jnp.where(both, s[BLOCK:], NEG)
            m = jnp.max(jnp.maximum(sa, sb), axis=0, keepdims=True)
            pa, pb = jnp.exp(sa - m), jnp.exp(sb - m)
            total = jnp.sum(pa + pb, axis=0, keepdims=True)
            p = jnp.concatenate([pa, pb], axis=0).astype(BF16)
            acc = nn(jnp.concatenate([kvbuf[ea, 1], kvbuf[eb, 1]], axis=1), p)
            stat_ref[u, 0:1, :] = m
            stat_ref[u, 1:2, :] = total
            acc_ref[u] = acc
            store(i, m, total, acc)
        return 0

    lax.fori_loop(0, lax.div(units + GROUP - 1, GROUP), group, 0)

    def join(k, _):
        i = long_ref[k]
        n = cnt_ref[i]
        u = first_ref[i]

        def more(k, carry):
            m, total, acc = carry
            mk, tk = stat_ref[k, 0:1, :], stat_ref[k, 1:2, :]
            top = jnp.maximum(m, mk)
            old, new = jnp.exp(m - top), jnp.exp(mk - top)
            return top, total * old + tk * new, acc * old + acc_ref[k] * new

        start = (stat_ref[u, 0:1, :], stat_ref[u, 1:2, :], acc_ref[u])
        store(i, *lax.fori_loop(u + 1, u + lax.shift_right_logical(n + 1, 1), more, start))
        return 0

    lax.fori_loop(0, size_ref[1], join, 0)
    for r in range(4):
        part = logs[r * 16 : (r + 1) * 16, :]
        for t in range(3):
            term = part.astype(BF16)
            obuf[r, 2048 + t * 16 : 2064 + t * 16, :] = term
            part = part - term.astype(F32)
        pltpu.make_async_copy(obuf.at[r], outs[r], osem.at[r]).start()
    for r in range(4):
        pltpu.make_async_copy(obuf.at[r], outs[r], osem.at[r]).wait()


def far(j, cnt, lists, sources, qs):
    out = jax.ShapeDtypeStruct((OROWS, BLOCK), BF16)
    return pl.pallas_call(
        functools.partial(far_kernel, j),
        in_specs=[SMEM] * 5 + [ANY] * 9,
        out_specs=[ANY] * 4,
        out_shape=[out] * 4,
        scratch_shapes=[
            pltpu.VMEM((128, 2, BLOCK, HD), BF16),
            pltpu.VMEM((8, 8, BLOCK, HD), BF16),
            pltpu.VMEM((4, OROWS, BLOCK), BF16),
            pltpu.VMEM((UNITS, HD, BLOCK), F32),
            pltpu.VMEM((UNITS, 8, BLOCK), F32),
            pltpu.VMEM((64, BLOCK), F32),
            pltpu.SemaphoreType.DMA((5,)),
            pltpu.SemaphoreType.DMA((4,)),
            pltpu.SemaphoreType.DMA((4,)),
        ],
        compiler_params=params(),
        cost_estimate=BRIEF,
        name="far",
    )(cnt, *lists, *sources, *qs)


def merge_kernel(a, b, c, d, keep, send):
    parts = (a, b, c, d)
    logs = [sum(p[2048 + t * 16 : 2064 + t * 16, :].astype(F32) for t in range(3)) for p in parts]
    peak = functools.reduce(jnp.maximum, logs)
    shares = [jnp.where(x > 0.5 * NEG, jnp.exp(x - peak), 0.0) for x in logs]
    total = sum(shares)
    joint = jnp.where(total > 0.0, peak + jnp.log(total), NEG)
    total = jnp.where(total > 0.0, total, 1.0)
    live = [x > 0.5 * NEG for x in logs]
    shares = [x / total for x in shares]
    for s, out in enumerate((keep, send)):
        for i in range(8):
            row = s * 8 + i
            rows = slice(row * HD, (row + 1) * HD)
            out[i * HD : (i + 1) * HD, :] = sum(
                jnp.where(on[row : row + 1, :], x[row : row + 1, :] * p[rows, :].astype(F32), 0.0)
                for on, x, p in zip(live, shares, parts)
            )
        out[1024:1032, :] = joint[s * 8 : (s + 1) * 8, :]


def merge(parts):
    out = jax.ShapeDtypeStruct((FROWS, BLOCK), F32)
    return pl.pallas_call(
        merge_kernel,
        out_shape=[out, out],
        compiler_params=params(),
        cost_estimate=BRIEF,
        name="merge",
    )(*parts)


def finish_kernel(near_a, lse_a, near_b, lse_b, far_a, far_b, out):
    for s, (o, log, f) in enumerate(((near_a, lse_a, far_a), (near_b, lse_b, far_b))):
        here, away = log[0], f[1024:1032, :]
        peak = jnp.maximum(here, away)
        wn, wf = jnp.exp(here - peak), jnp.exp(away - peak)
        total = wn + wf
        wn, wf = wn / total, wf / total
        for b in range(8):
            both = wn[b : b + 1, :] * o[0, b] + wf[b : b + 1, :] * f[b * HD : (b + 1) * HD, :]
            out[s, b * BLOCK : (b + 1) * BLOCK, :] = both.T.astype(BF16)


def finish(j, o, lse, far_keep, far_other):
    def at(slot):
        return [
            pl.BlockSpec((1, 8, HD, BLOCK), lambda i: (slot, 0, 0, 0)),
            pl.BlockSpec((1, 8, BLOCK), lambda i: (slot, 0, 0)),
        ]

    whole = pl.BlockSpec((FROWS, BLOCK), lambda i: (0, 0))
    return pl.pallas_call(
        finish_kernel,
        grid=(1,),
        in_specs=at(j) + at(2 + j) + [whole, whole],
        out_specs=pl.BlockSpec((2, 1024, HD), lambda i: (0, 0, 0)),
        out_shape=jax.ShapeDtypeStruct((2, 1024, HD), BF16),
        compiler_params=params(),
        cost_estimate=BRIEF,
        name="finish",
    )(o, lse, o, lse, far_keep, far_other)


def pick_kernel(place_ref, *rest):
    for j in range(2):
        for k in range(8):
            rest[16 + j][k * HD : (k + 1) * HD, :] = rest[j * 8 + k][...]


def pick(place, w_out):
    def weight(j, rel, s):
        return pl.BlockSpec((HD, 512), lambda i, p: ((p[1] + rel) % NX * 4 + (2 * p[0] + 2 * s + j) % 4, p[1]))

    out = jax.ShapeDtypeStruct((1024, 512), BF16)
    return pl.pallas_call(
        pick_kernel,
        grid_spec=pltpu.PrefetchScalarGridSpec(
            num_scalar_prefetch=1,
            grid=(1,),
            in_specs=[weight(j, rel, s) for j in range(2) for rel in range(4) for s in range(2)],
            out_specs=[pl.BlockSpec((1024, 512), lambda i, p: (0, 0))] * 2,
        ),
        out_shape=[out, out],
        compiler_params=params(),
        cost_estimate=BRIEF,
        name="pick",
    )(place, *[w_out] * 16)


def mix_kernel(place_ref, a0, a1, a2, a3, weight, carried, out):
    left = jnp.concatenate([a[s] for a in (a0, a1, a2, a3) for s in range(2)], axis=1)
    out[...] = (carried[...].astype(F32) + nn(left, weight[...])).astype(out.dtype)


def mix(place, parts, weight, carried, kind):
    column = 0 if carried.shape[1] == 512 else 1
    return pl.pallas_call(
        mix_kernel,
        grid_spec=pltpu.PrefetchScalarGridSpec(
            num_scalar_prefetch=1,
            grid=(4,),
            in_specs=[pl.BlockSpec((2, 256, HD), lambda i, p: (0, i, 0))] * 4
            + [pl.BlockSpec((1024, 512), lambda i, p: (0, 0))]
            + [pl.BlockSpec((256, 512), lambda i, p: (i, p[1] * column))],
            out_specs=pl.BlockSpec((256, 512), lambda i, p: (i, 0)),
        ),
        out_shape=jax.ShapeDtypeStruct((1024, 512), kind),
        compiler_params=params(),
        cost_estimate=BRIEF,
        name="mix",
    )(place, *parts, weight, carried)


def line_codes(wake_blocks, wake_frames, wake_counts, y, z, c):
    live = jnp.arange(WMAX, dtype=jnp.int32)[None, :] < wake_counts[:, None]
    word = jnp.where(live, wake_frames * 256 + wake_blocks, -1).reshape(NY, NZ, NC, 8, WMAX)
    by_y = lax.dynamic_index_in_dim(word, y, 0, keepdims=False)
    by_z = lax.dynamic_index_in_dim(word, z, 1, keepdims=False)
    here = jnp.where(c == 0, by_y, by_z)
    here = lax.dynamic_slice_in_dim(jnp.concatenate([here, here], axis=0), jnp.where(c == 0, z, y), 4, 0)
    here = lax.dynamic_slice_in_dim(jnp.concatenate([here, here], axis=1), c, 2, 1)
    word = here.reshape(64, WMAX)
    block, frame = word & 255, word >> 8
    hc, hz, hy = (block >> 3) & 1, (block >> 4) & 3, (block >> 6) & 3
    in_line = (word >= 0) & (jnp.where(c == 0, hz, hy) == jnp.where(c == 0, z, y))
    piece = (jnp.where(c == 0, hy, hz) - jnp.where(c == 0, y, z)) & 3
    code = piece * 32 + (hc ^ c) * 16 + (frame & 1) * 8 + (block & 7)
    code = jnp.where(in_line, code, -1)
    return code.reshape(512), jnp.sum(in_line.astype(jnp.int32), axis=1)


def on_device(tokens, norm_gain, w_query, w_key, w_value, w_out, kv_cache, wake_blocks, wake_frames, wake_counts):
    tok = lax.axis_index("tok").astype(jnp.int32)
    mp = lax.axis_index("mp").astype(jnp.int32)
    c, z, y = tok % NC, (tok // NC) % NZ, tok // (NC * NZ)
    core = c.reshape(1)
    place = jnp.stack([c, mp])

    def after(x, *deps):
        return lax.optimization_barrier((x, *deps))[0]

    got0 = core_swap(split_cache(2 - 2 * core, kv_cache))
    rows0 = lax.dynamic_update_slice(split_cache(2 * core, kv_cache, 2), got0, (16, 0, 0, 0))
    up0, down0 = rows_perm(rows0, 1), rows_perm(rows0, -1)

    normed, q_keep, q_send = query(core, tokens, after(norm_gain, rows0), w_query)
    mine = jnp.concatenate([q_keep, core_swap(q_send)], axis=0).reshape(2, 2, 8, BLOCK, HD)
    q1, q3, q2 = query_perm(mine, -1), query_perm(mine, 1), query_perm(mine, 2)
    core1 = after(core, mine)
    send1, keep1 = split_cache(3 - 2 * core1, kv_cache), split_cache(1 + 2 * core1, kv_cache, 2)
    normed, keep1, send1 = lax.optimization_barrier((normed, keep1, send1))
    k_all, v_all, swap, edge = project(core, normed, w_key, w_value)
    send1, swap, edge, q1, q2, q3 = lax.optimization_barrier((send1, swap, edge, q1, q2, q3))
    swapped, halo = core_swap(swap), halo_perm(edge)
    rows1 = lax.dynamic_update_slice(keep1, core_swap(send1), (16, 0, 0, 0))
    up20, down20 = rows_perm(up0[:16], 1), rows_perm(down0[16:], -1)
    code, cnt = line_codes(wake_blocks, wake_frames, wake_counts, y, z, c)
    lists = plan(cnt, code)
    rows1, up20, down20, *lists = lax.optimization_barrier((rows1, up20, down20, *lists))
    up1, down1 = rows_perm(rows1, 1), rows_perm(rows1, -1)
    qs = [mine, q1, q2, q3]

    def returned(parts):
        return [parts[0], query_perm(parts[1], 1), query_perm(parts[2], 2), query_perm(parts[3], -1)]

    def gather(heads):
        return [heads, mp_perm(heads, -1), mp_perm(heads, 2), mp_perm(heads, 1)]

    parts = far(0, cnt, lists, [rows0, down0, up20, down20, up0], qs)
    weights = pick(after(place, parts[0]), w_out)
    halo, swapped, *_ = lax.optimization_barrier((halo, swapped, parts[0]))
    near_o, near_lse = near(core, q_keep, q_send, k_all, v_all, halo, swapped)
    back = returned(parts)
    back[1], back[3], up1, down1 = lax.optimization_barrier((back[1], back[3], up1, down1))
    up21, down21 = rows_perm(up1[:16], 1), rows_perm(down1[16:], -1)
    back[0], near_lse, *weights = lax.optimization_barrier((back[0], near_lse, *weights))
    own, other = merge(back)
    heads = finish(0, near_o, near_lse, own, core_swap(other))
    gathered = gather(heads)

    parts = far(1, cnt, lists, [after(rows1, heads), down1, up21, down21, up1], qs)
    *parts, gathered[1], gathered[3] = lax.optimization_barrier((*parts, gathered[1], gathered[3]))
    back = returned(parts)
    back[0], gathered[2] = lax.optimization_barrier((back[0], gathered[2]))
    own, other = merge(back)
    heads = finish(1, near_o, near_lse, own, core_swap(other))
    gathered[0] = after(gathered[0], heads)
    acc = mix(place, gathered, weights[0], tokens, F32)
    return mix(place, gather(heads), weights[1], acc, BF16)


def solution(mesh):
    return jax.shard_map(
        on_device,
        mesh=mesh,
        in_specs=(
            P("tok", None),
            P(),
            P(None, "mp"),
            P(None, "mp"),
            P(None, "mp"),
            P(),
            P(None, "tok", None, "mp"),
            P(),
            P(),
            P(),
        ),
        out_specs=P("tok", "mp"),
        check_vma=False,
    )
```

```python
import functools
import math

import jax
import jax.numpy as jnp
from jax import lax
from jax.experimental import pallas as pl
from jax.experimental.pallas import tpu as pltpu
from jax.sharding import PartitionSpec as P

HD = 128
BLOCK = 128
WMAX = 8
NEG = -1e30
SCALE = 1.0 / math.sqrt(HD)
NY, NZ, NC, NX = 4, 4, 2, 4
F32, BF16 = jnp.float32, jnp.bfloat16
ANY = pl.BlockSpec(memory_space=pl.ANY)
SMEM = pl.BlockSpec(memory_space=pltpu.SMEM)
BRIEF = pl.CostEstimate(flops=1, transcendentals=0, bytes_accessed=1)
OROWS = 2048 + 48
FROWS = 1024 + 8


def params(mib=48):
    return pltpu.CompilerParams(vmem_limit_bytes=mib << 20)


def tok_of(y, z, c):
    return ((y % NY) * NZ + z % NZ) * NC + c % NC


def chips():
    return [(y, z, c) for y in range(NY) for z in range(NZ) for c in range(NC)]


def rows_perm(x, d):
    pairs = [(tok_of(y, z, c), tok_of(y + d, z, c) if c == 0 else tok_of(y, z + d, c)) for y, z, c in chips()]
    return lax.ppermute(x, "tok", pairs)


def query_perm(x, d):
    pairs = [(tok_of(y, z, c), tok_of(y, z + d, c) if c == 0 else tok_of(y + d, z, c)) for y, z, c in chips()]
    return lax.ppermute(x, "tok", pairs)


def core_swap(x):
    return lax.ppermute(x, "tok", [(tok_of(y, z, c), tok_of(y, z, 1 - c)) for y, z, c in chips()])


def halo_perm(x):
    n = NY * NZ * NC
    return lax.ppermute(x, "tok", [(i, (i + (1 if i % 2 else -1)) % n) for i in range(n)])


def mp_perm(x, d):
    return lax.ppermute(x, "mp", [(i, (i + d) % NX) for i in range(NX)])


def nt(a, b):
    return lax.dot_general(a, b, (((1,), (1,)), ((), ())), preferred_element_type=F32)


def nn(a, b):
    return lax.dot_general(a, b, (((1,), (0,)), ((), ())), preferred_element_type=F32)


def split_cache_kernel(head_ref, src, out):
    for b in range(2):
        rows = slice(b * BLOCK, (b + 1) * BLOCK)
        out[b, 0] = src[0, rows, 0, :]
        out[b, 1] = src[0, rows, 1, :].T


def split_cache(head, rows, holders=1):
    return pl.pallas_call(
        split_cache_kernel,
        grid_spec=pltpu.PrefetchScalarGridSpec(
            num_scalar_prefetch=1,
            grid=(8,),
            in_specs=[pl.BlockSpec((1, 256, 2, HD), lambda i, h: (i // 4, i % 4, 0, h[0]))],
            out_specs=pl.BlockSpec((2, 2, BLOCK, HD), lambda i, h: (i, 0, 0, 0)),
        ),
        out_shape=jax.ShapeDtypeStruct((16 * holders, 2, BLOCK, HD), BF16),
        compiler_params=params(),
        cost_estimate=BRIEF,
        name="split_cache",
    )(head, rows)


def normalise(tok_ref, gain_ref):
    x = tok_ref[...].astype(F32)
    inverse = lax.rsqrt(jnp.mean(x * x, axis=1, keepdims=True) + 1e-05)
    return (x * inverse * gain_ref[...]).astype(BF16)


def both_cores(core, put):
    for here in range(2):
        pl.when(core == here)(functools.partial(put, here))


def query_kernel(core_ref, tok_ref, gain_ref, wq, normed_ref, keep, send):
    normed = normalise(tok_ref, gain_ref)
    normed_ref[...] = normed
    q = nn(normed, wq[...]).astype(BF16)

    def put(here):
        for h in range(4):
            slot = (h - 2 * here) % 4
            out = keep if slot < 2 else send
            out[slot % 2] = q[:, h * HD : (h + 1) * HD]

    both_cores(core_ref[0], put)


def query(core, tokens, gain, wq):
    n, d = tokens.shape
    half = jax.ShapeDtypeStruct((2, n, HD), BF16)
    heads = pl.BlockSpec((2, 256, HD), lambda i, c: (0, i, 0))
    return pl.pallas_call(
        query_kernel,
        grid_spec=pltpu.PrefetchScalarGridSpec(
            num_scalar_prefetch=1,
            grid=(n // 256,),
            in_specs=[
                pl.BlockSpec((256, d), lambda i, c: (i, 0)),
                pl.BlockSpec((1, d), lambda i, c: (0, 0)),
                pl.BlockSpec((d, wq.shape[1]), lambda i, c: (0, 0), pipeline_mode=pl.Buffered(1)),
            ],
            out_specs=[pl.BlockSpec((256, d), lambda i, c: (i, 0)), heads, heads],
        ),
        out_shape=[jax.ShapeDtypeStruct((n, d), BF16), half, half],
        compiler_params=params(),
        cost_estimate=BRIEF,
        name="query",
    )(core, tokens, gain.reshape(1, d), wq)


def project_kernel(core_ref, normed_ref, wk, wv, k_all, v_all, swap, edge):
    step = pl.program_id(0)
    normed = normed_ref[...]
    k = nn(normed, wk[...]).astype(BF16)
    v = nn(normed, wv[...])

    def put(here):
        to_first = swap if here else edge
        to_last = edge if here else swap
        for h in range(4):
            slot = (h - 2 * here) % 4
            lanes = slice(h * HD, (h + 1) * HD)
            for b in range(2):
                rows = slice(b * BLOCK, (b + 1) * BLOCK)
                kb = k[rows, lanes]
                vb = v[rows, lanes].T.astype(BF16)
                k_all[slot, b] = kb
                v_all[slot, b] = vb
                out, when = (to_first, 0) if b == 0 else (to_last, pl.num_programs(0) - 1)

                @pl.when(step == when)
                def _():
                    out[slot * HD : (slot + 1) * HD, :] = kb
                    out[(4 + slot) * HD : (5 + slot) * HD, :] = vb

    both_cores(core_ref[0], put)


def project(core, normed, wk, wv):
    n, d = normed.shape
    weight = pl.BlockSpec((d, wk.shape[1]), lambda i, c: (0, 0), pipeline_mode=pl.Buffered(1))
    blocks = pl.BlockSpec((4, 2, BLOCK, HD), lambda i, c: (0, i, 0, 0))
    edge = pl.BlockSpec((1024, HD), lambda i, c: (0, 0))
    return pl.pallas_call(
        project_kernel,
        grid_spec=pltpu.PrefetchScalarGridSpec(
            num_scalar_prefetch=1,
            grid=(n // 256,),
            in_specs=[pl.BlockSpec((256, d), lambda i, c: (i, 0)), weight, weight],
            out_specs=[blocks, blocks, edge, edge],
        ),
        out_shape=[
            jax.ShapeDtypeStruct((4, 8, BLOCK, HD), BF16),
            jax.ShapeDtypeStruct((4, 8, HD, BLOCK), BF16),
            jax.ShapeDtypeStruct((1024, HD), BF16),
            jax.ShapeDtypeStruct((1024, HD), BF16),
        ],
        compiler_params=params(),
        cost_estimate=BRIEF,
        name="project",
    )(core, normed, wk, wv)


def near_kernel(core_ref, qa_ref, qb_ref, k_ref, v_ref, ka, va, kb, vb, o_ref, lse_ref):
    first = core_ref[0] == 0
    klo, khi = jnp.where(first, ka[0], kb[0]), jnp.where(first, kb[0], ka[0])
    vlo, vhi = jnp.where(first, va[0], vb[0]), jnp.where(first, vb[0], va[0])
    mine = pl.program_id(0) < 2
    for b in range(8):
        rows = slice(b * BLOCK, (b + 1) * BLOCK)
        q = jnp.where(mine, qa_ref[0, rows], qb_ref[0, rows])
        ks = [klo if b == 0 else k_ref[0, b - 1], k_ref[0, b], khi if b == 7 else k_ref[0, b + 1]]
        vs = [vlo if b == 0 else v_ref[0, b - 1], v_ref[0, b], vhi if b == 7 else v_ref[0, b + 1]]
        s = [nt(k, q) * SCALE for k in ks]
        m = jnp.max(jnp.maximum(jnp.maximum(s[0], s[1]), s[2]), axis=0, keepdims=True)
        p = [jnp.exp(x - m) for x in s]
        total = jnp.sum(p[0] + p[1] + p[2], axis=0, keepdims=True)
        acc = nn(vs[0], p[0].astype(BF16)) + nn(vs[1], p[1].astype(BF16)) + nn(vs[2], p[2].astype(BF16))
        o_ref[0, b] = acc / total
        lse_ref[0, b : b + 1, :] = m + jnp.log(total)


def near(core, keep, send, k, v, halo, swapped):
    blocks = pl.BlockSpec((1, 8, BLOCK, HD), lambda s, c: (s, 0, 0, 0))

    def edge(first):
        return pl.BlockSpec((1, BLOCK, HD), lambda s, c: (first + (s + 2) % 4, 0, 0))

    return pl.pallas_call(
        near_kernel,
        grid_spec=pltpu.PrefetchScalarGridSpec(
            num_scalar_prefetch=1,
            grid=(4,),
            in_specs=[pl.BlockSpec((1, 1024, HD), lambda s, c: (s % 2, 0, 0))] * 2
            + [blocks, blocks, edge(0), edge(4), edge(0), edge(4)],
            out_specs=[blocks, pl.BlockSpec((1, 8, HD), lambda s, c: (s, 0, 0))],
        ),
        out_shape=[jax.ShapeDtypeStruct((4, 8, HD, BLOCK), F32), jax.ShapeDtypeStruct((4, 8, BLOCK), F32)],
        compiler_params=params(),
        cost_estimate=BRIEF,
        name="near",
    )(core, keep, send, k, v, *[e.reshape(8, BLOCK, HD) for e in (halo, halo, swapped, swapped)])


GROUP = 4
UNITS = 96 + GROUP


def plan_kernel(cnt_ref, code_ref, unit_ref, first_ref, long_ref, size_ref, list_ref):
    def scan(i, carry):
        u, m = carry
        n = cnt_ref[i]
        first_ref[i] = u

        def named(carry):
            u, m = carry
            at = jnp.int32(0)
            for w in range(WMAX):
                code = code_ref[i * WMAX + w]
                list_ref[at] = code
                at = at + (code >= 0).astype(jnp.int32)

            def unit(k, u):
                both = (2 * k + 1 < n).astype(jnp.int32)
                unit_ref[u] = both * (1 << 22) + i * (1 << 16) + list_ref[2 * k] * 256 + list_ref[2 * k + both]
                return u + 1

            long_ref[m] = i
            return lax.fori_loop(0, lax.shift_right_logical(n + 1, 1), unit, u), m + (n > 2).astype(jnp.int32)

        return lax.cond(n > 0, named, lambda carry: carry, (u, m))

    units, longs = lax.fori_loop(0, 64, scan, (jnp.int32(0), jnp.int32(0)))
    for g in range(GROUP):
        unit_ref[units + g] = -1
    size_ref[0] = units
    size_ref[1] = longs


def plan(cnt, code):
    def out(n):
        return jax.ShapeDtypeStruct((n,), jnp.int32)

    return pl.pallas_call(
        plan_kernel,
        in_specs=[SMEM] * 2,
        out_specs=[SMEM] * 4,
        out_shape=[out(UNITS), out(64), out(64), out(2)],
        scratch_shapes=[pltpu.SMEM((2 * WMAX,), jnp.int32)],
        compiler_params=params(16),
        cost_estimate=BRIEF,
        name="plan",
    )(cnt, code)


def far_kernel(j, cnt_ref, unit_ref, first_ref, long_ref, size_ref, *rest):
    sources, qs, outs = rest[:5], rest[5:9], rest[9:13]
    kvbuf, qbuf, obuf, acc_ref, stat_ref, logs, kvsem, qsem, osem = rest[13:]
    units = size_ref[0]
    copies = [pltpu.make_async_copy(qs[r].at[:, j], qbuf.at[pl.ds(2 * r, 2)], qsem.at[r]) for r in range(4)]
    for k, (first, size) in enumerate(((0, 32), (32, 32), (64, 16), (80, 16), (96, 32))):
        copies.append(pltpu.make_async_copy(sources[k], kvbuf.at[pl.ds(first, size)], kvsem.at[k]))
    for copy in copies:
        copy.start()
    logs[...] = jnp.full((64, BLOCK), NEG, F32)
    for copy in copies:
        copy.wait()

    def store(i, m, total, acc):
        rows = pl.ds(pl.multiple_of(lax.bitwise_and(i, 15) * HD, HD), HD)
        obuf[lax.shift_right_logical(i, 4), rows, :] = (acc * (1.0 / total)).astype(BF16)
        logs[pl.ds(i, 1), :] = m + jnp.log(total)

    def group(g, _):
        for t in range(GROUP):
            u = g * GROUP + t
            unit = unit_ref[u]
            unit = jnp.where(unit >= 0, unit, unit_ref[g * GROUP])
            both = lax.shift_right_logical(unit, 22) == 1
            i = lax.bitwise_and(lax.shift_right_logical(unit, 16), 63)
            ea = lax.bitwise_and(lax.shift_right_logical(unit, 8), 127)
            eb = lax.bitwise_and(unit, 127)
            q = qbuf[lax.shift_right_logical(i, 3), lax.bitwise_and(i, 7)]
            s = nt(jnp.concatenate([kvbuf[ea, 0], kvbuf[eb, 0]], axis=0), q) * SCALE
            sa, sb = s[:BLOCK], jnp.where(both, s[BLOCK:], NEG)
            m = jnp.max(jnp.maximum(sa, sb), axis=0, keepdims=True)
            pa, pb = jnp.exp(sa - m), jnp.exp(sb - m)
            total = jnp.sum(pa + pb, axis=0, keepdims=True)
            p = jnp.concatenate([pa, pb], axis=0).astype(BF16)
            acc = nn(jnp.concatenate([kvbuf[ea, 1], kvbuf[eb, 1]], axis=1), p)
            stat_ref[u, 0:1, :] = m
            stat_ref[u, 1:2, :] = total
            acc_ref[u] = acc
            store(i, m, total, acc)
        return 0

    lax.fori_loop(0, lax.div(units + GROUP - 1, GROUP), group, 0)

    def join(k, _):
        i = long_ref[k]
        n = cnt_ref[i]
        u = first_ref[i]

        def more(k, carry):
            m, total, acc = carry
            mk, tk = stat_ref[k, 0:1, :], stat_ref[k, 1:2, :]
            top = jnp.maximum(m, mk)
            old, new = jnp.exp(m - top), jnp.exp(mk - top)
            return top, total * old + tk * new, acc * old + acc_ref[k] * new

        start = (stat_ref[u, 0:1, :], stat_ref[u, 1:2, :], acc_ref[u])
        store(i, *lax.fori_loop(u + 1, u + lax.shift_right_logical(n + 1, 1), more, start))
        return 0

    lax.fori_loop(0, size_ref[1], join, 0)
    for r in range(4):
        part = logs[r * 16 : (r + 1) * 16, :]
        for t in range(3):
            term = part.astype(BF16)
            obuf[r, 2048 + t * 16 : 2064 + t * 16, :] = term
            part = part - term.astype(F32)
        pltpu.make_async_copy(obuf.at[r], outs[r], osem.at[r]).start()
    for r in range(4):
        pltpu.make_async_copy(obuf.at[r], outs[r], osem.at[r]).wait()


def far(j, cnt, lists, sources, qs):
    out = jax.ShapeDtypeStruct((OROWS, BLOCK), BF16)
    return pl.pallas_call(
        functools.partial(far_kernel, j),
        in_specs=[SMEM] * 5 + [ANY] * 9,
        out_specs=[ANY] * 4,
        out_shape=[out] * 4,
        scratch_shapes=[
            pltpu.VMEM((128, 2, BLOCK, HD), BF16),
            pltpu.VMEM((8, 8, BLOCK, HD), BF16),
            pltpu.VMEM((4, OROWS, BLOCK), BF16),
            pltpu.VMEM((UNITS, HD, BLOCK), F32),
            pltpu.VMEM((UNITS, 8, BLOCK), F32),
            pltpu.VMEM((64, BLOCK), F32),
            pltpu.SemaphoreType.DMA((5,)),
            pltpu.SemaphoreType.DMA((4,)),
            pltpu.SemaphoreType.DMA((4,)),
        ],
        compiler_params=params(),
        cost_estimate=BRIEF,
        name="far",
    )(cnt, *lists, *sources, *qs)


def merge_kernel(a, b, c, d, keep, send):
    parts = (a, b, c, d)
    logs = [sum(p[2048 + t * 16 : 2064 + t * 16, :].astype(F32) for t in range(3)) for p in parts]
    peak = functools.reduce(jnp.maximum, logs)
    shares = [jnp.where(x > 0.5 * NEG, jnp.exp(x - peak), 0.0) for x in logs]
    total = sum(shares)
    joint = jnp.where(total > 0.0, peak + jnp.log(total), NEG)
    total = jnp.where(total > 0.0, total, 1.0)
    live = [x > 0.5 * NEG for x in logs]
    shares = [x / total for x in shares]
    for s, out in enumerate((keep, send)):
        for i in range(8):
            row = s * 8 + i
            rows = slice(row * HD, (row + 1) * HD)
            out[i * HD : (i + 1) * HD, :] = sum(
                jnp.where(on[row : row + 1, :], x[row : row + 1, :] * p[rows, :].astype(F32), 0.0)
                for on, x, p in zip(live, shares, parts)
            )
        out[1024:1032, :] = joint[s * 8 : (s + 1) * 8, :]


def merge(parts):
    out = jax.ShapeDtypeStruct((FROWS, BLOCK), F32)
    return pl.pallas_call(
        merge_kernel,
        out_shape=[out, out],
        compiler_params=params(),
        cost_estimate=BRIEF,
        name="merge",
    )(*parts)


def finish_kernel(near_a, lse_a, near_b, lse_b, far_a, far_b, out):
    for s, (o, log, f) in enumerate(((near_a, lse_a, far_a), (near_b, lse_b, far_b))):
        here, away = log[0], f[1024:1032, :]
        peak = jnp.maximum(here, away)
        wn, wf = jnp.exp(here - peak), jnp.exp(away - peak)
        total = wn + wf
        wn, wf = wn / total, wf / total
        for b in range(8):
            both = wn[b : b + 1, :] * o[0, b] + wf[b : b + 1, :] * f[b * HD : (b + 1) * HD, :]
            out[s, b * BLOCK : (b + 1) * BLOCK, :] = both.T.astype(BF16)


def finish(j, o, lse, far_keep, far_other):
    def at(slot):
        return [
            pl.BlockSpec((1, 8, HD, BLOCK), lambda i: (slot, 0, 0, 0)),
            pl.BlockSpec((1, 8, BLOCK), lambda i: (slot, 0, 0)),
        ]

    whole = pl.BlockSpec((FROWS, BLOCK), lambda i: (0, 0))
    return pl.pallas_call(
        finish_kernel,
        grid=(1,),
        in_specs=at(j) + at(2 + j) + [whole, whole],
        out_specs=pl.BlockSpec((2, 1024, HD), lambda i: (0, 0, 0)),
        out_shape=jax.ShapeDtypeStruct((2, 1024, HD), BF16),
        compiler_params=params(),
        cost_estimate=BRIEF,
        name="finish",
    )(o, lse, o, lse, far_keep, far_other)


def pick_kernel(place_ref, *rest):
    for j in range(2):
        for k in range(8):
            rest[16 + j][k * HD : (k + 1) * HD, :] = rest[j * 8 + k][...]


def pick(place, w_out):
    def weight(j, rel, s):
        return pl.BlockSpec((HD, 512), lambda i, p: ((p[1] + rel) % NX * 4 + (2 * p[0] + 2 * s + j) % 4, p[1]))

    out = jax.ShapeDtypeStruct((1024, 512), BF16)
    return pl.pallas_call(
        pick_kernel,
        grid_spec=pltpu.PrefetchScalarGridSpec(
            num_scalar_prefetch=1,
            grid=(1,),
            in_specs=[weight(j, rel, s) for j in range(2) for rel in range(4) for s in range(2)],
            out_specs=[pl.BlockSpec((1024, 512), lambda i, p: (0, 0))] * 2,
        ),
        out_shape=[out, out],
        compiler_params=params(),
        cost_estimate=BRIEF,
        name="pick",
    )(place, *[w_out] * 16)


def mix_kernel(place_ref, a0, a1, a2, a3, weight, carried, out):
    left = jnp.concatenate([a[s] for a in (a0, a1, a2, a3) for s in range(2)], axis=1)
    out[...] = (carried[...].astype(F32) + nn(left, weight[...])).astype(out.dtype)


def mix(place, parts, weight, carried, kind):
    column = 0 if carried.shape[1] == 512 else 1
    return pl.pallas_call(
        mix_kernel,
        grid_spec=pltpu.PrefetchScalarGridSpec(
            num_scalar_prefetch=1,
            grid=(4,),
            in_specs=[pl.BlockSpec((2, 256, HD), lambda i, p: (0, i, 0))] * 4
            + [pl.BlockSpec((1024, 512), lambda i, p: (0, 0))]
            + [pl.BlockSpec((256, 512), lambda i, p: (i, p[1] * column))],
            out_specs=pl.BlockSpec((256, 512), lambda i, p: (i, 0)),
        ),
        out_shape=jax.ShapeDtypeStruct((1024, 512), kind),
        compiler_params=params(),
        cost_estimate=BRIEF,
        name="mix",
    )(place, *parts, weight, carried)


def line_codes(wake_blocks, wake_frames, wake_counts, y, z, c):
    live = jnp.arange(WMAX, dtype=jnp.int32)[None, :] < wake_counts[:, None]
    word = jnp.where(live, wake_frames * 256 + wake_blocks, -1).reshape(NY, NZ, NC, 8, WMAX)
    by_y = lax.dynamic_index_in_dim(word, y, 0, keepdims=False)
    by_z = lax.dynamic_index_in_dim(word, z, 1, keepdims=False)
    here = jnp.where(c == 0, by_y, by_z)
    here = lax.dynamic_slice_in_dim(jnp.concatenate([here, here], axis=0), jnp.where(c == 0, z, y), 4, 0)
    here = lax.dynamic_slice_in_dim(jnp.concatenate([here, here], axis=1), c, 2, 1)
    word = here.reshape(64, WMAX)
    block, frame = word & 255, word >> 8
    hc, hz, hy = (block >> 3) & 1, (block >> 4) & 3, (block >> 6) & 3
    in_line = (word >= 0) & (jnp.where(c == 0, hz, hy) == jnp.where(c == 0, z, y))
    piece = (jnp.where(c == 0, hy, hz) - jnp.where(c == 0, y, z)) & 3
    code = piece * 32 + (hc ^ c) * 16 + (frame & 1) * 8 + (block & 7)
    code = jnp.where(in_line, code, -1)
    return code.reshape(512), jnp.sum(in_line.astype(jnp.int32), axis=1)


def on_device(tokens, norm_gain, w_query, w_key, w_value, w_out, kv_cache, wake_blocks, wake_frames, wake_counts):
    tok = lax.axis_index("tok").astype(jnp.int32)
    mp = lax.axis_index("mp").astype(jnp.int32)
    c, z, y = tok % NC, (tok // NC) % NZ, tok // (NC * NZ)
    core = c.reshape(1)
    place = jnp.stack([c, mp])

    def after(x, *deps):
        return lax.optimization_barrier((x, *deps))[0]

    got0 = core_swap(split_cache(2 - 2 * core, kv_cache))
    rows0 = lax.dynamic_update_slice(split_cache(2 * core, kv_cache, 2), got0, (16, 0, 0, 0))
    up0, down0 = rows_perm(rows0, 1), rows_perm(rows0, -1)

    normed, q_keep, q_send = query(core, tokens, after(norm_gain, rows0), w_query)
    mine = jnp.concatenate([q_keep, core_swap(q_send)], axis=0).reshape(2, 2, 8, BLOCK, HD)
    q1, q3, q2 = query_perm(mine, -1), query_perm(mine, 1), query_perm(mine, 2)
    core1 = after(core, mine)
    send1, keep1 = split_cache(3 - 2 * core1, kv_cache), split_cache(1 + 2 * core1, kv_cache, 2)
    code, cnt = line_codes(wake_blocks, wake_frames, wake_counts, y, z, c)
    tops, bottoms = up0[:16], down0[16:]
    held = (normed, keep1, send1, code, cnt, tops, bottoms)
    normed, keep1, send1, code, cnt, tops, bottoms = lax.optimization_barrier(held)
    k_all, v_all, swap, edge = project(core, normed, w_key, w_value)
    send1, swap, edge, q1, q2, q3 = lax.optimization_barrier((send1, swap, edge, q1, q2, q3))
    swapped, halo = core_swap(swap), halo_perm(edge)
    rows1 = lax.dynamic_update_slice(keep1, core_swap(send1), (16, 0, 0, 0))
    up20, down20 = rows_perm(tops, 1), rows_perm(bottoms, -1)
    lists = plan(cnt, code)
    near_o, near_lse = near(core, q_keep, q_send, k_all, v_all, halo, swapped)
    held = (rows1, up20, down20, near_o, near_lse, *lists)
    rows1, up20, down20, near_o, near_lse, *lists = lax.optimization_barrier(held)
    up1, down1 = rows_perm(rows1, 1), rows_perm(rows1, -1)
    qs = [mine, q1, q2, q3]

    def returned(parts):
        return [parts[0], query_perm(parts[1], 1), query_perm(parts[2], 2), query_perm(parts[3], -1)]

    def gather(heads):
        return [heads, mp_perm(heads, -1), mp_perm(heads, 2), mp_perm(heads, 1)]

    parts = far(0, cnt, lists, [rows0, down0, up20, down20, up0], qs)
    weights = pick(after(place, parts[0]), w_out)
    back = returned(parts)
    back[1], back[3], up1, down1 = lax.optimization_barrier((back[1], back[3], up1, down1))
    up21, down21 = rows_perm(up1[:16], 1), rows_perm(down1[16:], -1)
    back[0], near_lse, *weights = lax.optimization_barrier((back[0], near_lse, *weights))
    own, other = merge(back)
    heads = finish(0, near_o, near_lse, own, core_swap(other))
    gathered = gather(heads)

    parts = far(1, cnt, lists, [after(rows1, heads), down1, up21, down21, up1], qs)
    *parts, gathered[1], gathered[3] = lax.optimization_barrier((*parts, gathered[1], gathered[3]))
    back = returned(parts)
    back[0], gathered[2] = lax.optimization_barrier((back[0], gathered[2]))
    own, other = merge(back)
    heads = finish(1, near_o, near_lse, own, core_swap(other))
    gathered[0] = after(gathered[0], heads)
    acc = mix(place, gathered, weights[0], tokens, F32)
    return mix(place, gather(heads), weights[1], acc, BF16)


def solution(mesh):
    return jax.shard_map(
        on_device,
        mesh=mesh,
        in_specs=(
            P("tok", None),
            P(),
            P(None, "mp"),
            P(None, "mp"),
            P(None, "mp"),
            P(),
            P(None, "tok", None, "mp"),
            P(),
            P(),
            P(),
        ),
        out_specs=P("tok", "mp"),
        check_vma=False,
    )
```

```python
import functools
import math

import jax
import jax.numpy as jnp
from jax import lax
from jax.experimental import pallas as pl
from jax.experimental.pallas import tpu as pltpu
from jax.sharding import PartitionSpec as P

HD = 128
BLOCK = 128
WMAX = 8
NEG = -1e30
SCALE = 1.0 / math.sqrt(HD)
NY, NZ, NC, NX = 4, 4, 2, 4
F32, BF16 = jnp.float32, jnp.bfloat16
ANY = pl.BlockSpec(memory_space=pl.ANY)
SMEM = pl.BlockSpec(memory_space=pltpu.SMEM)
BRIEF = pl.CostEstimate(flops=1, transcendentals=0, bytes_accessed=1)
OROWS = 2048 + 48
FROWS = 1024 + 8


def params(mib=48):
    return pltpu.CompilerParams(vmem_limit_bytes=mib << 20)


def tok_of(y, z, c):
    return ((y % NY) * NZ + z % NZ) * NC + c % NC


def chips():
    return [(y, z, c) for y in range(NY) for z in range(NZ) for c in range(NC)]


def rows_perm(x, d):
    pairs = [(tok_of(y, z, c), tok_of(y + d, z, c) if c == 0 else tok_of(y, z + d, c)) for y, z, c in chips()]
    return lax.ppermute(x, "tok", pairs)


def query_perm(x, d):
    pairs = [(tok_of(y, z, c), tok_of(y, z + d, c) if c == 0 else tok_of(y + d, z, c)) for y, z, c in chips()]
    return lax.ppermute(x, "tok", pairs)


def core_swap(x):
    return lax.ppermute(x, "tok", [(tok_of(y, z, c), tok_of(y, z, 1 - c)) for y, z, c in chips()])


def halo_perm(x):
    n = NY * NZ * NC
    return lax.ppermute(x, "tok", [(i, (i + (1 if i % 2 else -1)) % n) for i in range(n)])


def mp_perm(x, d):
    return lax.ppermute(x, "mp", [(i, (i + d) % NX) for i in range(NX)])


def nt(a, b):
    return lax.dot_general(a, b, (((1,), (1,)), ((), ())), preferred_element_type=F32)


def nn(a, b):
    return lax.dot_general(a, b, (((1,), (0,)), ((), ())), preferred_element_type=F32)


def split_cache_kernel(head_ref, src, out):
    for b in range(2):
        rows = slice(b * BLOCK, (b + 1) * BLOCK)
        out[b, 0] = src[0, rows, 0, :]
        out[b, 1] = src[0, rows, 1, :].T


def split_cache(head, rows, holders=1):
    return pl.pallas_call(
        split_cache_kernel,
        grid_spec=pltpu.PrefetchScalarGridSpec(
            num_scalar_prefetch=1,
            grid=(8,),
            in_specs=[pl.BlockSpec((1, 256, 2, HD), lambda i, h: (i // 4, i % 4, 0, h[0]))],
            out_specs=pl.BlockSpec((2, 2, BLOCK, HD), lambda i, h: (i, 0, 0, 0)),
        ),
        out_shape=jax.ShapeDtypeStruct((16 * holders, 2, BLOCK, HD), BF16),
        compiler_params=params(),
        cost_estimate=BRIEF,
        name="split_cache",
    )(head, rows)


def normalise(tok_ref, gain_ref):
    x = tok_ref[...].astype(F32)
    inverse = lax.rsqrt(jnp.mean(x * x, axis=1, keepdims=True) + 1e-05)
    return (x * inverse * gain_ref[...]).astype(BF16)


def both_cores(core, put):
    for here in range(2):
        pl.when(core == here)(functools.partial(put, here))


def query_kernel(core_ref, tok_ref, gain_ref, wq, normed_ref, keep, send):
    normed = normalise(tok_ref, gain_ref)
    normed_ref[...] = normed
    q = nn(normed, wq[...]).astype(BF16)

    def put(here):
        for h in range(4):
            slot = (h - 2 * here) % 4
            out = keep if slot < 2 else send
            out[slot % 2] = q[:, h * HD : (h + 1) * HD]

    both_cores(core_ref[0], put)


def query(core, tokens, gain, wq):
    n, d = tokens.shape
    half = jax.ShapeDtypeStruct((2, n, HD), BF16)
    heads = pl.BlockSpec((2, 256, HD), lambda i, c: (0, i, 0))
    return pl.pallas_call(
        query_kernel,
        grid_spec=pltpu.PrefetchScalarGridSpec(
            num_scalar_prefetch=1,
            grid=(n // 256,),
            in_specs=[
                pl.BlockSpec((256, d), lambda i, c: (i, 0)),
                pl.BlockSpec((1, d), lambda i, c: (0, 0)),
                pl.BlockSpec((d, wq.shape[1]), lambda i, c: (0, 0), pipeline_mode=pl.Buffered(1)),
            ],
            out_specs=[pl.BlockSpec((256, d), lambda i, c: (i, 0)), heads, heads],
        ),
        out_shape=[jax.ShapeDtypeStruct((n, d), BF16), half, half],
        compiler_params=params(),
        cost_estimate=BRIEF,
        name="query",
    )(core, tokens, gain.reshape(1, d), wq)


def project_kernel(core_ref, normed_ref, wk, wv, k_all, v_all, swap, edge):
    step = pl.program_id(0)
    normed = normed_ref[...]
    k = nn(normed, wk[...]).astype(BF16)
    v = nn(normed, wv[...])

    def put(here):
        to_first = swap if here else edge
        to_last = edge if here else swap
        for h in range(4):
            slot = (h - 2 * here) % 4
            lanes = slice(h * HD, (h + 1) * HD)
            for b in range(2):
                rows = slice(b * BLOCK, (b + 1) * BLOCK)
                kb = k[rows, lanes]
                vb = v[rows, lanes].T.astype(BF16)
                k_all[slot, b] = kb
                v_all[slot, b] = vb
                out, when = (to_first, 0) if b == 0 else (to_last, pl.num_programs(0) - 1)

                @pl.when(step == when)
                def _():
                    out[slot * HD : (slot + 1) * HD, :] = kb
                    out[(4 + slot) * HD : (5 + slot) * HD, :] = vb

    both_cores(core_ref[0], put)


def project(core, normed, wk, wv):
    n, d = normed.shape
    weight = pl.BlockSpec((d, wk.shape[1]), lambda i, c: (0, 0), pipeline_mode=pl.Buffered(1))
    blocks = pl.BlockSpec((4, 2, BLOCK, HD), lambda i, c: (0, i, 0, 0))
    edge = pl.BlockSpec((1024, HD), lambda i, c: (0, 0))
    return pl.pallas_call(
        project_kernel,
        grid_spec=pltpu.PrefetchScalarGridSpec(
            num_scalar_prefetch=1,
            grid=(n // 256,),
            in_specs=[pl.BlockSpec((256, d), lambda i, c: (i, 0)), weight, weight],
            out_specs=[blocks, blocks, edge, edge],
        ),
        out_shape=[
            jax.ShapeDtypeStruct((4, 8, BLOCK, HD), BF16),
            jax.ShapeDtypeStruct((4, 8, HD, BLOCK), BF16),
            jax.ShapeDtypeStruct((1024, HD), BF16),
            jax.ShapeDtypeStruct((1024, HD), BF16),
        ],
        compiler_params=params(),
        cost_estimate=BRIEF,
        name="project",
    )(core, normed, wk, wv)


def near_kernel(core_ref, qa_ref, qb_ref, k_ref, v_ref, ka, va, kb, vb, o_ref, lse_ref):
    first = core_ref[0] == 0
    klo, khi = jnp.where(first, ka[0], kb[0]), jnp.where(first, kb[0], ka[0])
    vlo, vhi = jnp.where(first, va[0], vb[0]), jnp.where(first, vb[0], va[0])
    mine = pl.program_id(0) < 2
    for b in range(8):
        rows = slice(b * BLOCK, (b + 1) * BLOCK)
        q = jnp.where(mine, qa_ref[0, rows], qb_ref[0, rows])
        ks = [klo if b == 0 else k_ref[0, b - 1], k_ref[0, b], khi if b == 7 else k_ref[0, b + 1]]
        vs = [vlo if b == 0 else v_ref[0, b - 1], v_ref[0, b], vhi if b == 7 else v_ref[0, b + 1]]
        s = [nt(k, q) * SCALE for k in ks]
        m = jnp.max(jnp.maximum(jnp.maximum(s[0], s[1]), s[2]), axis=0, keepdims=True)
        p = [jnp.exp(x - m) for x in s]
        total = jnp.sum(p[0] + p[1] + p[2], axis=0, keepdims=True)
        acc = nn(vs[0], p[0].astype(BF16)) + nn(vs[1], p[1].astype(BF16)) + nn(vs[2], p[2].astype(BF16))
        o_ref[0, b] = acc / total
        lse_ref[0, b : b + 1, :] = m + jnp.log(total)


def near(core, keep, send, k, v, halo, swapped):
    blocks = pl.BlockSpec((1, 8, BLOCK, HD), lambda s, c: (s, 0, 0, 0))

    def edge(first):
        return pl.BlockSpec((1, BLOCK, HD), lambda s, c: (first + (s + 2) % 4, 0, 0))

    return pl.pallas_call(
        near_kernel,
        grid_spec=pltpu.PrefetchScalarGridSpec(
            num_scalar_prefetch=1,
            grid=(4,),
            in_specs=[pl.BlockSpec((1, 1024, HD), lambda s, c: (s % 2, 0, 0))] * 2
            + [blocks, blocks, edge(0), edge(4), edge(0), edge(4)],
            out_specs=[blocks, pl.BlockSpec((1, 8, HD), lambda s, c: (s, 0, 0))],
        ),
        out_shape=[jax.ShapeDtypeStruct((4, 8, HD, BLOCK), F32), jax.ShapeDtypeStruct((4, 8, BLOCK), F32)],
        compiler_params=params(),
        cost_estimate=BRIEF,
        name="near",
    )(core, keep, send, k, v, *[e.reshape(8, BLOCK, HD) for e in (halo, halo, swapped, swapped)])


GROUP = 4
UNITS = 96 + GROUP


def plan_kernel(cnt_ref, code_ref, unit_ref, first_ref, long_ref, size_ref, list_ref):
    def scan(i, carry):
        u, m = carry
        n = cnt_ref[i]
        first_ref[i] = u

        def named(carry):
            u, m = carry
            at = jnp.int32(0)
            for w in range(WMAX):
                code = code_ref[i * WMAX + w]
                list_ref[at] = code
                at = at + (code >= 0).astype(jnp.int32)

            def unit(k, u):
                both = (2 * k + 1 < n).astype(jnp.int32)
                unit_ref[u] = both * (1 << 22) + i * (1 << 16) + list_ref[2 * k] * 256 + list_ref[2 * k + both]
                return u + 1

            long_ref[m] = i
            return lax.fori_loop(0, lax.shift_right_logical(n + 1, 1), unit, u), m + (n > 2).astype(jnp.int32)

        return lax.cond(n > 0, named, lambda carry: carry, (u, m))

    units, longs = lax.fori_loop(0, 64, scan, (jnp.int32(0), jnp.int32(0)))
    for g in range(GROUP):
        unit_ref[units + g] = -1
    size_ref[0] = units
    size_ref[1] = longs


def plan(cnt, code):
    def out(n):
        return jax.ShapeDtypeStruct((n,), jnp.int32)

    return pl.pallas_call(
        plan_kernel,
        in_specs=[SMEM] * 2,
        out_specs=[SMEM] * 4,
        out_shape=[out(UNITS), out(64), out(64), out(2)],
        scratch_shapes=[pltpu.SMEM((2 * WMAX,), jnp.int32)],
        compiler_params=params(16),
        cost_estimate=BRIEF,
        name="plan",
    )(cnt, code)


def far_kernel(j, cnt_ref, unit_ref, first_ref, long_ref, size_ref, *rest):
    sources, qs, outs = rest[:5], rest[5:9], rest[9:13]
    kvbuf, qbuf, obuf, acc_ref, stat_ref, logs, kvsem, qsem, osem = rest[13:]
    units = size_ref[0]
    copies = [pltpu.make_async_copy(qs[r].at[:, j], qbuf.at[pl.ds(2 * r, 2)], qsem.at[r]) for r in range(4)]
    for k, (first, size) in enumerate(((0, 32), (32, 32), (64, 16), (80, 16), (96, 32))):
        copies.append(pltpu.make_async_copy(sources[k], kvbuf.at[pl.ds(first, size)], kvsem.at[k]))
    for copy in copies:
        copy.start()
    logs[...] = jnp.full((64, BLOCK), NEG, F32)
    for copy in copies:
        copy.wait()

    def store(i, m, total, acc):
        rows = pl.ds(pl.multiple_of(lax.bitwise_and(i, 15) * HD, HD), HD)
        obuf[lax.shift_right_logical(i, 4), rows, :] = (acc * (1.0 / total)).astype(BF16)
        logs[pl.ds(i, 1), :] = m + jnp.log(total)

    def group(g, _):
        for t in range(GROUP):
            u = g * GROUP + t
            unit = unit_ref[u]
            unit = jnp.where(unit >= 0, unit, unit_ref[g * GROUP])
            both = lax.shift_right_logical(unit, 22) == 1
            i = lax.bitwise_and(lax.shift_right_logical(unit, 16), 63)
            ea = lax.bitwise_and(lax.shift_right_logical(unit, 8), 127)
            eb = lax.bitwise_and(unit, 127)
            q = qbuf[lax.shift_right_logical(i, 3), lax.bitwise_and(i, 7)]
            s = nt(jnp.concatenate([kvbuf[ea, 0], kvbuf[eb, 0]], axis=0), q) * SCALE
            sa, sb = s[:BLOCK], jnp.where(both, s[BLOCK:], NEG)
            m = jnp.max(jnp.maximum(sa, sb), axis=0, keepdims=True)
            pa, pb = jnp.exp(sa - m), jnp.exp(sb - m)
            total = jnp.sum(pa + pb, axis=0, keepdims=True)
            p = jnp.concatenate([pa, pb], axis=0).astype(BF16)
            acc = nn(jnp.concatenate([kvbuf[ea, 1], kvbuf[eb, 1]], axis=1), p)
            stat_ref[u, 0:1, :] = m
            stat_ref[u, 1:2, :] = total
            acc_ref[u] = acc
            store(i, m, total, acc)
        return 0

    lax.fori_loop(0, lax.div(units + GROUP - 1, GROUP), group, 0)

    def join(k, _):
        i = long_ref[k]
        n = cnt_ref[i]
        u = first_ref[i]

        def more(k, carry):
            m, total, acc = carry
            mk, tk = stat_ref[k, 0:1, :], stat_ref[k, 1:2, :]
            top = jnp.maximum(m, mk)
            old, new = jnp.exp(m - top), jnp.exp(mk - top)
            return top, total * old + tk * new, acc * old + acc_ref[k] * new

        start = (stat_ref[u, 0:1, :], stat_ref[u, 1:2, :], acc_ref[u])
        store(i, *lax.fori_loop(u + 1, u + lax.shift_right_logical(n + 1, 1), more, start))
        return 0

    lax.fori_loop(0, size_ref[1], join, 0)
    for r in range(4):
        part = logs[r * 16 : (r + 1) * 16, :]
        for t in range(3):
            term = part.astype(BF16)
            obuf[r, 2048 + t * 16 : 2064 + t * 16, :] = term
            part = part - term.astype(F32)
        pltpu.make_async_copy(obuf.at[r], outs[r], osem.at[r]).start()
    for r in range(4):
        pltpu.make_async_copy(obuf.at[r], outs[r], osem.at[r]).wait()


def far(j, cnt, lists, sources, qs):
    out = jax.ShapeDtypeStruct((OROWS, BLOCK), BF16)
    return pl.pallas_call(
        functools.partial(far_kernel, j),
        in_specs=[SMEM] * 5 + [ANY] * 9,
        out_specs=[ANY] * 4,
        out_shape=[out] * 4,
        scratch_shapes=[
            pltpu.VMEM((128, 2, BLOCK, HD), BF16),
            pltpu.VMEM((8, 8, BLOCK, HD), BF16),
            pltpu.VMEM((4, OROWS, BLOCK), BF16),
            pltpu.VMEM((UNITS, HD, BLOCK), F32),
            pltpu.VMEM((UNITS, 8, BLOCK), F32),
            pltpu.VMEM((64, BLOCK), F32),
            pltpu.SemaphoreType.DMA((5,)),
            pltpu.SemaphoreType.DMA((4,)),
            pltpu.SemaphoreType.DMA((4,)),
        ],
        compiler_params=params(),
        cost_estimate=BRIEF,
        name="far",
    )(cnt, *lists, *sources, *qs)


def merge_kernel(a, b, c, d, keep, send):
    parts = (a, b, c, d)
    logs = [sum(p[2048 + t * 16 : 2064 + t * 16, :].astype(F32) for t in range(3)) for p in parts]
    peak = functools.reduce(jnp.maximum, logs)
    shares = [jnp.where(x > 0.5 * NEG, jnp.exp(x - peak), 0.0) for x in logs]
    total = sum(shares)
    joint = jnp.where(total > 0.0, peak + jnp.log(total), NEG)
    total = jnp.where(total > 0.0, total, 1.0)
    live = [x > 0.5 * NEG for x in logs]
    shares = [x / total for x in shares]
    for s, out in enumerate((keep, send)):
        for i in range(8):
            row = s * 8 + i
            rows = slice(row * HD, (row + 1) * HD)
            out[i * HD : (i + 1) * HD, :] = sum(
                jnp.where(on[row : row + 1, :], x[row : row + 1, :] * p[rows, :].astype(F32), 0.0)
                for on, x, p in zip(live, shares, parts)
            )
        out[1024:1032, :] = joint[s * 8 : (s + 1) * 8, :]


def merge(parts):
    out = jax.ShapeDtypeStruct((FROWS, BLOCK), F32)
    return pl.pallas_call(
        merge_kernel,
        out_shape=[out, out],
        compiler_params=params(),
        cost_estimate=BRIEF,
        name="merge",
    )(*parts)


def finish_kernel(near_a, lse_a, near_b, lse_b, far_a, far_b, out):
    for s, (o, log, f) in enumerate(((near_a, lse_a, far_a), (near_b, lse_b, far_b))):
        here, away = log[0], f[1024:1032, :]
        peak = jnp.maximum(here, away)
        wn, wf = jnp.exp(here - peak), jnp.exp(away - peak)
        total = wn + wf
        wn, wf = wn / total, wf / total
        for b in range(8):
            both = wn[b : b + 1, :] * o[0, b] + wf[b : b + 1, :] * f[b * HD : (b + 1) * HD, :]
            out[s, b * BLOCK : (b + 1) * BLOCK, :] = both.T.astype(BF16)


def finish(j, o, lse, far_keep, far_other):
    def at(slot):
        return [
            pl.BlockSpec((1, 8, HD, BLOCK), lambda i: (slot, 0, 0, 0)),
            pl.BlockSpec((1, 8, BLOCK), lambda i: (slot, 0, 0)),
        ]

    whole = pl.BlockSpec((FROWS, BLOCK), lambda i: (0, 0))
    return pl.pallas_call(
        finish_kernel,
        grid=(1,),
        in_specs=at(j) + at(2 + j) + [whole, whole],
        out_specs=pl.BlockSpec((2, 1024, HD), lambda i: (0, 0, 0)),
        out_shape=jax.ShapeDtypeStruct((2, 1024, HD), BF16),
        compiler_params=params(),
        cost_estimate=BRIEF,
        name="finish",
    )(o, lse, o, lse, far_keep, far_other)


def pick_kernel(place_ref, *rest):
    for j in range(2):
        for k in range(8):
            rest[16 + j][k * HD : (k + 1) * HD, :] = rest[j * 8 + k][...]


def pick(place, w_out):
    def weight(j, rel, s):
        return pl.BlockSpec((HD, 512), lambda i, p: ((p[1] + rel) % NX * 4 + (2 * p[0] + 2 * s + j) % 4, p[1]))

    out = jax.ShapeDtypeStruct((1024, 512), BF16)
    return pl.pallas_call(
        pick_kernel,
        grid_spec=pltpu.PrefetchScalarGridSpec(
            num_scalar_prefetch=1,
            grid=(1,),
            in_specs=[weight(j, rel, s) for j in range(2) for rel in range(4) for s in range(2)],
            out_specs=[pl.BlockSpec((1024, 512), lambda i, p: (0, 0))] * 2,
        ),
        out_shape=[out, out],
        compiler_params=params(),
        cost_estimate=BRIEF,
        name="pick",
    )(place, *[w_out] * 16)


def mix_kernel(place_ref, a0, a1, a2, a3, weight, carried, out):
    left = jnp.concatenate([a[s] for a in (a0, a1, a2, a3) for s in range(2)], axis=1)
    out[...] = (carried[...].astype(F32) + nn(left, weight[...])).astype(out.dtype)


def mix(place, parts, weight, carried, kind):
    column = 0 if carried.shape[1] == 512 else 1
    return pl.pallas_call(
        mix_kernel,
        grid_spec=pltpu.PrefetchScalarGridSpec(
            num_scalar_prefetch=1,
            grid=(4,),
            in_specs=[pl.BlockSpec((2, 256, HD), lambda i, p: (0, i, 0))] * 4
            + [pl.BlockSpec((1024, 512), lambda i, p: (0, 0))]
            + [pl.BlockSpec((256, 512), lambda i, p: (i, p[1] * column))],
            out_specs=pl.BlockSpec((256, 512), lambda i, p: (i, 0)),
        ),
        out_shape=jax.ShapeDtypeStruct((1024, 512), kind),
        compiler_params=params(),
        cost_estimate=BRIEF,
        name="mix",
    )(place, *parts, weight, carried)


def line_codes(wake_blocks, wake_frames, wake_counts, y, z, c):
    live = jnp.arange(WMAX, dtype=jnp.int32)[None, :] < wake_counts[:, None]
    word = jnp.where(live, wake_frames * 256 + wake_blocks, -1).reshape(NY, NZ, NC, 8, WMAX)
    by_y = lax.dynamic_index_in_dim(word, y, 0, keepdims=False)
    by_z = lax.dynamic_index_in_dim(word, z, 1, keepdims=False)
    here = jnp.where(c == 0, by_y, by_z)
    here = lax.dynamic_slice_in_dim(jnp.concatenate([here, here], axis=0), jnp.where(c == 0, z, y), 4, 0)
    here = lax.dynamic_slice_in_dim(jnp.concatenate([here, here], axis=1), c, 2, 1)
    word = here.reshape(64, WMAX)
    block, frame = word & 255, word >> 8
    hc, hz, hy = (block >> 3) & 1, (block >> 4) & 3, (block >> 6) & 3
    in_line = (word >= 0) & (jnp.where(c == 0, hz, hy) == jnp.where(c == 0, z, y))
    piece = (jnp.where(c == 0, hy, hz) - jnp.where(c == 0, y, z)) & 3
    code = piece * 32 + (hc ^ c) * 16 + (frame & 1) * 8 + (block & 7)
    code = jnp.where(in_line, code, -1)
    return code.reshape(512), jnp.sum(in_line.astype(jnp.int32), axis=1)


def on_device(tokens, norm_gain, w_query, w_key, w_value, w_out, kv_cache, wake_blocks, wake_frames, wake_counts):
    tok = lax.axis_index("tok").astype(jnp.int32)
    mp = lax.axis_index("mp").astype(jnp.int32)
    c, z, y = tok % NC, (tok // NC) % NZ, tok // (NC * NZ)
    core = c.reshape(1)
    place = jnp.stack([c, mp])

    def after(x, *deps):
        return lax.optimization_barrier((x, *deps))[0]

    got0 = core_swap(split_cache(2 - 2 * core, kv_cache))
    rows0 = lax.dynamic_update_slice(split_cache(2 * core, kv_cache, 2), got0, (16, 0, 0, 0))
    up0, down0 = rows_perm(rows0, 1), rows_perm(rows0, -1)

    normed, q_keep, q_send = query(core, tokens, after(norm_gain, rows0), w_query)
    mine = jnp.concatenate([q_keep, core_swap(q_send)], axis=0).reshape(2, 2, 8, BLOCK, HD)
    q1, q3, q2 = query_perm(mine, -1), query_perm(mine, 1), query_perm(mine, 2)
    core1 = after(core, mine)
    send1, keep1 = split_cache(3 - 2 * core1, kv_cache), split_cache(1 + 2 * core1, kv_cache, 2)
    code, cnt = line_codes(wake_blocks, wake_frames, wake_counts, y, z, c)
    tops, bottoms = up0[:16], down0[16:]
    normed, keep1, send1, code, cnt = lax.optimization_barrier((normed, keep1, send1, code, cnt))
    k_all, v_all, swap, edge = project(core, normed, w_key, w_value)
    held = (send1, swap, edge, q1, q2, q3, tops, bottoms)
    send1, swap, edge, q1, q2, q3, tops, bottoms = lax.optimization_barrier(held)
    swapped, halo = core_swap(swap), halo_perm(edge)
    rows1 = lax.dynamic_update_slice(keep1, core_swap(send1), (16, 0, 0, 0))
    up20, down20 = rows_perm(tops, 1), rows_perm(bottoms, -1)
    lists = plan(cnt, code)
    held = (rows1, up20, down20, halo, swapped, *lists)
    rows1, up20, down20, halo, swapped, *lists = lax.optimization_barrier(held)
    near_o, near_lse = near(core, q_keep, q_send, k_all, v_all, halo, swapped)
    up1, down1 = rows_perm(rows1, 1), rows_perm(rows1, -1)
    qs = [mine, q1, q2, q3]

    def returned(parts):
        return [parts[0], query_perm(parts[1], 1), query_perm(parts[2], 2), query_perm(parts[3], -1)]

    def gather(heads):
        return [heads, mp_perm(heads, -1), mp_perm(heads, 2), mp_perm(heads, 1)]

    parts = far(0, cnt, lists, [after(rows0, near_o), down0, up20, down20, up0], qs)
    weights = pick(after(place, parts[0]), w_out)
    back = returned(parts)
    back[1], back[3], up1, down1 = lax.optimization_barrier((back[1], back[3], up1, down1))
    up21, down21 = rows_perm(up1[:16], 1), rows_perm(down1[16:], -1)
    back[0], near_lse, *weights = lax.optimization_barrier((back[0], near_lse, *weights))
    own, other = merge(back)
    heads = finish(0, near_o, near_lse, own, core_swap(other))
    gathered = gather(heads)

    parts = far(1, cnt, lists, [after(rows1, heads), down1, up21, down21, up1], qs)
    *parts, gathered[1], gathered[3] = lax.optimization_barrier((*parts, gathered[1], gathered[3]))
    back = returned(parts)
    back[0], gathered[2] = lax.optimization_barrier((back[0], gathered[2]))
    own, other = merge(back)
    heads = finish(1, near_o, near_lse, own, core_swap(other))
    gathered[0] = after(gathered[0], heads)
    acc = mix(place, gathered, weights[0], tokens, F32)
    return mix(place, gather(heads), weights[1], acc, BF16)


def solution(mesh):
    return jax.shard_map(
        on_device,
        mesh=mesh,
        in_specs=(
            P("tok", None),
            P(),
            P(None, "mp"),
            P(None, "mp"),
            P(None, "mp"),
            P(),
            P(None, "tok", None, "mp"),
            P(),
            P(),
            P(),
        ),
        out_specs=P("tok", "mp"),
        check_vma=False,
    )
```

```python
import functools
import math

import jax
import jax.numpy as jnp
from jax import lax
from jax.experimental import pallas as pl
from jax.experimental.pallas import tpu as pltpu
from jax.sharding import PartitionSpec as P

HD = 128
BLOCK = 128
WMAX = 8
NEG = -1e30
SCALE = 1.0 / math.sqrt(HD)
NY, NZ, NC, NX = 4, 4, 2, 4
F32, BF16 = jnp.float32, jnp.bfloat16
ANY = pl.BlockSpec(memory_space=pl.ANY)
SMEM = pl.BlockSpec(memory_space=pltpu.SMEM)
BRIEF = pl.CostEstimate(flops=1, transcendentals=0, bytes_accessed=1)
OROWS = 2048 + 48
FROWS = 1024 + 8


def params(mib=48):
    return pltpu.CompilerParams(vmem_limit_bytes=mib << 20)


def tok_of(y, z, c):
    return ((y % NY) * NZ + z % NZ) * NC + c % NC


def chips():
    return [(y, z, c) for y in range(NY) for z in range(NZ) for c in range(NC)]


def rows_perm(x, d):
    pairs = [(tok_of(y, z, c), tok_of(y + d, z, c) if c == 0 else tok_of(y, z + d, c)) for y, z, c in chips()]
    return lax.ppermute(x, "tok", pairs)


def query_perm(x, d):
    pairs = [(tok_of(y, z, c), tok_of(y, z + d, c) if c == 0 else tok_of(y + d, z, c)) for y, z, c in chips()]
    return lax.ppermute(x, "tok", pairs)


def core_swap(x):
    return lax.ppermute(x, "tok", [(tok_of(y, z, c), tok_of(y, z, 1 - c)) for y, z, c in chips()])


def halo_perm(x):
    n = NY * NZ * NC
    return lax.ppermute(x, "tok", [(i, (i + (1 if i % 2 else -1)) % n) for i in range(n)])


def mp_perm(x, d):
    return lax.ppermute(x, "mp", [(i, (i + d) % NX) for i in range(NX)])


def nt(a, b):
    return lax.dot_general(a, b, (((1,), (1,)), ((), ())), preferred_element_type=F32)


def nn(a, b):
    return lax.dot_general(a, b, (((1,), (0,)), ((), ())), preferred_element_type=F32)


def split_cache_kernel(head_ref, src, out):
    for b in range(2):
        rows = slice(b * BLOCK, (b + 1) * BLOCK)
        out[b, 0] = src[0, rows, 0, :]
        out[b, 1] = src[0, rows, 1, :].T


def split_cache(head, rows, holders=1):
    return pl.pallas_call(
        split_cache_kernel,
        grid_spec=pltpu.PrefetchScalarGridSpec(
            num_scalar_prefetch=1,
            grid=(8,),
            in_specs=[pl.BlockSpec((1, 256, 2, HD), lambda i, h: (i // 4, i % 4, 0, h[0]))],
            out_specs=pl.BlockSpec((2, 2, BLOCK, HD), lambda i, h: (i, 0, 0, 0)),
        ),
        out_shape=jax.ShapeDtypeStruct((16 * holders, 2, BLOCK, HD), BF16),
        compiler_params=params(),
        cost_estimate=BRIEF,
        name="split_cache",
    )(head, rows)


def normalise(tok_ref, gain_ref):
    x = tok_ref[...].astype(F32)
    inverse = lax.rsqrt(jnp.mean(x * x, axis=1, keepdims=True) + 1e-05)
    return (x * inverse * gain_ref[...]).astype(BF16)


def both_cores(core, put):
    for here in range(2):
        pl.when(core == here)(functools.partial(put, here))


def query_kernel(core_ref, tok_ref, gain_ref, wq, normed_ref, keep, send):
    normed = normalise(tok_ref, gain_ref)
    normed_ref[...] = normed
    q = nn(normed, wq[...]).astype(BF16)

    def put(here):
        for h in range(4):
            slot = (h - 2 * here) % 4
            out = keep if slot < 2 else send
            out[slot % 2] = q[:, h * HD : (h + 1) * HD]

    both_cores(core_ref[0], put)


def query(core, tokens, gain, wq):
    n, d = tokens.shape
    half = jax.ShapeDtypeStruct((2, n, HD), BF16)
    heads = pl.BlockSpec((2, 256, HD), lambda i, c: (0, i, 0))
    return pl.pallas_call(
        query_kernel,
        grid_spec=pltpu.PrefetchScalarGridSpec(
            num_scalar_prefetch=1,
            grid=(n // 256,),
            in_specs=[
                pl.BlockSpec((256, d), lambda i, c: (i, 0)),
                pl.BlockSpec((1, d), lambda i, c: (0, 0)),
                pl.BlockSpec((d, wq.shape[1]), lambda i, c: (0, 0), pipeline_mode=pl.Buffered(1)),
            ],
            out_specs=[pl.BlockSpec((256, d), lambda i, c: (i, 0)), heads, heads],
        ),
        out_shape=[jax.ShapeDtypeStruct((n, d), BF16), half, half],
        compiler_params=params(),
        cost_estimate=BRIEF,
        name="query",
    )(core, tokens, gain.reshape(1, d), wq)


def project_kernel(core_ref, normed_ref, wk, wv, k_all, v_all, swap, edge):
    step = pl.program_id(0)
    normed = normed_ref[...]
    k = nn(normed, wk[...]).astype(BF16)
    v = nn(normed, wv[...])

    def put(here):
        to_first = swap if here else edge
        to_last = edge if here else swap
        for h in range(4):
            slot = (h - 2 * here) % 4
            lanes = slice(h * HD, (h + 1) * HD)
            for b in range(2):
                rows = slice(b * BLOCK, (b + 1) * BLOCK)
                kb = k[rows, lanes]
                vb = v[rows, lanes].T.astype(BF16)
                k_all[slot, b] = kb
                v_all[slot, b] = vb
                out, when = (to_first, 0) if b == 0 else (to_last, pl.num_programs(0) - 1)

                @pl.when(step == when)
                def _():
                    out[slot * HD : (slot + 1) * HD, :] = kb
                    out[(4 + slot) * HD : (5 + slot) * HD, :] = vb

    both_cores(core_ref[0], put)


def project(core, normed, wk, wv):
    n, d = normed.shape
    weight = pl.BlockSpec((d, wk.shape[1]), lambda i, c: (0, 0), pipeline_mode=pl.Buffered(1))
    blocks = pl.BlockSpec((4, 2, BLOCK, HD), lambda i, c: (0, i, 0, 0))
    edge = pl.BlockSpec((1024, HD), lambda i, c: (0, 0))
    return pl.pallas_call(
        project_kernel,
        grid_spec=pltpu.PrefetchScalarGridSpec(
            num_scalar_prefetch=1,
            grid=(n // 256,),
            in_specs=[pl.BlockSpec((256, d), lambda i, c: (i, 0)), weight, weight],
            out_specs=[blocks, blocks, edge, edge],
        ),
        out_shape=[
            jax.ShapeDtypeStruct((4, 8, BLOCK, HD), BF16),
            jax.ShapeDtypeStruct((4, 8, HD, BLOCK), BF16),
            jax.ShapeDtypeStruct((1024, HD), BF16),
            jax.ShapeDtypeStruct((1024, HD), BF16),
        ],
        compiler_params=params(),
        cost_estimate=BRIEF,
        name="project",
    )(core, normed, wk, wv)


def near_kernel(core_ref, qa_ref, qb_ref, k_ref, v_ref, ka, va, kb, vb, o_ref, lse_ref):
    first = core_ref[0] == 0
    klo, khi = jnp.where(first, ka[0], kb[0]), jnp.where(first, kb[0], ka[0])
    vlo, vhi = jnp.where(first, va[0], vb[0]), jnp.where(first, vb[0], va[0])
    mine = pl.program_id(0) < 2
    for b in range(8):
        rows = slice(b * BLOCK, (b + 1) * BLOCK)
        q = jnp.where(mine, qa_ref[0, rows], qb_ref[0, rows])
        ks = [klo if b == 0 else k_ref[0, b - 1], k_ref[0, b], khi if b == 7 else k_ref[0, b + 1]]
        vs = [vlo if b == 0 else v_ref[0, b - 1], v_ref[0, b], vhi if b == 7 else v_ref[0, b + 1]]
        s = [nt(k, q) * SCALE for k in ks]
        m = jnp.max(jnp.maximum(jnp.maximum(s[0], s[1]), s[2]), axis=0, keepdims=True)
        p = [jnp.exp(x - m) for x in s]
        total = jnp.sum(p[0] + p[1] + p[2], axis=0, keepdims=True)
        acc = nn(vs[0], p[0].astype(BF16)) + nn(vs[1], p[1].astype(BF16)) + nn(vs[2], p[2].astype(BF16))
        o_ref[0, b] = acc / total
        lse_ref[0, b : b + 1, :] = m + jnp.log(total)


def near(core, keep, send, k, v, halo, swapped):
    blocks = pl.BlockSpec((1, 8, BLOCK, HD), lambda s, c: (s, 0, 0, 0))

    def edge(first):
        return pl.BlockSpec((1, BLOCK, HD), lambda s, c: (first + (s + 2) % 4, 0, 0))

    return pl.pallas_call(
        near_kernel,
        grid_spec=pltpu.PrefetchScalarGridSpec(
            num_scalar_prefetch=1,
            grid=(4,),
            in_specs=[pl.BlockSpec((1, 1024, HD), lambda s, c: (s % 2, 0, 0))] * 2
            + [blocks, blocks, edge(0), edge(4), edge(0), edge(4)],
            out_specs=[blocks, pl.BlockSpec((1, 8, HD), lambda s, c: (s, 0, 0))],
        ),
        out_shape=[jax.ShapeDtypeStruct((4, 8, HD, BLOCK), F32), jax.ShapeDtypeStruct((4, 8, BLOCK), F32)],
        compiler_params=params(),
        cost_estimate=BRIEF,
        name="near",
    )(core, keep, send, k, v, *[e.reshape(8, BLOCK, HD) for e in (halo, halo, swapped, swapped)])


GROUP = 4
UNITS = 96 + GROUP


def plan_kernel(cnt_ref, code_ref, unit_ref, first_ref, long_ref, size_ref, list_ref):
    def scan(i, carry):
        u, m = carry
        n = cnt_ref[i]
        first_ref[i] = u

        def named(carry):
            u, m = carry
            at = jnp.int32(0)
            for w in range(WMAX):
                code = code_ref[i * WMAX + w]
                list_ref[at] = code
                at = at + (code >= 0).astype(jnp.int32)

            def unit(k, u):
                both = (2 * k + 1 < n).astype(jnp.int32)
                unit_ref[u] = both * (1 << 22) + i * (1 << 16) + list_ref[2 * k] * 256 + list_ref[2 * k + both]
                return u + 1

            long_ref[m] = i
            return lax.fori_loop(0, lax.shift_right_logical(n + 1, 1), unit, u), m + (n > 2).astype(jnp.int32)

        return lax.cond(n > 0, named, lambda carry: carry, (u, m))

    units, longs = lax.fori_loop(0, 64, scan, (jnp.int32(0), jnp.int32(0)))
    for g in range(GROUP):
        unit_ref[units + g] = -1
    size_ref[0] = units
    size_ref[1] = longs


def plan(cnt, code):
    def out(n):
        return jax.ShapeDtypeStruct((n,), jnp.int32)

    return pl.pallas_call(
        plan_kernel,
        in_specs=[SMEM] * 2,
        out_specs=[SMEM] * 4,
        out_shape=[out(UNITS), out(64), out(64), out(2)],
        scratch_shapes=[pltpu.SMEM((2 * WMAX,), jnp.int32)],
        compiler_params=params(16),
        cost_estimate=BRIEF,
        name="plan",
    )(cnt, code)


def far_kernel(j, cnt_ref, unit_ref, first_ref, long_ref, size_ref, *rest):
    sources, qs, outs = rest[:5], rest[5:9], rest[9:13]
    kvbuf, qbuf, obuf, acc_ref, stat_ref, logs, kvsem, qsem, osem = rest[13:]
    units = size_ref[0]
    copies = [pltpu.make_async_copy(qs[r].at[:, j], qbuf.at[pl.ds(2 * r, 2)], qsem.at[r]) for r in range(4)]
    for k, (first, size) in enumerate(((0, 32), (32, 32), (64, 16), (80, 16), (96, 32))):
        copies.append(pltpu.make_async_copy(sources[k], kvbuf.at[pl.ds(first, size)], kvsem.at[k]))
    for copy in copies:
        copy.start()
    logs[...] = jnp.full((64, BLOCK), NEG, F32)
    for copy in copies:
        copy.wait()

    def store(i, m, total, acc):
        rows = pl.ds(pl.multiple_of(lax.bitwise_and(i, 15) * HD, HD), HD)
        obuf[lax.shift_right_logical(i, 4), rows, :] = (acc * (1.0 / total)).astype(BF16)
        logs[pl.ds(i, 1), :] = m + jnp.log(total)

    def group(g, _):
        for t in range(GROUP):
            u = g * GROUP + t
            unit = unit_ref[u]
            unit = jnp.where(unit >= 0, unit, unit_ref[g * GROUP])
            both = lax.shift_right_logical(unit, 22) == 1
            i = lax.bitwise_and(lax.shift_right_logical(unit, 16), 63)
            ea = lax.bitwise_and(lax.shift_right_logical(unit, 8), 127)
            eb = lax.bitwise_and(unit, 127)
            q = qbuf[lax.shift_right_logical(i, 3), lax.bitwise_and(i, 7)]
            s = nt(jnp.concatenate([kvbuf[ea, 0], kvbuf[eb, 0]], axis=0), q) * SCALE
            sa, sb = s[:BLOCK], jnp.where(both, s[BLOCK:], NEG)
            m = jnp.max(jnp.maximum(sa, sb), axis=0, keepdims=True)
            pa, pb = jnp.exp(sa - m), jnp.exp(sb - m)
            total = jnp.sum(pa + pb, axis=0, keepdims=True)
            p = jnp.concatenate([pa, pb], axis=0).astype(BF16)
            acc = nn(jnp.concatenate([kvbuf[ea, 1], kvbuf[eb, 1]], axis=1), p)
            stat_ref[u, 0:1, :] = m
            stat_ref[u, 1:2, :] = total
            acc_ref[u] = acc
            store(i, m, total, acc)
        return 0

    lax.fori_loop(0, lax.div(units + GROUP - 1, GROUP), group, 0)

    def join(k, _):
        i = long_ref[k]
        n = cnt_ref[i]
        u = first_ref[i]

        def more(k, carry):
            m, total, acc = carry
            mk, tk = stat_ref[k, 0:1, :], stat_ref[k, 1:2, :]
            top = jnp.maximum(m, mk)
            old, new = jnp.exp(m - top), jnp.exp(mk - top)
            return top, total * old + tk * new, acc * old + acc_ref[k] * new

        start = (stat_ref[u, 0:1, :], stat_ref[u, 1:2, :], acc_ref[u])
        store(i, *lax.fori_loop(u + 1, u + lax.shift_right_logical(n + 1, 1), more, start))
        return 0

    lax.fori_loop(0, size_ref[1], join, 0)
    for r in range(4):
        part = logs[r * 16 : (r + 1) * 16, :]
        for t in range(3):
            term = part.astype(BF16)
            obuf[r, 2048 + t * 16 : 2064 + t * 16, :] = term
            part = part - term.astype(F32)
        pltpu.make_async_copy(obuf.at[r], outs[r], osem.at[r]).start()
    for r in range(4):
        pltpu.make_async_copy(obuf.at[r], outs[r], osem.at[r]).wait()


def far(j, cnt, lists, sources, qs):
    out = jax.ShapeDtypeStruct((OROWS, BLOCK), BF16)
    return pl.pallas_call(
        functools.partial(far_kernel, j),
        in_specs=[SMEM] * 5 + [ANY] * 9,
        out_specs=[ANY] * 4,
        out_shape=[out] * 4,
        scratch_shapes=[
            pltpu.VMEM((128, 2, BLOCK, HD), BF16),
            pltpu.VMEM((8, 8, BLOCK, HD), BF16),
            pltpu.VMEM((4, OROWS, BLOCK), BF16),
            pltpu.VMEM((UNITS, HD, BLOCK), F32),
            pltpu.VMEM((UNITS, 8, BLOCK), F32),
            pltpu.VMEM((64, BLOCK), F32),
            pltpu.SemaphoreType.DMA((5,)),
            pltpu.SemaphoreType.DMA((4,)),
            pltpu.SemaphoreType.DMA((4,)),
        ],
        compiler_params=params(),
        cost_estimate=BRIEF,
        name="far",
    )(cnt, *lists, *sources, *qs)


def merge_kernel(a, b, c, d, keep, send):
    parts = (a, b, c, d)
    logs = [sum(p[2048 + t * 16 : 2064 + t * 16, :].astype(F32) for t in range(3)) for p in parts]
    peak = functools.reduce(jnp.maximum, logs)
    shares = [jnp.where(x > 0.5 * NEG, jnp.exp(x - peak), 0.0) for x in logs]
    total = sum(shares)
    joint = jnp.where(total > 0.0, peak + jnp.log(total), NEG)
    total = jnp.where(total > 0.0, total, 1.0)
    live = [x > 0.5 * NEG for x in logs]
    shares = [x / total for x in shares]
    for s, out in enumerate((keep, send)):
        for i in range(8):
            row = s * 8 + i
            rows = slice(row * HD, (row + 1) * HD)
            out[i * HD : (i + 1) * HD, :] = sum(
                jnp.where(on[row : row + 1, :], x[row : row + 1, :] * p[rows, :].astype(F32), 0.0)
                for on, x, p in zip(live, shares, parts)
            )
        out[1024:1032, :] = joint[s * 8 : (s + 1) * 8, :]


def merge(parts):
    out = jax.ShapeDtypeStruct((FROWS, BLOCK), F32)
    return pl.pallas_call(
        merge_kernel,
        out_shape=[out, out],
        compiler_params=params(),
        cost_estimate=BRIEF,
        name="merge",
    )(*parts)


def finish_kernel(near_a, lse_a, near_b, lse_b, far_a, far_b, out):
    for s, (o, log, f) in enumerate(((near_a, lse_a, far_a), (near_b, lse_b, far_b))):
        here, away = log[0], f[1024:1032, :]
        peak = jnp.maximum(here, away)
        wn, wf = jnp.exp(here - peak), jnp.exp(away - peak)
        total = wn + wf
        wn, wf = wn / total, wf / total
        for b in range(8):
            both = wn[b : b + 1, :] * o[0, b] + wf[b : b + 1, :] * f[b * HD : (b + 1) * HD, :]
            out[s, b * BLOCK : (b + 1) * BLOCK, :] = both.T.astype(BF16)


def finish(j, o, lse, far_keep, far_other):
    def at(slot):
        return [
            pl.BlockSpec((1, 8, HD, BLOCK), lambda i: (slot, 0, 0, 0)),
            pl.BlockSpec((1, 8, BLOCK), lambda i: (slot, 0, 0)),
        ]

    whole = pl.BlockSpec((FROWS, BLOCK), lambda i: (0, 0))
    return pl.pallas_call(
        finish_kernel,
        grid=(1,),
        in_specs=at(j) + at(2 + j) + [whole, whole],
        out_specs=pl.BlockSpec((2, 1024, HD), lambda i: (0, 0, 0)),
        out_shape=jax.ShapeDtypeStruct((2, 1024, HD), BF16),
        compiler_params=params(),
        cost_estimate=BRIEF,
        name="finish",
    )(o, lse, o, lse, far_keep, far_other)


def pick_kernel(place_ref, *rest):
    for j in range(2):
        for k in range(8):
            rest[16 + j][k * HD : (k + 1) * HD, :] = rest[j * 8 + k][...]


def pick(place, w_out):
    def weight(j, rel, s):
        return pl.BlockSpec((HD, 512), lambda i, p: ((p[1] + rel) % NX * 4 + (2 * p[0] + 2 * s + j) % 4, p[1]))

    out = jax.ShapeDtypeStruct((1024, 512), BF16)
    return pl.pallas_call(
        pick_kernel,
        grid_spec=pltpu.PrefetchScalarGridSpec(
            num_scalar_prefetch=1,
            grid=(1,),
            in_specs=[weight(j, rel, s) for j in range(2) for rel in range(4) for s in range(2)],
            out_specs=[pl.BlockSpec((1024, 512), lambda i, p: (0, 0))] * 2,
        ),
        out_shape=[out, out],
        compiler_params=params(),
        cost_estimate=BRIEF,
        name="pick",
    )(place, *[w_out] * 16)


def mix_kernel(place_ref, a0, a1, a2, a3, weight, carried, out):
    left = jnp.concatenate([a[s] for a in (a0, a1, a2, a3) for s in range(2)], axis=1)
    out[...] = (carried[...].astype(F32) + nn(left, weight[...])).astype(out.dtype)


def mix(place, parts, weight, carried, kind):
    column = 0 if carried.shape[1] == 512 else 1
    return pl.pallas_call(
        mix_kernel,
        grid_spec=pltpu.PrefetchScalarGridSpec(
            num_scalar_prefetch=1,
            grid=(4,),
            in_specs=[pl.BlockSpec((2, 256, HD), lambda i, p: (0, i, 0))] * 4
            + [pl.BlockSpec((1024, 512), lambda i, p: (0, 0))]
            + [pl.BlockSpec((256, 512), lambda i, p: (i, p[1] * column))],
            out_specs=pl.BlockSpec((256, 512), lambda i, p: (i, 0)),
        ),
        out_shape=jax.ShapeDtypeStruct((1024, 512), kind),
        compiler_params=params(),
        cost_estimate=BRIEF,
        name="mix",
    )(place, *parts, weight, carried)


def line_codes(wake_blocks, wake_frames, wake_counts, y, z, c):
    live = jnp.arange(WMAX, dtype=jnp.int32)[None, :] < wake_counts[:, None]
    word = jnp.where(live, wake_frames * 256 + wake_blocks, -1).reshape(NY, NZ, NC, 8, WMAX)
    by_y = lax.dynamic_index_in_dim(word, y, 0, keepdims=False)
    by_z = lax.dynamic_index_in_dim(word, z, 1, keepdims=False)
    here = jnp.where(c == 0, by_y, by_z)
    here = lax.dynamic_slice_in_dim(jnp.concatenate([here, here], axis=0), jnp.where(c == 0, z, y), 4, 0)
    here = lax.dynamic_slice_in_dim(jnp.concatenate([here, here], axis=1), c, 2, 1)
    word = here.reshape(64, WMAX)
    block, frame = word & 255, word >> 8
    hc, hz, hy = (block >> 3) & 1, (block >> 4) & 3, (block >> 6) & 3
    in_line = (word >= 0) & (jnp.where(c == 0, hz, hy) == jnp.where(c == 0, z, y))
    piece = (jnp.where(c == 0, hy, hz) - jnp.where(c == 0, y, z)) & 3
    code = piece * 32 + (hc ^ c) * 16 + (frame & 1) * 8 + (block & 7)
    code = jnp.where(in_line, code, -1)
    return code.reshape(512), jnp.sum(in_line.astype(jnp.int32), axis=1)


def on_device(tokens, norm_gain, w_query, w_key, w_value, w_out, kv_cache, wake_blocks, wake_frames, wake_counts):
    tok = lax.axis_index("tok").astype(jnp.int32)
    mp = lax.axis_index("mp").astype(jnp.int32)
    c, z, y = tok % NC, (tok // NC) % NZ, tok // (NC * NZ)
    core = c.reshape(1)
    place = jnp.stack([c, mp])

    def after(x, *deps):
        return lax.optimization_barrier((x, *deps))[0]

    got0 = core_swap(split_cache(2 - 2 * core, kv_cache))
    rows0 = lax.dynamic_update_slice(split_cache(2 * core, kv_cache, 2), got0, (16, 0, 0, 0))
    up0, down0 = rows_perm(rows0, 1), rows_perm(rows0, -1)

    normed, q_keep, q_send = query(core, tokens, after(norm_gain, rows0), w_query)
    mine = jnp.concatenate([q_keep, core_swap(q_send)], axis=0).reshape(2, 2, 8, BLOCK, HD)
    q1, q3, q2 = query_perm(mine, -1), query_perm(mine, 1), query_perm(mine, 2)
    core1 = after(core, mine)
    send1, keep1 = split_cache(3 - 2 * core1, kv_cache), split_cache(1 + 2 * core1, kv_cache, 2)
    code, cnt = line_codes(wake_blocks, wake_frames, wake_counts, y, z, c)
    tops, bottoms = up0[:16], down0[16:]
    normed, keep1, send1, code, cnt = lax.optimization_barrier((normed, keep1, send1, code, cnt))
    k_all, v_all, swap, edge = project(core, normed, w_key, w_value)
    held = (send1, swap, edge, q1, q2, q3, tops, bottoms)
    send1, swap, edge, q1, q2, q3, tops, bottoms = lax.optimization_barrier(held)
    swapped, halo = core_swap(swap), halo_perm(edge)
    rows1 = lax.dynamic_update_slice(keep1, core_swap(send1), (16, 0, 0, 0))
    up20, down20 = rows_perm(tops, 1), rows_perm(bottoms, -1)
    lists = plan(cnt, code)
    held = (rows1, up20, down20, halo, swapped, *lists)
    rows1, up20, down20, halo, swapped, *lists = lax.optimization_barrier(held)
    near_o, near_lse = near(core, q_keep, q_send, k_all, v_all, halo, swapped)
    up1, down1 = rows_perm(rows1, 1), rows_perm(rows1, -1)
    qs = [mine, q1, q2, q3]

    def returned(parts):
        return [parts[0], query_perm(parts[1], 1), query_perm(parts[2], 2), query_perm(parts[3], -1)]

    def gather(heads):
        return [heads, mp_perm(heads, -1), mp_perm(heads, 2), mp_perm(heads, 1)]

    parts = far(0, cnt, lists, [after(rows0, near_o), down0, up20, down20, up0], qs)
    weights = pick(after(place, parts[0]), w_out)
    back = returned(parts)
    back[1], back[3], up1, down1 = lax.optimization_barrier((back[1], back[3], up1, down1))
    tops1, bottoms1 = up1[:16], down1[16:]
    back[0], tops1, bottoms1 = lax.optimization_barrier((back[0], tops1, bottoms1))
    up21, down21 = rows_perm(tops1, 1), rows_perm(bottoms1, -1)
    back[0], near_lse, *weights = lax.optimization_barrier((back[0], near_lse, *weights))
    own, other = merge(back)
    heads = finish(0, near_o, near_lse, own, core_swap(other))
    gathered = gather(heads)

    parts = far(1, cnt, lists, [after(rows1, heads), down1, up21, down21, up1], qs)
    *parts, gathered[1], gathered[3] = lax.optimization_barrier((*parts, gathered[1], gathered[3]))
    back = returned(parts)
    back[0], gathered[2] = lax.optimization_barrier((back[0], gathered[2]))
    own, other = merge(back)
    heads = finish(1, near_o, near_lse, own, core_swap(other))
    gathered[0] = after(gathered[0], heads)
    acc = mix(place, gathered, weights[0], tokens, F32)
    return mix(place, gather(heads), weights[1], acc, BF16)


def solution(mesh):
    return jax.shard_map(
        on_device,
        mesh=mesh,
        in_specs=(
            P("tok", None),
            P(),
            P(None, "mp"),
            P(None, "mp"),
            P(None, "mp"),
            P(),
            P(None, "tok", None, "mp"),
            P(),
            P(),
            P(),
        ),
        out_specs=P("tok", "mp"),
        check_vma=False,
    )
```

```python
import functools
import math

import jax
import jax.numpy as jnp
from jax import lax
from jax.experimental import pallas as pl
from jax.experimental.pallas import tpu as pltpu
from jax.sharding import PartitionSpec as P

HD = 128
BLOCK = 128
WMAX = 8
NEG = -1e30
SCALE = 1.0 / math.sqrt(HD)
NY, NZ, NC, NX = 4, 4, 2, 4
F32, BF16 = jnp.float32, jnp.bfloat16
ANY = pl.BlockSpec(memory_space=pl.ANY)
SMEM = pl.BlockSpec(memory_space=pltpu.SMEM)
BRIEF = pl.CostEstimate(flops=1, transcendentals=0, bytes_accessed=1)
OROWS = 2048 + 48
FROWS = 1024 + 8


def params(mib=48):
    return pltpu.CompilerParams(vmem_limit_bytes=mib << 20)


def tok_of(y, z, c):
    return ((y % NY) * NZ + z % NZ) * NC + c % NC


def chips():
    return [(y, z, c) for y in range(NY) for z in range(NZ) for c in range(NC)]


def rows_perm(x, d):
    pairs = [(tok_of(y, z, c), tok_of(y + d, z, c) if c == 0 else tok_of(y, z + d, c)) for y, z, c in chips()]
    return lax.ppermute(x, "tok", pairs)


def query_perm(x, d):
    pairs = [(tok_of(y, z, c), tok_of(y, z + d, c) if c == 0 else tok_of(y + d, z, c)) for y, z, c in chips()]
    return lax.ppermute(x, "tok", pairs)


def core_swap(x):
    return lax.ppermute(x, "tok", [(tok_of(y, z, c), tok_of(y, z, 1 - c)) for y, z, c in chips()])


def halo_perm(x):
    n = NY * NZ * NC
    return lax.ppermute(x, "tok", [(i, (i + (1 if i % 2 else -1)) % n) for i in range(n)])


def mp_perm(x, d):
    return lax.ppermute(x, "mp", [(i, (i + d) % NX) for i in range(NX)])


def nt(a, b):
    return lax.dot_general(a, b, (((1,), (1,)), ((), ())), preferred_element_type=F32)


def nn(a, b):
    return lax.dot_general(a, b, (((1,), (0,)), ((), ())), preferred_element_type=F32)


def split_cache_kernel(head_ref, src, out):
    for b in range(2):
        rows = slice(b * BLOCK, (b + 1) * BLOCK)
        out[b, 0] = src[0, rows, 0, :]
        out[b, 1] = src[0, rows, 1, :].T


def split_cache(head, rows, holders=1):
    return pl.pallas_call(
        split_cache_kernel,
        grid_spec=pltpu.PrefetchScalarGridSpec(
            num_scalar_prefetch=1,
            grid=(8,),
            in_specs=[pl.BlockSpec((1, 256, 2, HD), lambda i, h: (i // 4, i % 4, 0, h[0]))],
            out_specs=pl.BlockSpec((2, 2, BLOCK, HD), lambda i, h: (i, 0, 0, 0)),
        ),
        out_shape=jax.ShapeDtypeStruct((16 * holders, 2, BLOCK, HD), BF16),
        compiler_params=params(),
        cost_estimate=BRIEF,
        name="split_cache",
    )(head, rows)


def normalise(tok_ref, gain_ref):
    x = tok_ref[...].astype(F32)
    inverse = lax.rsqrt(jnp.mean(x * x, axis=1, keepdims=True) + 1e-05)
    return (x * inverse * gain_ref[...]).astype(BF16)


def both_cores(core, put):
    for here in range(2):
        pl.when(core == here)(functools.partial(put, here))


def query_kernel(core_ref, tok_ref, gain_ref, wq, normed_ref, keep, send):
    normed = normalise(tok_ref, gain_ref)
    normed_ref[...] = normed
    q = nn(normed, wq[...]).astype(BF16)

    def put(here):
        for h in range(4):
            slot = (h - 2 * here) % 4
            out = keep if slot < 2 else send
            out[slot % 2] = q[:, h * HD : (h + 1) * HD]

    both_cores(core_ref[0], put)


def query(core, tokens, gain, wq):
    n, d = tokens.shape
    half = jax.ShapeDtypeStruct((2, n, HD), BF16)
    heads = pl.BlockSpec((2, 256, HD), lambda i, c: (0, i, 0))
    return pl.pallas_call(
        query_kernel,
        grid_spec=pltpu.PrefetchScalarGridSpec(
            num_scalar_prefetch=1,
            grid=(n // 256,),
            in_specs=[
                pl.BlockSpec((256, d), lambda i, c: (i, 0)),
                pl.BlockSpec((1, d), lambda i, c: (0, 0)),
                pl.BlockSpec((d, wq.shape[1]), lambda i, c: (0, 0), pipeline_mode=pl.Buffered(1)),
            ],
            out_specs=[pl.BlockSpec((256, d), lambda i, c: (i, 0)), heads, heads],
        ),
        out_shape=[jax.ShapeDtypeStruct((n, d), BF16), half, half],
        compiler_params=params(),
        cost_estimate=BRIEF,
        name="query",
    )(core, tokens, gain.reshape(1, d), wq)


def project_kernel(core_ref, normed_ref, wk, wv, k_all, v_all, swap, edge):
    step = pl.program_id(0)
    normed = normed_ref[...]
    k = nn(normed, wk[...]).astype(BF16)
    v = nn(normed, wv[...])

    def put(here):
        to_first = swap if here else edge
        to_last = edge if here else swap
        for h in range(4):
            slot = (h - 2 * here) % 4
            lanes = slice(h * HD, (h + 1) * HD)
            for b in range(2):
                rows = slice(b * BLOCK, (b + 1) * BLOCK)
                kb = k[rows, lanes]
                vb = v[rows, lanes].T.astype(BF16)
                k_all[slot, b] = kb
                v_all[slot, b] = vb
                out, when = (to_first, 0) if b == 0 else (to_last, pl.num_programs(0) - 1)

                @pl.when(step == when)
                def _():
                    out[slot * HD : (slot + 1) * HD, :] = kb
                    out[(4 + slot) * HD : (5 + slot) * HD, :] = vb

    both_cores(core_ref[0], put)


def project(core, normed, wk, wv):
    n, d = normed.shape
    weight = pl.BlockSpec((d, wk.shape[1]), lambda i, c: (0, 0), pipeline_mode=pl.Buffered(1))
    blocks = pl.BlockSpec((4, 2, BLOCK, HD), lambda i, c: (0, i, 0, 0))
    edge = pl.BlockSpec((1024, HD), lambda i, c: (0, 0))
    return pl.pallas_call(
        project_kernel,
        grid_spec=pltpu.PrefetchScalarGridSpec(
            num_scalar_prefetch=1,
            grid=(n // 256,),
            in_specs=[pl.BlockSpec((256, d), lambda i, c: (i, 0)), weight, weight],
            out_specs=[blocks, blocks, edge, edge],
        ),
        out_shape=[
            jax.ShapeDtypeStruct((4, 8, BLOCK, HD), BF16),
            jax.ShapeDtypeStruct((4, 8, HD, BLOCK), BF16),
            jax.ShapeDtypeStruct((1024, HD), BF16),
            jax.ShapeDtypeStruct((1024, HD), BF16),
        ],
        compiler_params=params(),
        cost_estimate=BRIEF,
        name="project",
    )(core, normed, wk, wv)


def near_kernel(core_ref, qa_ref, qb_ref, k_ref, v_ref, ka, va, kb, vb, o_ref, lse_ref):
    first = core_ref[0] == 0
    klo, khi = jnp.where(first, ka[0], kb[0]), jnp.where(first, kb[0], ka[0])
    vlo, vhi = jnp.where(first, va[0], vb[0]), jnp.where(first, vb[0], va[0])
    mine = pl.program_id(0) < 2
    for b in range(8):
        rows = slice(b * BLOCK, (b + 1) * BLOCK)
        q = jnp.where(mine, qa_ref[0, rows], qb_ref[0, rows])
        ks = [klo if b == 0 else k_ref[0, b - 1], k_ref[0, b], khi if b == 7 else k_ref[0, b + 1]]
        vs = [vlo if b == 0 else v_ref[0, b - 1], v_ref[0, b], vhi if b == 7 else v_ref[0, b + 1]]
        s = [nt(k, q) * SCALE for k in ks]
        m = jnp.max(jnp.maximum(jnp.maximum(s[0], s[1]), s[2]), axis=0, keepdims=True)
        p = [jnp.exp(x - m) for x in s]
        total = jnp.sum(p[0] + p[1] + p[2], axis=0, keepdims=True)
        acc = nn(vs[0], p[0].astype(BF16)) + nn(vs[1], p[1].astype(BF16)) + nn(vs[2], p[2].astype(BF16))
        o_ref[0, b] = acc / total
        lse_ref[0, b : b + 1, :] = m + jnp.log(total)


def near(core, keep, send, k, v, halo, swapped):
    blocks = pl.BlockSpec((1, 8, BLOCK, HD), lambda s, c: (s, 0, 0, 0))

    def edge(first):
        return pl.BlockSpec((1, BLOCK, HD), lambda s, c: (first + (s + 2) % 4, 0, 0))

    return pl.pallas_call(
        near_kernel,
        grid_spec=pltpu.PrefetchScalarGridSpec(
            num_scalar_prefetch=1,
            grid=(4,),
            in_specs=[pl.BlockSpec((1, 1024, HD), lambda s, c: (s % 2, 0, 0))] * 2
            + [blocks, blocks, edge(0), edge(4), edge(0), edge(4)],
            out_specs=[blocks, pl.BlockSpec((1, 8, HD), lambda s, c: (s, 0, 0))],
        ),
        out_shape=[jax.ShapeDtypeStruct((4, 8, HD, BLOCK), F32), jax.ShapeDtypeStruct((4, 8, BLOCK), F32)],
        compiler_params=params(),
        cost_estimate=BRIEF,
        name="near",
    )(core, keep, send, k, v, *[e.reshape(8, BLOCK, HD) for e in (halo, halo, swapped, swapped)])


GROUP = 4
UNITS = 96 + GROUP


def plan_kernel(cnt_ref, code_ref, unit_ref, first_ref, long_ref, size_ref, list_ref):
    def scan(i, carry):
        u, m = carry
        n = cnt_ref[i]
        first_ref[i] = u

        def named(carry):
            u, m = carry
            at = jnp.int32(0)
            for w in range(WMAX):
                code = code_ref[i * WMAX + w]
                list_ref[at] = code
                at = at + (code >= 0).astype(jnp.int32)

            def unit(k, u):
                both = (2 * k + 1 < n).astype(jnp.int32)
                unit_ref[u] = both * (1 << 22) + i * (1 << 16) + list_ref[2 * k] * 256 + list_ref[2 * k + both]
                return u + 1

            long_ref[m] = i
            return lax.fori_loop(0, lax.shift_right_logical(n + 1, 1), unit, u), m + (n > 2).astype(jnp.int32)

        return lax.cond(n > 0, named, lambda carry: carry, (u, m))

    units, longs = lax.fori_loop(0, 64, scan, (jnp.int32(0), jnp.int32(0)))
    for g in range(GROUP):
        unit_ref[units + g] = -1
    size_ref[0] = units
    size_ref[1] = longs


def plan(cnt, code):
    def out(n):
        return jax.ShapeDtypeStruct((n,), jnp.int32)

    return pl.pallas_call(
        plan_kernel,
        in_specs=[SMEM] * 2,
        out_specs=[SMEM] * 4,
        out_shape=[out(UNITS), out(64), out(64), out(2)],
        scratch_shapes=[pltpu.SMEM((2 * WMAX,), jnp.int32)],
        compiler_params=params(16),
        cost_estimate=BRIEF,
        name="plan",
    )(cnt, code)


def far_kernel(j, cnt_ref, unit_ref, first_ref, long_ref, size_ref, *rest):
    sources, qs, outs = rest[:5], rest[5:9], rest[9:13]
    kvbuf, qbuf, obuf, acc_ref, stat_ref, logs, kvsem, qsem, osem = rest[13:]
    units = size_ref[0]
    copies = [pltpu.make_async_copy(qs[r].at[:, j], qbuf.at[pl.ds(2 * r, 2)], qsem.at[r]) for r in range(4)]
    for k, (first, size) in enumerate(((0, 32), (32, 32), (64, 16), (80, 16), (96, 32))):
        copies.append(pltpu.make_async_copy(sources[k], kvbuf.at[pl.ds(first, size)], kvsem.at[k]))
    for copy in copies:
        copy.start()
    logs[...] = jnp.full((64, BLOCK), NEG, F32)
    for copy in copies:
        copy.wait()

    def store(i, m, total, acc):
        rows = pl.ds(pl.multiple_of(lax.bitwise_and(i, 15) * HD, HD), HD)
        obuf[lax.shift_right_logical(i, 4), rows, :] = (acc * (1.0 / total)).astype(BF16)
        logs[pl.ds(i, 1), :] = m + jnp.log(total)

    def group(g, _):
        for t in range(GROUP):
            u = g * GROUP + t
            unit = unit_ref[u]
            unit = jnp.where(unit >= 0, unit, unit_ref[g * GROUP])
            both = lax.shift_right_logical(unit, 22) == 1
            i = lax.bitwise_and(lax.shift_right_logical(unit, 16), 63)
            ea = lax.bitwise_and(lax.shift_right_logical(unit, 8), 127)
            eb = lax.bitwise_and(unit, 127)
            q = qbuf[lax.shift_right_logical(i, 3), lax.bitwise_and(i, 7)]
            s = nt(jnp.concatenate([kvbuf[ea, 0], kvbuf[eb, 0]], axis=0), q) * SCALE
            sa, sb = s[:BLOCK], jnp.where(both, s[BLOCK:], NEG)
            m = jnp.max(jnp.maximum(sa, sb), axis=0, keepdims=True)
            pa, pb = jnp.exp(sa - m), jnp.exp(sb - m)
            total = jnp.sum(pa + pb, axis=0, keepdims=True)
            p = jnp.concatenate([pa, pb], axis=0).astype(BF16)
            acc = nn(jnp.concatenate([kvbuf[ea, 1], kvbuf[eb, 1]], axis=1), p)
            stat_ref[u, 0:1, :] = m
            stat_ref[u, 1:2, :] = total
            acc_ref[u] = acc
            store(i, m, total, acc)
        return 0

    lax.fori_loop(0, lax.div(units + GROUP - 1, GROUP), group, 0)

    def join(k, _):
        i = long_ref[k]
        n = cnt_ref[i]
        u = first_ref[i]

        def more(k, carry):
            m, total, acc = carry
            mk, tk = stat_ref[k, 0:1, :], stat_ref[k, 1:2, :]
            top = jnp.maximum(m, mk)
            old, new = jnp.exp(m - top), jnp.exp(mk - top)
            return top, total * old + tk * new, acc * old + acc_ref[k] * new

        start = (stat_ref[u, 0:1, :], stat_ref[u, 1:2, :], acc_ref[u])
        store(i, *lax.fori_loop(u + 1, u + lax.shift_right_logical(n + 1, 1), more, start))
        return 0

    lax.fori_loop(0, size_ref[1], join, 0)
    for r in range(4):
        part = logs[r * 16 : (r + 1) * 16, :]
        for t in range(3):
            term = part.astype(BF16)
            obuf[r, 2048 + t * 16 : 2064 + t * 16, :] = term
            part = part - term.astype(F32)
        pltpu.make_async_copy(obuf.at[r], outs[r], osem.at[r]).start()
    for r in range(4):
        pltpu.make_async_copy(obuf.at[r], outs[r], osem.at[r]).wait()


def far(j, cnt, lists, sources, qs):
    out = jax.ShapeDtypeStruct((OROWS, BLOCK), BF16)
    return pl.pallas_call(
        functools.partial(far_kernel, j),
        in_specs=[SMEM] * 5 + [ANY] * 9,
        out_specs=[ANY] * 4,
        out_shape=[out] * 4,
        scratch_shapes=[
            pltpu.VMEM((128, 2, BLOCK, HD), BF16),
            pltpu.VMEM((8, 8, BLOCK, HD), BF16),
            pltpu.VMEM((4, OROWS, BLOCK), BF16),
            pltpu.VMEM((UNITS, HD, BLOCK), F32),
            pltpu.VMEM((UNITS, 8, BLOCK), F32),
            pltpu.VMEM((64, BLOCK), F32),
            pltpu.SemaphoreType.DMA((5,)),
            pltpu.SemaphoreType.DMA((4,)),
            pltpu.SemaphoreType.DMA((4,)),
        ],
        compiler_params=params(),
        cost_estimate=BRIEF,
        name="far",
    )(cnt, *lists, *sources, *qs)


def merge_kernel(a, b, c, d, keep, send):
    parts = (a, b, c, d)
    logs = [sum(p[2048 + t * 16 : 2064 + t * 16, :].astype(F32) for t in range(3)) for p in parts]
    peak = functools.reduce(jnp.maximum, logs)
    shares = [jnp.where(x > 0.5 * NEG, jnp.exp(x - peak), 0.0) for x in logs]
    total = sum(shares)
    joint = jnp.where(total > 0.0, peak + jnp.log(total), NEG)
    total = jnp.where(total > 0.0, total, 1.0)
    live = [x > 0.5 * NEG for x in logs]
    shares = [x / total for x in shares]
    for s, out in enumerate((keep, send)):
        for i in range(8):
            row = s * 8 + i
            rows = slice(row * HD, (row + 1) * HD)
            out[i * HD : (i + 1) * HD, :] = sum(
                jnp.where(on[row : row + 1, :], x[row : row + 1, :] * p[rows, :].astype(F32), 0.0)
                for on, x, p in zip(live, shares, parts)
            )
        out[1024:1032, :] = joint[s * 8 : (s + 1) * 8, :]


def merge(parts):
    out = jax.ShapeDtypeStruct((FROWS, BLOCK), F32)
    return pl.pallas_call(
        merge_kernel,
        out_shape=[out, out],
        compiler_params=params(),
        cost_estimate=BRIEF,
        name="merge",
    )(*parts)


def finish_kernel(near_a, lse_a, near_b, lse_b, far_a, far_b, out):
    for s, (o, log, f) in enumerate(((near_a, lse_a, far_a), (near_b, lse_b, far_b))):
        here, away = log[0], f[1024:1032, :]
        peak = jnp.maximum(here, away)
        wn, wf = jnp.exp(here - peak), jnp.exp(away - peak)
        total = wn + wf
        wn, wf = wn / total, wf / total
        for b in range(8):
            both = wn[b : b + 1, :] * o[0, b] + wf[b : b + 1, :] * f[b * HD : (b + 1) * HD, :]
            out[s, b * BLOCK : (b + 1) * BLOCK, :] = both.T.astype(BF16)


def finish(j, o, lse, far_keep, far_other):
    def at(slot):
        return [
            pl.BlockSpec((1, 8, HD, BLOCK), lambda i: (slot, 0, 0, 0)),
            pl.BlockSpec((1, 8, BLOCK), lambda i: (slot, 0, 0)),
        ]

    whole = pl.BlockSpec((FROWS, BLOCK), lambda i: (0, 0))
    return pl.pallas_call(
        finish_kernel,
        grid=(1,),
        in_specs=at(j) + at(2 + j) + [whole, whole],
        out_specs=pl.BlockSpec((2, 1024, HD), lambda i: (0, 0, 0)),
        out_shape=jax.ShapeDtypeStruct((2, 1024, HD), BF16),
        compiler_params=params(),
        cost_estimate=BRIEF,
        name="finish",
    )(o, lse, o, lse, far_keep, far_other)


def pick_kernel(place_ref, *rest):
    for j in range(2):
        for k in range(8):
            rest[16 + j][k * HD : (k + 1) * HD, :] = rest[j * 8 + k][...]


def pick(place, w_out):
    def weight(j, rel, s):
        return pl.BlockSpec((HD, 512), lambda i, p: ((p[1] + rel) % NX * 4 + (2 * p[0] + 2 * s + j) % 4, p[1]))

    out = jax.ShapeDtypeStruct((1024, 512), BF16)
    return pl.pallas_call(
        pick_kernel,
        grid_spec=pltpu.PrefetchScalarGridSpec(
            num_scalar_prefetch=1,
            grid=(1,),
            in_specs=[weight(j, rel, s) for j in range(2) for rel in range(4) for s in range(2)],
            out_specs=[pl.BlockSpec((1024, 512), lambda i, p: (0, 0))] * 2,
        ),
        out_shape=[out, out],
        compiler_params=params(),
        cost_estimate=BRIEF,
        name="pick",
    )(place, *[w_out] * 16)


def mix_kernel(place_ref, a0, a1, a2, a3, weight, carried, out):
    left = jnp.concatenate([a[s] for a in (a0, a1, a2, a3) for s in range(2)], axis=1)
    out[...] = (carried[...].astype(F32) + nn(left, weight[...])).astype(out.dtype)


def mix(place, parts, weight, carried, kind):
    column = 0 if carried.shape[1] == 512 else 1
    return pl.pallas_call(
        mix_kernel,
        grid_spec=pltpu.PrefetchScalarGridSpec(
            num_scalar_prefetch=1,
            grid=(4,),
            in_specs=[pl.BlockSpec((2, 256, HD), lambda i, p: (0, i, 0))] * 4
            + [pl.BlockSpec((1024, 512), lambda i, p: (0, 0))]
            + [pl.BlockSpec((256, 512), lambda i, p: (i, p[1] * column))],
            out_specs=pl.BlockSpec((256, 512), lambda i, p: (i, 0)),
        ),
        out_shape=jax.ShapeDtypeStruct((1024, 512), kind),
        compiler_params=params(),
        cost_estimate=BRIEF,
        name="mix",
    )(place, *parts, weight, carried)


def line_codes(wake_blocks, wake_frames, wake_counts, y, z, c):
    live = jnp.arange(WMAX, dtype=jnp.int32)[None, :] < wake_counts[:, None]
    word = jnp.where(live, wake_frames * 256 + wake_blocks, -1).reshape(NY, NZ, NC, 8, WMAX)
    by_y = lax.dynamic_index_in_dim(word, y, 0, keepdims=False)
    by_z = lax.dynamic_index_in_dim(word, z, 1, keepdims=False)
    here = jnp.where(c == 0, by_y, by_z)
    here = lax.dynamic_slice_in_dim(jnp.concatenate([here, here], axis=0), jnp.where(c == 0, z, y), 4, 0)
    here = lax.dynamic_slice_in_dim(jnp.concatenate([here, here], axis=1), c, 2, 1)
    word = here.reshape(64, WMAX)
    block, frame = word & 255, word >> 8
    hc, hz, hy = (block >> 3) & 1, (block >> 4) & 3, (block >> 6) & 3
    in_line = (word >= 0) & (jnp.where(c == 0, hz, hy) == jnp.where(c == 0, z, y))
    piece = (jnp.where(c == 0, hy, hz) - jnp.where(c == 0, y, z)) & 3
    code = piece * 32 + (hc ^ c) * 16 + (frame & 1) * 8 + (block & 7)
    code = jnp.where(in_line, code, -1)
    return code.reshape(512), jnp.sum(in_line.astype(jnp.int32), axis=1)


def on_device(tokens, norm_gain, w_query, w_key, w_value, w_out, kv_cache, wake_blocks, wake_frames, wake_counts):
    tok = lax.axis_index("tok").astype(jnp.int32)
    mp = lax.axis_index("mp").astype(jnp.int32)
    c, z, y = tok % NC, (tok // NC) % NZ, tok // (NC * NZ)
    core = c.reshape(1)
    place = jnp.stack([c, mp])

    def after(x, *deps):
        return lax.optimization_barrier((x, *deps))[0]

    got0 = core_swap(split_cache(2 - 2 * core, kv_cache))
    rows0 = lax.dynamic_update_slice(split_cache(2 * core, kv_cache, 2), got0, (16, 0, 0, 0))
    up0, down0 = rows_perm(rows0, 1), rows_perm(rows0, -1)

    normed, q_keep, q_send = query(core, tokens, after(norm_gain, rows0), w_query)
    mine = jnp.concatenate([q_keep, core_swap(q_send)], axis=0).reshape(2, 2, 8, BLOCK, HD)
    q1, q3, q2 = query_perm(mine, -1), query_perm(mine, 1), query_perm(mine, 2)
    core1 = after(core, mine)
    send1, keep1 = split_cache(3 - 2 * core1, kv_cache), split_cache(1 + 2 * core1, kv_cache, 2)
    code, cnt = line_codes(wake_blocks, wake_frames, wake_counts, y, z, c)
    tops, bottoms = up0[:16], down0[16:]
    normed, keep1, send1, code, cnt = lax.optimization_barrier((normed, keep1, send1, code, cnt))
    k_all, v_all, swap, edge = project(core, normed, w_key, w_value)
    held = (send1, swap, edge, q1, q2, q3, tops, bottoms)
    send1, swap, edge, q1, q2, q3, tops, bottoms = lax.optimization_barrier(held)
    swapped, halo = core_swap(swap), halo_perm(edge)
    rows1 = lax.dynamic_update_slice(keep1, core_swap(send1), (16, 0, 0, 0))
    up20, down20 = rows_perm(tops, 1), rows_perm(bottoms, -1)
    lists = plan(cnt, code)
    held = (rows1, up20, down20, halo, swapped, *lists)
    rows1, up20, down20, halo, swapped, *lists = lax.optimization_barrier(held)
    up1, down1 = rows_perm(rows1, 1), rows_perm(rows1, -1)
    qs = [mine, q1, q2, q3]

    def returned(parts):
        return [parts[0], query_perm(parts[1], 1), query_perm(parts[2], 2), query_perm(parts[3], -1)]

    def gather(heads):
        return [heads, mp_perm(heads, -1), mp_perm(heads, 2), mp_perm(heads, 1)]

    parts = far(0, cnt, lists, [rows0, down0, up20, down20, up0], qs)
    weights = pick(after(place, parts[0]), w_out)
    near_o, near_lse = near(core, q_keep, q_send, k_all, v_all, after(halo, parts[0]), swapped)
    back = returned(parts)
    back[1], back[3], up1, down1 = lax.optimization_barrier((back[1], back[3], up1, down1))
    tops1, bottoms1 = up1[:16], down1[16:]
    back[0], tops1, bottoms1 = lax.optimization_barrier((back[0], tops1, bottoms1))
    up21, down21 = rows_perm(tops1, 1), rows_perm(bottoms1, -1)
    back[0], near_lse, *weights = lax.optimization_barrier((back[0], near_lse, *weights))
    own, other = merge(back)
    heads = finish(0, near_o, near_lse, own, core_swap(other))
    gathered = gather(heads)

    parts = far(1, cnt, lists, [after(rows1, heads), down1, up21, down21, up1], qs)
    *parts, gathered[1], gathered[3] = lax.optimization_barrier((*parts, gathered[1], gathered[3]))
    back = returned(parts)
    back[0], gathered[2] = lax.optimization_barrier((back[0], gathered[2]))
    own, other = merge(back)
    heads = finish(1, near_o, near_lse, own, core_swap(other))
    gathered[0] = after(gathered[0], heads)
    acc = mix(place, gathered, weights[0], tokens, F32)
    return mix(place, gather(heads), weights[1], acc, BF16)


def solution(mesh):
    return jax.shard_map(
        on_device,
        mesh=mesh,
        in_specs=(
            P("tok", None),
            P(),
            P(None, "mp"),
            P(None, "mp"),
            P(None, "mp"),
            P(),
            P(None, "tok", None, "mp"),
            P(),
            P(),
            P(),
        ),
        out_specs=P("tok", "mp"),
        check_vma=False,
    )
```

```python
import functools
import math

import jax
import jax.numpy as jnp
from jax import lax
from jax.experimental import pallas as pl
from jax.experimental.pallas import tpu as pltpu
from jax.sharding import PartitionSpec as P

HD = 128
BLOCK = 128
WMAX = 8
NEG = -1e30
SCALE = 1.0 / math.sqrt(HD)
NY, NZ, NC, NX = 4, 4, 2, 4
F32, BF16 = jnp.float32, jnp.bfloat16
ANY = pl.BlockSpec(memory_space=pl.ANY)
SMEM = pl.BlockSpec(memory_space=pltpu.SMEM)
BRIEF = pl.CostEstimate(flops=1, transcendentals=0, bytes_accessed=1)
OROWS = 2048 + 48
FROWS = 1024 + 8


def params(mib=48):
    return pltpu.CompilerParams(vmem_limit_bytes=mib << 20)


def tok_of(y, z, c):
    return ((y % NY) * NZ + z % NZ) * NC + c % NC


def chips():
    return [(y, z, c) for y in range(NY) for z in range(NZ) for c in range(NC)]


def rows_perm(x, d):
    pairs = [(tok_of(y, z, c), tok_of(y + d, z, c) if c == 0 else tok_of(y, z + d, c)) for y, z, c in chips()]
    return lax.ppermute(x, "tok", pairs)


def query_perm(x, d):
    pairs = [(tok_of(y, z, c), tok_of(y, z + d, c) if c == 0 else tok_of(y + d, z, c)) for y, z, c in chips()]
    return lax.ppermute(x, "tok", pairs)


def core_swap(x):
    return lax.ppermute(x, "tok", [(tok_of(y, z, c), tok_of(y, z, 1 - c)) for y, z, c in chips()])


def halo_perm(x):
    n = NY * NZ * NC
    return lax.ppermute(x, "tok", [(i, (i + (1 if i % 2 else -1)) % n) for i in range(n)])


def mp_perm(x, d):
    return lax.ppermute(x, "mp", [(i, (i + d) % NX) for i in range(NX)])


def nt(a, b):
    return lax.dot_general(a, b, (((1,), (1,)), ((), ())), preferred_element_type=F32)


def nn(a, b):
    return lax.dot_general(a, b, (((1,), (0,)), ((), ())), preferred_element_type=F32)


def split_cache_kernel(head_ref, src, out):
    for b in range(2):
        rows = slice(b * BLOCK, (b + 1) * BLOCK)
        out[b, 0] = src[0, rows, 0, :]
        out[b, 1] = src[0, rows, 1, :].T


def split_cache(head, rows, holders=1):
    return pl.pallas_call(
        split_cache_kernel,
        grid_spec=pltpu.PrefetchScalarGridSpec(
            num_scalar_prefetch=1,
            grid=(8,),
            in_specs=[pl.BlockSpec((1, 256, 2, HD), lambda i, h: (i // 4, i % 4, 0, h[0]))],
            out_specs=pl.BlockSpec((2, 2, BLOCK, HD), lambda i, h: (i, 0, 0, 0)),
        ),
        out_shape=jax.ShapeDtypeStruct((16 * holders, 2, BLOCK, HD), BF16),
        compiler_params=params(),
        cost_estimate=BRIEF,
        name="split_cache",
    )(head, rows)


def normalise(tok_ref, gain_ref):
    x = tok_ref[...].astype(F32)
    inverse = lax.rsqrt(jnp.mean(x * x, axis=1, keepdims=True) + 1e-05)
    return (x * inverse * gain_ref[...]).astype(BF16)


def both_cores(core, put):
    for here in range(2):
        pl.when(core == here)(functools.partial(put, here))


def query_kernel(core_ref, tok_ref, gain_ref, wq, normed_ref, keep, send):
    normed = normalise(tok_ref, gain_ref)
    normed_ref[...] = normed
    q = nn(normed, wq[...]).astype(BF16)

    def put(here):
        for h in range(4):
            slot = (h - 2 * here) % 4
            out = keep if slot < 2 else send
            out[slot % 2] = q[:, h * HD : (h + 1) * HD]

    both_cores(core_ref[0], put)


def query(core, tokens, gain, wq):
    n, d = tokens.shape
    half = jax.ShapeDtypeStruct((2, n, HD), BF16)
    heads = pl.BlockSpec((2, 256, HD), lambda i, c: (0, i, 0))
    return pl.pallas_call(
        query_kernel,
        grid_spec=pltpu.PrefetchScalarGridSpec(
            num_scalar_prefetch=1,
            grid=(n // 256,),
            in_specs=[
                pl.BlockSpec((256, d), lambda i, c: (i, 0)),
                pl.BlockSpec((1, d), lambda i, c: (0, 0)),
                pl.BlockSpec((d, wq.shape[1]), lambda i, c: (0, 0), pipeline_mode=pl.Buffered(1)),
            ],
            out_specs=[pl.BlockSpec((256, d), lambda i, c: (i, 0)), heads, heads],
        ),
        out_shape=[jax.ShapeDtypeStruct((n, d), BF16), half, half],
        compiler_params=params(),
        cost_estimate=BRIEF,
        name="query",
    )(core, tokens, gain.reshape(1, d), wq)


def project_kernel(core_ref, normed_ref, wk, wv, k_all, v_all, swap, edge):
    step = pl.program_id(0)
    normed = normed_ref[...]
    k = nn(normed, wk[...]).astype(BF16)
    v = nn(normed, wv[...])

    def put(here):
        to_first = swap if here else edge
        to_last = edge if here else swap
        for h in range(4):
            slot = (h - 2 * here) % 4
            lanes = slice(h * HD, (h + 1) * HD)
            for b in range(2):
                rows = slice(b * BLOCK, (b + 1) * BLOCK)
                kb = k[rows, lanes]
                vb = v[rows, lanes].T.astype(BF16)
                k_all[slot, b] = kb
                v_all[slot, b] = vb
                out, when = (to_first, 0) if b == 0 else (to_last, pl.num_programs(0) - 1)

                @pl.when(step == when)
                def _():
                    out[slot * HD : (slot + 1) * HD, :] = kb
                    out[(4 + slot) * HD : (5 + slot) * HD, :] = vb

    both_cores(core_ref[0], put)


def project(core, normed, wk, wv):
    n, d = normed.shape
    weight = pl.BlockSpec((d, wk.shape[1]), lambda i, c: (0, 0), pipeline_mode=pl.Buffered(1))
    blocks = pl.BlockSpec((4, 2, BLOCK, HD), lambda i, c: (0, i, 0, 0))
    edge = pl.BlockSpec((1024, HD), lambda i, c: (0, 0))
    return pl.pallas_call(
        project_kernel,
        grid_spec=pltpu.PrefetchScalarGridSpec(
            num_scalar_prefetch=1,
            grid=(n // 256,),
            in_specs=[pl.BlockSpec((256, d), lambda i, c: (i, 0)), weight, weight],
            out_specs=[blocks, blocks, edge, edge],
        ),
        out_shape=[
            jax.ShapeDtypeStruct((4, 8, BLOCK, HD), BF16),
            jax.ShapeDtypeStruct((4, 8, HD, BLOCK), BF16),
            jax.ShapeDtypeStruct((1024, HD), BF16),
            jax.ShapeDtypeStruct((1024, HD), BF16),
        ],
        compiler_params=params(),
        cost_estimate=BRIEF,
        name="project",
    )(core, normed, wk, wv)


def near_kernel(core_ref, qa_ref, qb_ref, k_ref, v_ref, ka, va, kb, vb, o_ref, lse_ref):
    first = core_ref[0] == 0
    klo, khi = jnp.where(first, ka[0], kb[0]), jnp.where(first, kb[0], ka[0])
    vlo, vhi = jnp.where(first, va[0], vb[0]), jnp.where(first, vb[0], va[0])
    mine = pl.program_id(0) < 2
    for b in range(8):
        rows = slice(b * BLOCK, (b + 1) * BLOCK)
        q = jnp.where(mine, qa_ref[0, rows], qb_ref[0, rows])
        ks = [klo if b == 0 else k_ref[0, b - 1], k_ref[0, b], khi if b == 7 else k_ref[0, b + 1]]
        vs = [vlo if b == 0 else v_ref[0, b - 1], v_ref[0, b], vhi if b == 7 else v_ref[0, b + 1]]
        s = [nt(k, q) * SCALE for k in ks]
        m = jnp.max(jnp.maximum(jnp.maximum(s[0], s[1]), s[2]), axis=0, keepdims=True)
        p = [jnp.exp(x - m) for x in s]
        total = jnp.sum(p[0] + p[1] + p[2], axis=0, keepdims=True)
        acc = nn(vs[0], p[0].astype(BF16)) + nn(vs[1], p[1].astype(BF16)) + nn(vs[2], p[2].astype(BF16))
        o_ref[0, b] = acc / total
        lse_ref[0, b : b + 1, :] = m + jnp.log(total)


def near(core, keep, send, k, v, halo, swapped):
    blocks = pl.BlockSpec((1, 8, BLOCK, HD), lambda s, c: (s, 0, 0, 0))

    def edge(first):
        return pl.BlockSpec((1, BLOCK, HD), lambda s, c: (first + (s + 2) % 4, 0, 0))

    return pl.pallas_call(
        near_kernel,
        grid_spec=pltpu.PrefetchScalarGridSpec(
            num_scalar_prefetch=1,
            grid=(4,),
            in_specs=[pl.BlockSpec((1, 1024, HD), lambda s, c: (s % 2, 0, 0))] * 2
            + [blocks, blocks, edge(0), edge(4), edge(0), edge(4)],
            out_specs=[blocks, pl.BlockSpec((1, 8, HD), lambda s, c: (s, 0, 0))],
        ),
        out_shape=[jax.ShapeDtypeStruct((4, 8, HD, BLOCK), F32), jax.ShapeDtypeStruct((4, 8, BLOCK), F32)],
        compiler_params=params(),
        cost_estimate=BRIEF,
        name="near",
    )(core, keep, send, k, v, *[e.reshape(8, BLOCK, HD) for e in (halo, halo, swapped, swapped)])


GROUP = 4
UNITS = 96 + GROUP


def plan_kernel(cnt_ref, code_ref, unit_ref, first_ref, long_ref, size_ref, list_ref):
    def scan(i, carry):
        u, m = carry
        n = cnt_ref[i]
        first_ref[i] = u

        def named(carry):
            u, m = carry
            at = jnp.int32(0)
            for w in range(WMAX):
                code = code_ref[i * WMAX + w]
                list_ref[at] = code
                at = at + (code >= 0).astype(jnp.int32)

            def unit(k, u):
                both = (2 * k + 1 < n).astype(jnp.int32)
                unit_ref[u] = both * (1 << 22) + i * (1 << 16) + list_ref[2 * k] * 256 + list_ref[2 * k + both]
                return u + 1

            long_ref[m] = i
            return lax.fori_loop(0, lax.shift_right_logical(n + 1, 1), unit, u), m + (n > 2).astype(jnp.int32)

        return lax.cond(n > 0, named, lambda carry: carry, (u, m))

    units, longs = lax.fori_loop(0, 64, scan, (jnp.int32(0), jnp.int32(0)))
    for g in range(GROUP):
        unit_ref[units + g] = -1
    size_ref[0] = units
    size_ref[1] = longs


def plan(cnt, code):
    def out(n):
        return jax.ShapeDtypeStruct((n,), jnp.int32)

    return pl.pallas_call(
        plan_kernel,
        in_specs=[SMEM] * 2,
        out_specs=[SMEM] * 4,
        out_shape=[out(UNITS), out(64), out(64), out(2)],
        scratch_shapes=[pltpu.SMEM((2 * WMAX,), jnp.int32)],
        compiler_params=params(16),
        cost_estimate=BRIEF,
        name="plan",
    )(cnt, code)


def far_kernel(j, cnt_ref, unit_ref, first_ref, long_ref, size_ref, *rest):
    sources, qs, outs = rest[:5], rest[5:9], rest[9:13]
    kvbuf, qbuf, obuf, acc_ref, stat_ref, logs, kvsem, qsem, osem = rest[13:]
    units = size_ref[0]
    copies = [pltpu.make_async_copy(qs[r].at[:, j], qbuf.at[pl.ds(2 * r, 2)], qsem.at[r]) for r in range(4)]
    for k, (first, size) in enumerate(((0, 32), (32, 32), (64, 16), (80, 16), (96, 32))):
        copies.append(pltpu.make_async_copy(sources[k], kvbuf.at[pl.ds(first, size)], kvsem.at[k]))
    for copy in copies:
        copy.start()
    logs[...] = jnp.full((64, BLOCK), NEG, F32)
    for copy in copies:
        copy.wait()

    def store(i, m, total, acc):
        rows = pl.ds(pl.multiple_of(lax.bitwise_and(i, 15) * HD, HD), HD)
        obuf[lax.shift_right_logical(i, 4), rows, :] = (acc * (1.0 / total)).astype(BF16)
        logs[pl.ds(i, 1), :] = m + jnp.log(total)

    def group(g, _):
        for t in range(GROUP):
            u = g * GROUP + t
            unit = unit_ref[u]
            unit = jnp.where(unit >= 0, unit, unit_ref[g * GROUP])
            both = lax.shift_right_logical(unit, 22) == 1
            i = lax.bitwise_and(lax.shift_right_logical(unit, 16), 63)
            ea = lax.bitwise_and(lax.shift_right_logical(unit, 8), 127)
            eb = lax.bitwise_and(unit, 127)
            q = qbuf[lax.shift_right_logical(i, 3), lax.bitwise_and(i, 7)]
            s = nt(jnp.concatenate([kvbuf[ea, 0], kvbuf[eb, 0]], axis=0), q) * SCALE
            sa, sb = s[:BLOCK], jnp.where(both, s[BLOCK:], NEG)
            m = jnp.max(jnp.maximum(sa, sb), axis=0, keepdims=True)
            pa, pb = jnp.exp(sa - m), jnp.exp(sb - m)
            total = jnp.sum(pa + pb, axis=0, keepdims=True)
            p = jnp.concatenate([pa, pb], axis=0).astype(BF16)
            acc = nn(jnp.concatenate([kvbuf[ea, 1], kvbuf[eb, 1]], axis=1), p)
            stat_ref[u, 0:1, :] = m
            stat_ref[u, 1:2, :] = total
            acc_ref[u] = acc
            store(i, m, total, acc)
        return 0

    lax.fori_loop(0, lax.div(units + GROUP - 1, GROUP), group, 0)

    def join(k, _):
        i = long_ref[k]
        n = cnt_ref[i]
        u = first_ref[i]

        def more(k, carry):
            m, total, acc = carry
            mk, tk = stat_ref[k, 0:1, :], stat_ref[k, 1:2, :]
            top = jnp.maximum(m, mk)
            old, new = jnp.exp(m - top), jnp.exp(mk - top)
            return top, total * old + tk * new, acc * old + acc_ref[k] * new

        start = (stat_ref[u, 0:1, :], stat_ref[u, 1:2, :], acc_ref[u])
        store(i, *lax.fori_loop(u + 1, u + lax.shift_right_logical(n + 1, 1), more, start))
        return 0

    lax.fori_loop(0, size_ref[1], join, 0)
    for r in range(4):
        part = logs[r * 16 : (r + 1) * 16, :]
        for t in range(3):
            term = part.astype(BF16)
            obuf[r, 2048 + t * 16 : 2064 + t * 16, :] = term
            part = part - term.astype(F32)
        pltpu.make_async_copy(obuf.at[r], outs[r], osem.at[r]).start()
    for r in range(4):
        pltpu.make_async_copy(obuf.at[r], outs[r], osem.at[r]).wait()


def far(j, cnt, lists, sources, qs):
    out = jax.ShapeDtypeStruct((OROWS, BLOCK), BF16)
    return pl.pallas_call(
        functools.partial(far_kernel, j),
        in_specs=[SMEM] * 5 + [ANY] * 9,
        out_specs=[ANY] * 4,
        out_shape=[out] * 4,
        scratch_shapes=[
            pltpu.VMEM((128, 2, BLOCK, HD), BF16),
            pltpu.VMEM((8, 8, BLOCK, HD), BF16),
            pltpu.VMEM((4, OROWS, BLOCK), BF16),
            pltpu.VMEM((UNITS, HD, BLOCK), F32),
            pltpu.VMEM((UNITS, 8, BLOCK), F32),
            pltpu.VMEM((64, BLOCK), F32),
            pltpu.SemaphoreType.DMA((5,)),
            pltpu.SemaphoreType.DMA((4,)),
            pltpu.SemaphoreType.DMA((4,)),
        ],
        compiler_params=params(),
        cost_estimate=BRIEF,
        name="far",
    )(cnt, *lists, *sources, *qs)


def merge_kernel(a, b, c, d, keep, send):
    parts = (a, b, c, d)
    logs = [sum(p[2048 + t * 16 : 2064 + t * 16, :].astype(F32) for t in range(3)) for p in parts]
    peak = functools.reduce(jnp.maximum, logs)
    shares = [jnp.where(x > 0.5 * NEG, jnp.exp(x - peak), 0.0) for x in logs]
    total = sum(shares)
    joint = jnp.where(total > 0.0, peak + jnp.log(total), NEG)
    total = jnp.where(total > 0.0, total, 1.0)
    live = [x > 0.5 * NEG for x in logs]
    shares = [x / total for x in shares]
    for s, out in enumerate((keep, send)):
        for i in range(8):
            row = s * 8 + i
            rows = slice(row * HD, (row + 1) * HD)
            out[i * HD : (i + 1) * HD, :] = sum(
                jnp.where(on[row : row + 1, :], x[row : row + 1, :] * p[rows, :].astype(F32), 0.0)
                for on, x, p in zip(live, shares, parts)
            )
        out[1024:1032, :] = joint[s * 8 : (s + 1) * 8, :]


def merge(parts):
    out = jax.ShapeDtypeStruct((FROWS, BLOCK), F32)
    return pl.pallas_call(
        merge_kernel,
        out_shape=[out, out],
        compiler_params=params(),
        cost_estimate=BRIEF,
        name="merge",
    )(*parts)


def finish_kernel(near_a, lse_a, near_b, lse_b, far_a, far_b, out):
    for s, (o, log, f) in enumerate(((near_a, lse_a, far_a), (near_b, lse_b, far_b))):
        here, away = log[0], f[1024:1032, :]
        peak = jnp.maximum(here, away)
        wn, wf = jnp.exp(here - peak), jnp.exp(away - peak)
        total = wn + wf
        wn, wf = wn / total, wf / total
        for b in range(8):
            both = wn[b : b + 1, :] * o[0, b] + wf[b : b + 1, :] * f[b * HD : (b + 1) * HD, :]
            out[s, b * BLOCK : (b + 1) * BLOCK, :] = both.T.astype(BF16)


def finish(j, o, lse, far_keep, far_other):
    def at(slot):
        return [
            pl.BlockSpec((1, 8, HD, BLOCK), lambda i: (slot, 0, 0, 0)),
            pl.BlockSpec((1, 8, BLOCK), lambda i: (slot, 0, 0)),
        ]

    whole = pl.BlockSpec((FROWS, BLOCK), lambda i: (0, 0))
    return pl.pallas_call(
        finish_kernel,
        grid=(1,),
        in_specs=at(j) + at(2 + j) + [whole, whole],
        out_specs=pl.BlockSpec((2, 1024, HD), lambda i: (0, 0, 0)),
        out_shape=jax.ShapeDtypeStruct((2, 1024, HD), BF16),
        compiler_params=params(),
        cost_estimate=BRIEF,
        name="finish",
    )(o, lse, o, lse, far_keep, far_other)


def pick_kernel(place_ref, *rest):
    for j in range(2):
        for k in range(8):
            rest[16 + j][k * HD : (k + 1) * HD, :] = rest[j * 8 + k][...]


def pick(place, w_out):
    def weight(j, rel, s):
        return pl.BlockSpec((HD, 512), lambda i, p: ((p[1] + rel) % NX * 4 + (2 * p[0] + 2 * s + j) % 4, p[1]))

    out = jax.ShapeDtypeStruct((1024, 512), BF16)
    return pl.pallas_call(
        pick_kernel,
        grid_spec=pltpu.PrefetchScalarGridSpec(
            num_scalar_prefetch=1,
            grid=(1,),
            in_specs=[weight(j, rel, s) for j in range(2) for rel in range(4) for s in range(2)],
            out_specs=[pl.BlockSpec((1024, 512), lambda i, p: (0, 0))] * 2,
        ),
        out_shape=[out, out],
        compiler_params=params(),
        cost_estimate=BRIEF,
        name="pick",
    )(place, *[w_out] * 16)


def mix_kernel(place_ref, a0, a1, a2, a3, weight, carried, out):
    left = jnp.concatenate([a[s] for a in (a0, a1, a2, a3) for s in range(2)], axis=1)
    out[...] = (carried[...].astype(F32) + nn(left, weight[...])).astype(out.dtype)


def mix(place, parts, weight, carried, kind):
    column = 0 if carried.shape[1] == 512 else 1
    return pl.pallas_call(
        mix_kernel,
        grid_spec=pltpu.PrefetchScalarGridSpec(
            num_scalar_prefetch=1,
            grid=(4,),
            in_specs=[pl.BlockSpec((2, 256, HD), lambda i, p: (0, i, 0))] * 4
            + [pl.BlockSpec((1024, 512), lambda i, p: (0, 0))]
            + [pl.BlockSpec((256, 512), lambda i, p: (i, p[1] * column))],
            out_specs=pl.BlockSpec((256, 512), lambda i, p: (i, 0)),
        ),
        out_shape=jax.ShapeDtypeStruct((1024, 512), kind),
        compiler_params=params(),
        cost_estimate=BRIEF,
        name="mix",
    )(place, *parts, weight, carried)


def line_codes(wake_blocks, wake_frames, wake_counts, y, z, c):
    live = jnp.arange(WMAX, dtype=jnp.int32)[None, :] < wake_counts[:, None]
    word = jnp.where(live, wake_frames * 256 + wake_blocks, -1).reshape(NY, NZ, NC, 8, WMAX)
    by_y = lax.dynamic_index_in_dim(word, y, 0, keepdims=False)
    by_z = lax.dynamic_index_in_dim(word, z, 1, keepdims=False)
    here = jnp.where(c == 0, by_y, by_z)
    here = lax.dynamic_slice_in_dim(jnp.concatenate([here, here], axis=0), jnp.where(c == 0, z, y), 4, 0)
    here = lax.dynamic_slice_in_dim(jnp.concatenate([here, here], axis=1), c, 2, 1)
    word = here.reshape(64, WMAX)
    block, frame = word & 255, word >> 8
    hc, hz, hy = (block >> 3) & 1, (block >> 4) & 3, (block >> 6) & 3
    in_line = (word >= 0) & (jnp.where(c == 0, hz, hy) == jnp.where(c == 0, z, y))
    piece = (jnp.where(c == 0, hy, hz) - jnp.where(c == 0, y, z)) & 3
    code = piece * 32 + (hc ^ c) * 16 + (frame & 1) * 8 + (block & 7)
    code = jnp.where(in_line, code, -1)
    return code.reshape(512), jnp.sum(in_line.astype(jnp.int32), axis=1)


def on_device(tokens, norm_gain, w_query, w_key, w_value, w_out, kv_cache, wake_blocks, wake_frames, wake_counts):
    tok = lax.axis_index("tok").astype(jnp.int32)
    mp = lax.axis_index("mp").astype(jnp.int32)
    c, z, y = tok % NC, (tok // NC) % NZ, tok // (NC * NZ)
    core = c.reshape(1)
    place = jnp.stack([c, mp])

    def after(x, *deps):
        return lax.optimization_barrier((x, *deps))[0]

    got0 = core_swap(split_cache(2 - 2 * core, kv_cache))
    rows0 = lax.dynamic_update_slice(split_cache(2 * core, kv_cache, 2), got0, (16, 0, 0, 0))
    up0, down0 = rows_perm(rows0, 1), rows_perm(rows0, -1)

    normed, q_keep, q_send = query(core, tokens, after(norm_gain, rows0), w_query)
    mine = jnp.concatenate([q_keep, core_swap(q_send)], axis=0).reshape(2, 2, 8, BLOCK, HD)
    q1, q3, q2 = query_perm(mine, -1), query_perm(mine, 1), query_perm(mine, 2)
    core1 = after(core, mine)
    send1, keep1 = split_cache(3 - 2 * core1, kv_cache), split_cache(1 + 2 * core1, kv_cache, 2)
    code, cnt = line_codes(wake_blocks, wake_frames, wake_counts, y, z, c)
    tops, bottoms = up0[:16], down0[16:]
    normed, keep1, send1, code, cnt = lax.optimization_barrier((normed, keep1, send1, code, cnt))
    k_all, v_all, swap, edge = project(core, normed, w_key, w_value)
    held = (send1, swap, edge, q1, q2, q3, tops, bottoms)
    send1, swap, edge, q1, q2, q3, tops, bottoms = lax.optimization_barrier(held)
    swapped, halo = core_swap(swap), halo_perm(edge)
    rows1 = lax.dynamic_update_slice(keep1, core_swap(send1), (16, 0, 0, 0))
    up20, down20 = rows_perm(tops, 1), rows_perm(bottoms, -1)
    lists = plan(cnt, code)
    held = (rows1, up20, down20, halo, swapped, *lists)
    rows1, up20, down20, halo, swapped, *lists = lax.optimization_barrier(held)
    near_o, near_lse = near(core, q_keep, q_send, k_all, v_all, halo, swapped)
    up1, down1 = rows_perm(rows1, 1), rows_perm(rows1, -1)
    qs = [mine, q1, q2, q3]

    def returned(parts):
        return [parts[0], query_perm(parts[1], 1), query_perm(parts[2], 2), query_perm(parts[3], -1)]

    def gather(heads):
        return [heads, mp_perm(heads, -1), mp_perm(heads, 2), mp_perm(heads, 1)]

    parts = far(0, cnt, lists, [after(rows0, near_o), down0, up20, down20, up0], qs)
    weights = pick(after(place, parts[0]), w_out)
    back = returned(parts)
    tops1, bottoms1 = up1[:16], down1[16:]
    back[0], tops1, bottoms1 = lax.optimization_barrier((back[0], tops1, bottoms1))
    up21, down21 = rows_perm(tops1, 1), rows_perm(bottoms1, -1)
    back[0], near_lse, *weights = lax.optimization_barrier((back[0], near_lse, *weights))
    own, other = merge(back)
    heads = finish(0, near_o, near_lse, own, core_swap(other))
    gathered = gather(heads)

    parts = far(1, cnt, lists, [after(rows1, heads), down1, up21, down21, up1], qs)
    *parts, gathered[1], gathered[3] = lax.optimization_barrier((*parts, gathered[1], gathered[3]))
    back = returned(parts)
    back[0], gathered[2] = lax.optimization_barrier((back[0], gathered[2]))
    own, other = merge(back)
    heads = finish(1, near_o, near_lse, own, core_swap(other))
    gathered[0] = after(gathered[0], heads)
    acc = mix(place, gathered, weights[0], tokens, F32)
    return mix(place, gather(heads), weights[1], acc, BF16)


def solution(mesh):
    return jax.shard_map(
        on_device,
        mesh=mesh,
        in_specs=(
            P("tok", None),
            P(),
            P(None, "mp"),
            P(None, "mp"),
            P(None, "mp"),
            P(),
            P(None, "tok", None, "mp"),
            P(),
            P(),
            P(),
        ),
        out_specs=P("tok", "mp"),
        check_vma=False,
    )
```
